32 devices in a mesh: grp: 4 (over z), sub: 8 (over y, x, core).
Axes of the slice: x: 2, y: 2, z: 4, core: 2. Of those that a mesh axis runs over, the one named last changes fastest.
Arguments:
- leaf_l: float32 [8, 5120, 768], P('sub', 'grp'), may hold values from -0.21875 to 0.21875
- leaf_u: float32 [8, 3072, 1280], P('sub', 'grp'), may hold values from -6 to 6
- front: float32 [8, 1280, 1280], P('sub', 'grp'), may hold values from -6 to 6
- inv_diag: float32 [8, 5, 256, 256], P('sub'), may hold values from -0.375 to 0.375
- send_tiles: int32 [8, 4, 8, 2], P('sub', 'grp'), may hold values from 0 to 4, as said below
- counts: int32 [8, 4, 8], P('sub', 'grp'), may hold values from 0 to 2, as said below
- trail_list: int32 [8, 4, 32, 3], P('sub', 'grp'), may hold values from 0 to 7, as said below
- upper: float32 [4, 256, 256], replicated, may hold values from -0.0625 to 0.0625
- trailing: float32 [8, 1280, 256], P('sub', 'grp'), may hold values from -6 to 6
Outputs:
- panel: float32 [8, 1280, 1280], P('sub', 'grp')
- updated: float32 [8, 1280, 256], P('sub', 'grp')
The draws below stay inside these ranges and needn't reach their ends.
Inputs may be any that keep to these rules, and one draw needn't show every extreme that they name: `send_tiles`: each value is a tile column of the source strip. `counts`: at most 2 tiles go from one device to another; in every draw, for each strip g some destination front receives 2 tiles from every source front. `trail_list`: column 0 is a source front, column 1 a slot c with c < counts[s, g, d] for that entry's source s, strip g and destination d, column 2 an upper tile below 4.
All inputs are finite; a program needn't handle non-finite values.
Results may differ from the reference program's by a relative error of at most 0.0003.
Values sent between devices are 32-bit elements; how exact they have to be, the bound alone decides.
A program may use at most 128 MiB of HBM per device.

```python
import jax
import jax.numpy as jnp
from jax import lax

R = 1280
K = 768
TILE = 256
CAP = 2
NL = 32
NU = 4
NT = 5
STRIP = 320
FRONTS = 8
LEAVES = 4


def make_lists(key):
    base = jax.random.fold_in(key, 7)
    keys = jax.random.split(base, 5)
    amounts = jax.random.randint(keys[0], (FRONTS, LEAVES, FRONTS), 0, CAP + 1)
    full_dest = jax.random.randint(keys[1], (LEAVES,), 0, FRONTS)
    ident = jnp.arange(FRONTS, dtype=jnp.int32)
    is_full = ident[None, None, :] == full_dest[None, :, None]
    amounts = jnp.where(is_full, CAP, amounts)
    self_pair = ident[:, None, None] == ident[None, None, :]
    amounts = jnp.where(self_pair, jnp.maximum(amounts, 1), amounts)
    tiles = jax.random.randint(keys[2], (FRONTS, LEAVES, FRONTS, CAP), 0, NT)
    pairs = FRONTS * CAP
    pair_ids = jnp.arange(pairs, dtype=jnp.int32)
    source_of = pair_ids // CAP
    slot_of = pair_ids % CAP
    by_dest = jnp.transpose(amounts, (2, 1, 0))
    valid = slot_of[None, None, :] < by_dest[:, :, source_of]
    noise = jax.random.randint(keys[3], (FRONTS, LEAVES, pairs), 0, 65536)
    score = jnp.where(valid, noise * pairs + pair_ids, -1 - pair_ids)
    order = jnp.argsort(-score, axis=-1, stable=True).astype(jnp.int32)
    nvalid = jnp.sum(valid.astype(jnp.int32), axis=-1)
    positions = jnp.arange(NL, dtype=jnp.int32)
    picked = jnp.take_along_axis(order, positions[None, None, :] % nvalid[..., None], axis=-1)
    upper_ids = jax.random.randint(keys[4], (FRONTS, LEAVES, NL), 0, NU)
    lists = jnp.stack([picked // CAP, picked % CAP, upper_ids], axis=-1).astype(jnp.int32)
    return (tiles.astype(jnp.int32), amounts.astype(jnp.int32), lists)


def draw_send_tiles(key, part):
    return make_lists(key)[0]


def draw_counts(key, part):
    return make_lists(key)[1]


def draw_trail_list(key, part):
    return make_lists(key)[2]


def levels(stream_key, shape, cuts, low, largest):
    gain = 1.0
    for dim, shards_of in cuts:
        steps = jax.random.uniform(jax.random.fold_in(jax.random.fold_in(stream_key, 6), dim), (shards_of,), jnp.float32, low / len(cuts), largest / len(cuts))
        gain = gain * jnp.repeat(jnp.exp(steps), shape[dim] // shards_of).reshape((-1,) + (1,) * (len(shape) - 1 - dim))
    return gain


def centred(own_key, dims, spread, limit, cuts=(), held_as=jnp.bfloat16):
    values = spread * jax.random.normal(own_key, dims, jnp.float32)
    if cuts:
        values = values * levels(own_key, dims, cuts, -0.22, 0.18)
    return jnp.clip(values, -limit, limit).astype(held_as)


def setup_inputs(seed: int = 0) -> dict:
    key_list = jax.random.split(jax.random.key(seed), 10)
    return {
        "leaf_l": centred(key_list[0], (FRONTS, LEAVES * R, K), K ** -0.5, 0.21875, ((0, 8), (1, 4)), jnp.float32),
        "leaf_u": centred(key_list[1], (FRONTS, LEAVES * K, R), 1.0, 6.0, ((0, 8), (1, 4)), jnp.float32),
        "front": centred(key_list[2], (FRONTS, R, R), 1.0, 6.0, ((0, 8), (1, 4)), jnp.float32),
        "inv_diag": centred(key_list[3], (FRONTS, NT, TILE, TILE), TILE ** -0.5, 0.375, ((0, 8),), jnp.float32),
        "send_tiles": draw_send_tiles(jax.random.fold_in(key_list[9], 71), 0),
        "counts": draw_counts(jax.random.fold_in(key_list[9], 71), 0),
        "trail_list": draw_trail_list(jax.random.fold_in(key_list[9], 71), 0),
        "upper": centred(key_list[7], (NU, TILE, TILE), (TILE * NL) ** -0.5, 0.0625, (), jnp.float32),
        "trailing": centred(key_list[8], (FRONTS, R, TILE), 1.0, 6.0, ((0, 8), (1, 4)), jnp.float32),
    }


def reference(leaf_l, leaf_u, front, inv_diag, send_tiles, counts, trail_list, upper, trailing):
    precise = lax.Precision.HIGHEST

    def one_front(index):
        lower = leaf_l[index].reshape(LEAVES, R, K)
        uppers = leaf_u[index].reshape(LEAVES, K, R)
        schur = jnp.einsum("grk,gkc->rc", lower, uppers, precision=precise)
        assembled = front[index] - schur
        solved = jnp.einsum("rja,jab->rjb", assembled.reshape(R, NT, TILE), inv_diag[index], precision=precise)
        return solved.reshape(R, R)

    panel = lax.map(one_front, jnp.arange(FRONTS, dtype=jnp.int32))
    blocks = panel.reshape(FRONTS, LEAVES, STRIP, NT, TILE)

    def one_block(index):
        dest = index // LEAVES
        leaf = index % LEAVES
        entries = trail_list[dest, leaf]
        source = entries[:, 0]
        slot = entries[:, 1]
        which = entries[:, 2]
        tile_ids = send_tiles[source, leaf, dest, slot]
        live = (slot < counts[source, leaf, dest]).astype(panel.dtype)
        chosen = blocks[source, leaf]
        pieces = chosen[jnp.arange(NL, dtype=jnp.int32), :, tile_ids] * live[:, None, None]
        update = jnp.einsum("qrt,qtc->rc", pieces, upper[which], precision=precise)
        base = lax.dynamic_slice_in_dim(trailing[dest], (leaf * STRIP).astype(jnp.int32), STRIP, 0)
        return base - update

    updated = lax.map(one_block, jnp.arange(FRONTS * LEAVES, dtype=jnp.int32))
    return panel, updated.reshape(FRONTS, R, TILE)
```

```python
import functools

import jax
import jax.numpy as jnp
from jax import lax
from jax.experimental import pallas as pl
from jax.experimental.pallas import tpu as pltpu
from jax.sharding import PartitionSpec as P

MESH = pl.DeviceIdType.MESH
F32 = jnp.float32
BF16 = jnp.bfloat16
ROWS = (32, 16, 8)


def split(x):
    high = x.astype(BF16)
    return high, (x - high.astype(F32)).astype(BF16)


def dot(a, b):
    return jnp.dot(a, b, preferred_element_type=F32)


def dot3(stacked, high, low):
    m = stacked.shape[0] // 2
    both = dot(stacked, high)
    return both[:m] + both[m:] + dot(stacked[:m], low)


def kernel(
    G, N, C, rows, block,
    leaf_l, leaf_u, front, inv_diag, send_tiles, counts, trail_list, upper, trailing,
    pan, upd,
    l_buf, l_two, u_buf, u_hi, u_lo, s_buf, f_buf, d_buf, d_hi, d_lo, v_buf, v_hi, v_lo, t_buf, up_buf, dn_buf,
    lists, coef, x_buf, prod, part, got,
    in_sem, up_send, up_recv, dn_send, dn_recv, list_send, list_recv, x_send, x_recv,
):
    z = lax.axis_index("grp")
    me = lax.axis_index("sub")
    width = front.shape[2]
    tile = upper.shape[1]
    depth = u_buf.shape[0]
    nt = width // tile
    nu = upper.shape[0]
    cap = send_tiles.shape[2]
    strip = C * rows
    per = block // rows
    group = min(4, N // 2)
    steps = N.bit_length() - 1

    def bit(value, s):
        return lax.rem(lax.div(value, 1 << s), 2)

    def partner(s):
        return me + (1 << s) * (1 - 2 * bit(me, s))

    def dest_of(p):
        return sum((1 << s) * lax.rem(bit(me, s) + bit(p, steps - 1 - s), 2) for s in range(steps))

    def load_l(t):
        at = pl.ds(t * strip, strip)
        return pltpu.make_async_copy(leaf_l.at[0, at], l_buf.at[at], in_sem.at[t])

    def load_u(n):
        at = pl.ds(n * (depth // 3), depth // 3)
        return pltpu.make_async_copy(leaf_u.at[0, at], u_buf.at[at], in_sem.at[G + n])

    others = [
        pltpu.make_async_copy(front.at[0], f_buf, in_sem.at[G + 3]),
        pltpu.make_async_copy(inv_diag.at[0], d_buf, in_sem.at[G + 4]),
        pltpu.make_async_copy(trailing.at[0], t_buf, in_sem.at[G + 5]),
        pltpu.make_async_copy(upper, v_buf, in_sem.at[G + 6]),
    ]
    load_u(0).start()
    load_l(G - 1).start()
    load_u(1).start()
    load_u(2).start()
    load_l(0).start()

    barrier = pltpu.get_barrier_semaphore()

    @pl.loop(1, N)
    def _(p):
        pl.semaphore_signal(barrier, inc=1, device_id={"sub": dest_of(p)}, device_id_type=MESH)

    @pl.when(z > 0)
    def _():
        pl.semaphore_signal(barrier, inc=1, device_id={"grp": z - 1}, device_id_type=MESH)

    @pl.when(z < G - 1)
    def _():
        pl.semaphore_signal(barrier, inc=1, device_id={"grp": z + 1}, device_id_type=MESH)

    for n in range(3):
        load_u(n).wait()

        @pl.loop(n * (depth // 3), (n + 1) * (depth // 3), step=16)
        def _(r):
            at = pl.ds(pl.multiple_of(r, 16), 16)
            high, low = split(u_buf[at, :])
            u_hi[at, :] = high
            u_lo[at, :] = low

    load_l(G - 1).wait()
    load_l(0).wait()
    for t in range(1, G - 1):
        load_l(t).start()
    for other in others:
        other.start()

    pl.semaphore_wait(barrier, N - 1 + jnp.where(z > 0, 1, 0) + jnp.where(z < G - 1, 1, 0))

    def own_list():
        return pltpu.make_async_copy(trail_list.at[0], lists.at[me], list_recv.at[me])

    def list_copy(p, owner):
        return pltpu.make_async_remote_copy(
            src_ref=trail_list.at[0], dst_ref=lists.at[owner],
            send_sem=list_send.at[p], recv_sem=list_recv.at[owner],
            device_id={"sub": dest_of(p)}, device_id_type=MESH,
        )

    def up_copy(k):
        return pltpu.make_async_remote_copy(
            src_ref=up_buf.at[k], dst_ref=up_buf.at[k],
            send_sem=up_send.at[k], recv_sem=up_recv.at[k],
            device_id={"grp": z + 1}, device_id_type=MESH,
        )

    def dn_copy(k):
        return pltpu.make_async_remote_copy(
            src_ref=dn_buf.at[k], dst_ref=dn_buf.at[k],
            send_sem=dn_send.at[k], recv_sem=dn_recv.at[k],
            device_id={"grp": z - 1}, device_id_type=MESH,
        )

    def schur(row):
        at = pl.ds(pl.multiple_of(row, 8), block)
        high, low = split(l_buf[at, :])
        l_two[:block, :] = high
        l_two[block:, :] = low

        @pl.loop(0, nt)
        def _(n):
            cols = pl.ds(pl.multiple_of(n * tile, tile), tile)
            s_buf[at, cols] = dot3(l_two[...], u_hi[:, cols], u_lo[:, cols])

    def forward(buf, k, row, first):
        at = pl.ds(pl.multiple_of(row, 8), rows)

        @pl.when(first)
        def _():
            buf[k] = s_buf[at, :]

        @pl.when(jnp.logical_not(first))
        def _():
            buf[k] = buf[k] + s_buf[at, :]

    def weigh(p):
        d = dest_of(p)

        @pl.when(p == 0)
        def _():
            own_list().wait()

        @pl.when(p > 0)
        def _():
            list_copy(p, d).wait_recv()

        source, slot, which = lists[d, 0], lists[d, 1], lists[d, 2]
        pick = jnp.zeros_like(source)
        for c in range(cap):
            pick = jnp.where(slot == c, send_tiles[0, 0, c, d], pick)
        live = (source == me) & (slot < counts[0, 0, d])
        code = jnp.where(live, pick * nu + which, -1)
        terms = lax.broadcasted_iota(jnp.int32, (coef.shape[1], code.shape[1]), 0)
        total = jnp.sum(jnp.where(code == terms, 1.0, 0.0).astype(F32), axis=1, keepdims=True)
        coef[p] = jnp.broadcast_to(total, coef.shape[1:])

    def exchange(c, s):
        h = N >> (s + 1)
        return pltpu.make_async_remote_copy(
            src_ref=part.at[c, pl.ds(h, h)], dst_ref=got.at[c, pl.ds(h, h)],
            send_sem=x_send.at[c, s], recv_sem=x_recv.at[c, s],
            device_id={"sub": partner(s)}, device_id_type=MESH,
        )

    def solve(c):
        at = pl.ds(pl.multiple_of(c * rows, 8), rows)
        mine = pl.ds(pl.multiple_of(z * strip + c * rows, 8), rows)
        pan[at, :] = f_buf[at, :] - s_buf[mine, :]

        @pl.when(z > 0)
        def _():
            k = (G - 1 - z) * C + c
            up_copy(k).wait_recv()
            pan[at, :] = pan[at, :] - up_buf[k]

        @pl.when(z < G - 1)
        def _():
            k = z * C + c
            dn_copy(k).wait_recv()
            pan[at, :] = pan[at, :] - dn_buf[k]

        half = nt * rows
        for j in range(nt):
            cols = slice(j * tile, (j + 1) * tile)
            high, low = split(pan[at, cols])
            solved = dot3(jnp.concatenate([high, low], axis=0), d_hi[j], d_lo[j])
            pan[at, cols] = solved
            high, low = split(solved)
            x_buf[j * rows : (j + 1) * rows, :] = high
            x_buf[half + j * rows : half + (j + 1) * rows, :] = low
        for u in range(nu):
            prod[u] = dot3(x_buf[...], v_hi[u], v_lo[u])

        def mix(g):
            p0 = g * group

            @pl.loop(0, rows, step=8)
            def _(r):
                r = pl.multiple_of(r, 8)
                sums = [None] * group
                for j in range(nt):
                    for u in range(nu):
                        value = prod[u, pl.ds(j * rows + r, 8), :]
                        for q in range(group):
                            n = j * nu + u
                            term = coef[p0 + q, n : n + 1, :] * value
                            sums[q] = term if sums[q] is None else sums[q] + term
                for q in range(group):
                    part[c, p0 + q, pl.ds(r, 8), :] = sums[q]

        groups = N // group
        pl.loop(groups // 2, groups)(mix)
        exchange(c, 0).start()
        pl.loop(0, groups // 2)(mix)

    def stage(c, s):
        h = N >> (s + 1)
        exchange(c, s).wait_recv()
        if s < steps - 1:
            q = h // 2
            part[c, q:h] = part[c, q:h] + got[c, h + q : 2 * h]
            exchange(c, s + 1).start()
            part[c, 0:q] = part[c, 0:q] + got[c, h : h + q]
        else:
            at = pl.ds(pl.multiple_of(c * rows, 8), rows)
            upd[at, :] = t_buf[at, :] - (part[c, 0] + got[c, 1])

    lag_up, lag_dn = z, G - 1 - z
    base = jnp.maximum((G - 1 - z) * C + lag_up, z * C + lag_dn)
    last = max(max((G - 1 - i) * C + i, i * C + G - 1 - i) for i in range(G))

    @pl.loop(0, last + C + steps)
    def _(i):
        up, down, own = i - lag_up, i - lag_dn, i - base
        has_up = (up >= 0) & (up < (G - 1 - z) * C)
        has_dn = (down >= 0) & (down < z * C)
        up_row = (G - 1) * strip + lax.rem(jnp.maximum(up, 0), C) * rows - lax.div(jnp.maximum(up, 0), C) * strip

        @pl.loop(0, 3)
        def _(job):
            k = jnp.where(job == 0, up, jnp.where(job == 1, down, own + 1))
            has = ((job == 0) & has_up) | ((job == 1) & has_dn) | ((job == 2) & (k >= 0) & (k < C))
            row = jnp.where(job == 0, up_row, jnp.where(job == 1, down * rows, z * strip + k * rows))

            @pl.when(has & (lax.rem(jnp.maximum(k, 0), per) == 0))
            def _():
                schur(row)

        @pl.when(has_up)
        def _():
            @pl.when(z > 0)
            def _():
                up_copy(up).wait_recv()

            forward(up_buf, up, up_row, z == 0)
            up_copy(up).start()

        @pl.when(has_dn)
        def _():
            @pl.when(z < G - 1)
            def _():
                dn_copy(down).wait_recv()

            forward(dn_buf, down, down * rows, z == G - 1)
            dn_copy(down).start()

        @pl.when(i == 1)
        def _():
            own_list().start()

            @pl.loop(1, N)
            def _(p):
                list_copy(p, me).start()

            for t in range(1, G - 1):
                load_l(t).wait()
            for other in others:
                other.wait()
            for j in range(nt):
                high, low = split(d_buf[j])
                d_hi[j] = high
                d_lo[j] = low
            for u in range(nu):
                high, low = split(v_buf[u])
                v_hi[u] = high
                v_lo[u] = low

        @pl.when(i == 3)
        def _():
            pl.loop(0, N)(weigh)

        for s in reversed(range(steps)):
            @pl.when((own - 1 - s >= 0) & (own - 1 - s < C))
            def _():
                stage(own - 1 - s, s)

        @pl.when((own >= 0) & (own < C))
        def _():
            solve(own)

    @pl.loop(0, (G - 1 - z) * C)
    def _(k):
        up_copy(k).wait_send()

    @pl.loop(0, z * C)
    def _(k):
        dn_copy(k).wait_send()

    @pl.loop(1, N)
    def _(p):
        list_copy(p, me).wait_send()

    @pl.loop(0, C)
    def _(c):
        for s in range(steps):
            exchange(c, s).wait_send()


def per_device(leaf_l, leaf_u, front, inv_diag, send_tiles, counts, trail_list, upper, trailing):
    G = lax.axis_size("grp")
    N = lax.axis_size("sub")
    strip, width = front.shape[1:]
    depth = leaf_u.shape[1]
    tile = upper.shape[1]
    rows = next(r for r in ROWS if strip % r == 0)
    C = strip // rows
    block = 2 * rows if strip % (2 * rows) == 0 else strip
    nt, nu = width // tile, upper.shape[0]
    terms = -(-nt * nu // 8) * 8
    send_tiles = jnp.transpose(send_tiles, (0, 1, 3, 2))
    trail_list = jnp.transpose(trail_list, (0, 3, 1, 2))
    anywhere = pl.BlockSpec(memory_space=pl.ANY)
    vmem = pl.BlockSpec(memory_space=pltpu.VMEM)
    smem = pl.BlockSpec(memory_space=pltpu.SMEM)
    hops = (G - 1) * C
    steps = N.bit_length() - 1
    dma = pltpu.SemaphoreType.DMA
    panel, updated = pl.pallas_call(
        functools.partial(kernel, G, N, C, rows, block),
        out_shape=(pltpu.VMEM(front.shape[1:], F32), pltpu.VMEM(trailing.shape[1:], F32)),
        in_specs=[anywhere] * 4 + [smem, smem, vmem, anywhere, anywhere],
        out_specs=(vmem, vmem),
        scratch_shapes=[
            pltpu.VMEM(leaf_l.shape[1:], F32),
            pltpu.VMEM((2 * block, depth), BF16),
            pltpu.VMEM((depth, width), F32),
            pltpu.VMEM((depth, width), BF16),
            pltpu.VMEM((depth, width), BF16),
            pltpu.VMEM((G * strip, width), F32),
            pltpu.VMEM((strip, width), F32),
            pltpu.VMEM(inv_diag.shape[1:], F32),
            pltpu.VMEM(inv_diag.shape[1:], BF16),
            pltpu.VMEM(inv_diag.shape[1:], BF16),
            pltpu.VMEM(upper.shape, F32),
            pltpu.VMEM(upper.shape, BF16),
            pltpu.VMEM(upper.shape, BF16),
            pltpu.VMEM((strip, tile), F32),
            pltpu.VMEM((hops, rows, width), F32),
            pltpu.VMEM((hops, rows, width), F32),
            pltpu.VMEM((N,) + trail_list.shape[1:], jnp.int32),
            pltpu.VMEM((N, terms, tile), F32),
            pltpu.VMEM((2 * nt * rows, tile), BF16),
            pltpu.VMEM((nu, nt * rows, tile), F32),
            pltpu.VMEM((C, N, rows, tile), F32),
            pltpu.VMEM((C, N, rows, tile), F32),
            dma((G + 7,)),
            dma((hops,)), dma((hops,)), dma((hops,)), dma((hops,)),
            dma((N,)), dma((N,)),
            dma((C, steps)), dma((C, steps)),
        ],
        compiler_params=pltpu.CompilerParams(
            collective_id=0, has_side_effects=True, vmem_limit_bytes=60 << 20
        ),
    )(leaf_l, leaf_u, front, inv_diag, send_tiles, counts, trail_list, upper, trailing)
    return write_out(panel, updated)


def copy_kernel(cuts, panel, updated, panel_out, updated_out, sem):
    rows = panel.shape[0] // cuts
    copies = [pltpu.make_async_copy(updated, updated_out.at[0], sem.at[cuts])]
    for i in range(cuts):
        at = pl.ds(i * rows, rows)
        copies.append(pltpu.make_async_copy(panel.at[at], panel_out.at[0, at], sem.at[i]))
    for copy in copies:
        copy.start()
    for copy in copies:
        copy.wait()


def write_out(panel, updated):
    strip = panel.shape[0]
    cuts = next(n for n in (4, 2, 1) if strip % (8 * n) == 0)
    vmem = pl.BlockSpec(memory_space=pltpu.VMEM)
    anywhere = pl.BlockSpec(memory_space=pl.ANY)
    return pl.pallas_call(
        functools.partial(copy_kernel, cuts),
        out_shape=tuple(jax.ShapeDtypeStruct((1,) + x.shape, F32) for x in (panel, updated)),
        in_specs=[vmem, vmem],
        out_specs=(anywhere, anywhere),
        scratch_shapes=[pltpu.SemaphoreType.DMA((cuts + 1,))],
        compiler_params=pltpu.CompilerParams(vmem_limit_bytes=1 << 20),
    )(panel, updated)


def solution(mesh):
    placed = (
        P("sub", "grp", None),
        P("sub", "grp", None),
        P("sub", "grp", None),
        P("sub", None, None, None),
        P("sub", "grp", None, None),
        P("sub", "grp", None),
        P("sub", "grp", None, None),
        P(),
        P("sub", "grp", None),
    )
    return jax.shard_map(
        per_device,
        mesh=mesh,
        in_specs=placed,
        out_specs=(P("sub", "grp", None), P("sub", "grp", None)),
        check_vma=False,
    )
```

```python
import functools

import jax
import jax.numpy as jnp
from jax import lax
from jax.experimental import pallas as pl
from jax.experimental.pallas import tpu as pltpu
from jax.sharding import PartitionSpec as P

MESH = pl.DeviceIdType.MESH
F32 = jnp.float32
BF16 = jnp.bfloat16
ROWS = (32, 16, 8)
AHEAD = 3
LAG = 2


def split(x):
    high = x.astype(BF16)
    return high, (x - high.astype(F32)).astype(BF16)


def dot(a, b):
    return jnp.dot(a, b, preferred_element_type=F32)


def dot3(stacked, high, low):
    m = stacked.shape[0] // 2
    both = dot(stacked, high)
    return both[:m] + both[m:] + dot(stacked[:m], low)


def kernel(
    G, N, C, H, rows, block,
    leaf_l, leaf_u, front, inv_diag, send_tiles, counts, trail_list, upper, trailing,
    pan, upd,
    l_buf, l_two, u_buf, u_hi, u_lo, s_buf, f_buf, d_buf, d_hi, d_lo, v_buf, v_hi, v_lo, t_buf, mail,
    lists, coef, work, x_buf, prod, part, got, ahead,
    in_sem, up_send, up_recv, dn_send, dn_recv, list_send, list_recv, x_send, x_recv, coef_sem, ahead_send, ahead_recv,
):
    z = lax.axis_index("grp")
    me = lax.axis_index("sub")
    width = front.shape[2]
    tile = upper.shape[1]
    depth = u_buf.shape[0]
    nt = width // tile
    nu = upper.shape[0]
    cap = send_tiles.shape[2]
    strip = C * rows
    per = block // rows
    group = min(4, N // 2)
    steps = N.bit_length() - 1
    top = (G + 1) * C - 1
    low_end, high_end = z == 0, z == G - 1
    helper = (H > 0) & (low_end | high_end)
    helped_up, helped_dn = (H > 0) & (z == 1), (H > 0) & (z == G - 2)
    helped = helped_up | helped_dn
    ally = jnp.where(low_end | (z == G - 2), z + 1, z - 1)
    extra = jnp.where(helper, H, 0)

    def bit(value, s):
        return lax.rem(lax.div(value, 1 << s), 2)

    def partner(s):
        return me + (1 << s) * (1 - 2 * bit(me, s))

    def dest_of(p):
        return sum((1 << s) * lax.rem(bit(me, s) + bit(p, steps - 1 - s), 2) for s in range(steps))

    def load_l(t, first, count, n):
        at = pl.ds(t * strip + first, count)
        return pltpu.make_async_copy(leaf_l.at[0, at], l_buf.at[at], in_sem.at[n])

    def load_u(n):
        cols = pl.ds(pl.multiple_of(n * tile, tile), tile)
        return pltpu.make_async_copy(leaf_u.at[0, :, cols], u_buf.at[:, cols], in_sem.at[n])

    heads = [load_l(G - 1, 0, block, nt), load_l(0, 0, block, nt + 1)]
    tails = [load_l(t, 0, strip, nt + 1 + t) for t in range(1, G - 1)]
    if block < strip:
        tails = [
            load_l(G - 1, block, strip - block, nt + G),
            load_l(0, block, strip - block, nt + G + 1),
        ] + tails
    others = [
        pltpu.make_async_copy(front.at[0], f_buf, in_sem.at[nt + G + 2]),
        pltpu.make_async_copy(inv_diag.at[0], d_buf, in_sem.at[nt + G + 3]),
        pltpu.make_async_copy(trailing.at[0], t_buf, in_sem.at[nt + G + 4]),
        pltpu.make_async_copy(upper, v_buf, in_sem.at[nt + G + 5]),
    ]
    heads[0].start()
    heads[1].start()
    pl.loop(0, nt)(lambda n: load_u(n).start())
    for copy in tails + others:
        copy.start()

    barrier = pltpu.get_barrier_semaphore()

    @pl.loop(1, N)
    def _(p):
        pl.semaphore_signal(barrier, inc=1, device_id={"sub": dest_of(p)}, device_id_type=MESH)

    @pl.when(z > 0)
    def _():
        pl.semaphore_signal(barrier, inc=1, device_id={"grp": z - 1}, device_id_type=MESH)

    @pl.when(z < G - 1)
    def _():
        pl.semaphore_signal(barrier, inc=1, device_id={"grp": z + 1}, device_id_type=MESH)

    def own_list():
        return pltpu.make_async_copy(trail_list.at[0], lists.at[me], list_recv.at[me])

    def list_copy(p, owner):
        return pltpu.make_async_remote_copy(
            src_ref=trail_list.at[0], dst_ref=lists.at[owner],
            send_sem=list_send.at[p], recv_sem=list_recv.at[owner],
            device_id={"sub": dest_of(p)}, device_id_type=MESH,
        )

    def up_copy(k, cols=slice(None)):
        return pltpu.make_async_remote_copy(
            src_ref=mail.at[k, :, cols], dst_ref=mail.at[k, :, cols],
            send_sem=up_send.at[k], recv_sem=up_recv.at[k],
            device_id={"grp": z + 1}, device_id_type=MESH,
        )

    def dn_copy(k, cols=slice(None)):
        return pltpu.make_async_remote_copy(
            src_ref=mail.at[top - k, :, cols], dst_ref=mail.at[top - k, :, cols],
            send_sem=dn_send.at[k], recv_sem=dn_recv.at[k],
            device_id={"grp": z - 1}, device_id_type=MESH,
        )

    def coef_copy():
        return pltpu.make_async_remote_copy(
            src_ref=coef.at[0], dst_ref=coef.at[1],
            send_sem=coef_sem.at[0], recv_sem=coef_sem.at[1],
            device_id={"grp": ally}, device_id_type=MESH,
        )

    def ahead_copy(e):
        return pltpu.make_async_remote_copy(
            src_ref=ahead.at[e], dst_ref=ahead.at[e],
            send_sem=ahead_send.at[e], recv_sem=ahead_recv.at[e],
            device_id={"grp": ally}, device_id_type=MESH,
        )

    def halve(row):
        at = pl.ds(pl.multiple_of(row, 8), block)
        high, low = split(l_buf[at, :])
        l_two[:block, :] = high
        l_two[block:, :] = low

    def product(row, n):
        at = pl.ds(pl.multiple_of(row, 8), block)
        cols = pl.ds(pl.multiple_of(n * tile, tile), tile)
        s_buf[at, cols] = dot3(l_two[...], u_hi[:, cols], u_lo[:, cols])

    def schur(row):
        halve(row)
        pl.loop(0, nt)(lambda n: product(row, n))

    def forward(slot, row, first):
        at = pl.ds(pl.multiple_of(row, 8), rows)

        @pl.when(first)
        def _():
            mail[slot] = s_buf[at, :]

        @pl.when(jnp.logical_not(first))
        def _():
            mail[slot] = mail[slot] + s_buf[at, :]

    def begin(n):
        cols = pl.ds(pl.multiple_of(n * tile, tile), tile)
        load_u(n).wait()

        @pl.loop(0, depth, step=16)
        def _(r):
            at = pl.ds(pl.multiple_of(r, 16), 16)
            high, low = split(u_buf[at, cols])
            u_hi[at, cols] = high
            u_lo[at, cols] = low

        @pl.when(low_end)
        def _():
            product((G - 1) * strip, n)

        @pl.when(high_end)
        def _():
            product(0, n)

    def begin_send(n):
        cols = pl.ds(pl.multiple_of(n * tile, tile), tile)
        for k in range(per):
            @pl.when(low_end)
            def _():
                mail[k, :, cols] = s_buf[(G - 1) * strip + k * rows : (G - 1) * strip + (k + 1) * rows, cols]
                up_copy(k, cols).start()

            @pl.when(high_end)
            def _():
                mail[top - k, :, cols] = s_buf[k * rows : (k + 1) * rows, cols]
                dn_copy(k, cols).start()

    for head in heads:
        head.wait()

    @pl.when(low_end)
    def _():
        halve((G - 1) * strip)

    @pl.when(high_end)
    def _():
        halve(0)

    begin(0)
    pl.semaphore_wait(barrier, N - 1 + jnp.where(z > 0, 1, 0) + jnp.where(z < G - 1, 1, 0))
    begin_send(0)

    @pl.loop(1, nt)
    def _(n):
        begin(n)
        begin_send(n)

    def weigh(p):
        d = dest_of(p)

        @pl.when(p == 0)
        def _():
            own_list().wait()

        @pl.when(p > 0)
        def _():
            list_copy(p, d).wait_recv()

        source, slot, which = lists[d, 0], lists[d, 1], lists[d, 2]
        pick = jnp.zeros_like(source)
        for c in range(cap):
            pick = jnp.where(slot == c, send_tiles[0, 0, c, d], pick)
        live = (source == me) & (slot < counts[0, 0, d])
        code = jnp.where(live, pick * nu + which, -1)
        terms = lax.broadcasted_iota(jnp.int32, (coef.shape[2], code.shape[1]), 0)
        total = jnp.sum(jnp.where(code == terms, 1.0, 0.0).astype(F32), axis=1, keepdims=True)
        coef[0, p] = jnp.broadcast_to(total, coef.shape[2:])

    def exchange(e, s):
        h = N >> (s + 1)
        return pltpu.make_async_remote_copy(
            src_ref=part.at[e, pl.ds(h, h)], dst_ref=got.at[e, pl.ds(h, h)],
            send_sem=x_send.at[e, s], recv_sem=x_recv.at[e, s],
            device_id={"sub": partner(s)}, device_id_type=MESH,
        )

    def chunk(e):
        c = jnp.where(helper, e - H, jnp.where(helped, jnp.where(e < H, C - H + e, e - H), e))
        return jnp.maximum(c, 0)

    def strip_rows(c):
        return pl.ds(pl.multiple_of(c * rows, 8), rows)

    def solve(e):
        helping = helper & (e < H)
        late = helped & (e < H)
        c = chunk(e)
        at = strip_rows(c)
        k_late = (G - 1) * C - H + e

        @pl.when(helping)
        def _():
            there = ally * strip + (C - H + e) * rows
            work[...] = s_buf[pl.ds(pl.multiple_of(there, 8), rows), :]

        @pl.when(jnp.logical_not(helping))
        def _():
            work[...] = f_buf[at, :] - s_buf[pl.ds(pl.multiple_of(z * strip + c * rows, 8), rows), :]

            @pl.when((z > 0) & jnp.logical_not(late & helped_up))
            def _():
                k = (G - 1 - z) * C + c
                up_copy(k).wait_recv()
                work[...] = work[...] - mail[k]

            @pl.when((z < G - 1) & jnp.logical_not(late & helped_dn))
            def _():
                k = z * C + c
                dn_copy(k).wait_recv()
                work[...] = work[...] - mail[top - k]

        half = nt * rows
        for j in range(nt):
            cols = slice(j * tile, (j + 1) * tile)
            high, low = split(work[:, cols])
            solved = dot3(jnp.concatenate([high, low], axis=0), d_hi[j], d_lo[j])
            work[:, cols] = solved
            high, low = split(solved)
            x_buf[j * rows : (j + 1) * rows, :] = high
            x_buf[half + j * rows : half + (j + 1) * rows, :] = low

        @pl.when(jnp.logical_not(helping))
        def _():
            pan[at, :] = work[...]

        @pl.when(helping & low_end)
        def _():
            mail[k_late] = work[...]
            up_copy(k_late).start()

        @pl.when(helping & high_end)
        def _():
            mail[top - k_late] = work[...]
            dn_copy(k_late).start()

        for u in range(nu):
            prod[u] = dot3(x_buf[...], v_hi[u], v_lo[u])

        @pl.when(helping & (e == 0))
        def _():
            coef_copy().wait_recv()

        table = jnp.where(helping, 1, 0)

        def mix(g):
            p0 = g * group

            @pl.loop(0, rows, step=8)
            def _(r):
                r = pl.multiple_of(r, 8)
                sums = [None] * group
                for j in range(nt):
                    for u in range(nu):
                        value = prod[u, pl.ds(j * rows + r, 8), :]
                        for q in range(group):
                            n = j * nu + u
                            term = coef[table, p0 + q, n : n + 1, :] * value
                            sums[q] = term if sums[q] is None else sums[q] + term
                for q in range(group):
                    part[e, p0 + q, pl.ds(r, 8), :] = sums[q]

        groups = N // group
        pl.loop(groups // 2, groups)(mix)
        exchange(e, 0).start()
        pl.loop(0, groups // 2)(mix)

    def stage(e, s):
        h = N >> (s + 1)
        exchange(e, s).wait_recv()
        if s < steps - 1:
            q = h // 2
            part[e, q:h] = part[e, q:h] + got[e, h + q : 2 * h]
            exchange(e, s + 1).start()
            part[e, 0:q] = part[e, 0:q] + got[e, h : h + q]
        else:
            helping = helper & (e < H)

            @pl.when(helping)
            def _():
                ahead[e] = part[e, 0] + got[e, 1]
                ahead_copy(e).start()

            @pl.when(jnp.logical_not(helping))
            def _():
                at = strip_rows(chunk(e))
                upd[at, :] = t_buf[at, :] - (part[e, 0] + got[e, 1])

    lag_up, lag_dn = z, G - 1 - z
    base = jnp.maximum((G - 1 - z) * C + lag_up, z * C + lag_dn)
    last = max(max((G - 1 - i) * C + i, i * C + G - 1 - i) for i in range(G))

    @pl.loop(0, last + C + LAG * steps)
    def _(i):
        up, down, own = i - lag_up, i - lag_dn, i - base
        e = own + extra
        has_up = (up >= jnp.where(low_end, per, 0)) & (up < (G - 1 - z) * C)
        has_dn = (down >= jnp.where(high_end, per, 0)) & (down < z * C)
        plain = (G - 1) * C - extra
        up_row = (G - 1) * strip + lax.rem(jnp.maximum(up, 0), C) * rows - lax.div(jnp.maximum(up, 0), C) * strip

        @pl.loop(0, 3)
        def _(job):
            k = jnp.where(job == 0, up, jnp.where(job == 1, down, own + C))
            has = ((job == 0) & has_up) | ((job == 1) & has_dn) | ((job == 2) & (k >= 0) & (k < C))
            row = jnp.where(job == 0, up_row, jnp.where(job == 1, down * rows, z * strip + k * rows))

            @pl.when(has & (lax.rem(jnp.maximum(k, 0), per) == 0))
            def _():
                schur(row)

        @pl.when(has_up & (up < plain))
        def _():
            @pl.when(z > 0)
            def _():
                up_copy(up).wait_recv()

            forward(up, up_row, z == 0)
            up_copy(up).start()

        @pl.when(has_dn & (down < plain))
        def _():
            @pl.when(z < G - 1)
            def _():
                dn_copy(down).wait_recv()

            forward(top - down, down * rows, z == G - 1)
            dn_copy(down).start()

        @pl.when(i == 1)
        def _():
            own_list().start()

            @pl.loop(1, N)
            def _(p):
                list_copy(p, me).start()

            for copy in tails + others:
                copy.wait()
            for j in range(nt):
                high, low = split(d_buf[j])
                d_hi[j] = high
                d_lo[j] = low
            for u in range(nu):
                high, low = split(v_buf[u])
                v_hi[u] = high
                v_lo[u] = low

        @pl.when(i == 3)
        def _():
            pl.loop(0, N)(weigh)

            @pl.when(helped)
            def _():
                coef_copy().start()

        for s in reversed(range(steps)):
            old = e - LAG * (s + 1)

            @pl.when((old >= 0) & (old < C + extra))
            def _():
                stage(old, s)

        @pl.when((e >= 0) & (e < C + extra))
        def _():
            solve(e)

    @pl.when(helped)
    def _():
        @pl.loop(0, H)
        def _(e):
            at = strip_rows(C - H + e)
            k = (G - 1) * C - H + e

            @pl.when(helped_up)
            def _():
                up_copy(k).wait_recv()
                pan[at, :] = pan[at, :] - mail[k]

            @pl.when(helped_dn)
            def _():
                dn_copy(k).wait_recv()
                pan[at, :] = pan[at, :] - mail[top - k]

            ahead_copy(e).wait_recv()
            upd[at, :] = upd[at, :] + ahead[e]

        coef_copy().wait_send()

    @pl.when(helper)
    def _():
        pl.loop(0, H)(lambda e: ahead_copy(e).wait_send())

    @pl.loop(0, (G - 1 - z) * C)
    def _(k):
        up_copy(k).wait_send()

    @pl.loop(0, z * C)
    def _(k):
        dn_copy(k).wait_send()

    @pl.loop(1, N)
    def _(p):
        list_copy(p, me).wait_send()

    @pl.loop(0, C + extra)
    def _(e):
        for s in range(steps):
            exchange(e, s).wait_send()


def per_device(leaf_l, leaf_u, front, inv_diag, send_tiles, counts, trail_list, upper, trailing):
    G = lax.axis_size("grp")
    N = lax.axis_size("sub")
    strip, width = front.shape[1:]
    depth = leaf_u.shape[1]
    tile = upper.shape[1]
    rows = next(r for r in ROWS if strip % r == 0)
    C = strip // rows
    H = min(AHEAD, C) if G > 3 else 0
    block = 2 * rows if strip % (2 * rows) == 0 else strip
    nt, nu = width // tile, upper.shape[0]
    terms = -(-nt * nu // 8) * 8
    send_tiles = jnp.transpose(send_tiles, (0, 1, 3, 2))
    trail_list = jnp.transpose(trail_list, (0, 3, 1, 2))
    anywhere = pl.BlockSpec(memory_space=pl.ANY)
    vmem = pl.BlockSpec(memory_space=pltpu.VMEM)
    smem = pl.BlockSpec(memory_space=pltpu.SMEM)
    hops = (G - 1) * C
    steps = N.bit_length() - 1
    dma = pltpu.SemaphoreType.DMA
    panel, updated = pl.pallas_call(
        functools.partial(kernel, G, N, C, H, rows, block),
        out_shape=(pltpu.VMEM(front.shape[1:], F32), pltpu.VMEM(trailing.shape[1:], F32)),
        in_specs=[anywhere] * 4 + [smem, smem, vmem, anywhere, anywhere],
        out_specs=(vmem, vmem),
        scratch_shapes=[
            pltpu.VMEM(leaf_l.shape[1:], F32),
            pltpu.VMEM((2 * block, depth), BF16),
            pltpu.VMEM((depth, width), F32),
            pltpu.VMEM((depth, width), BF16),
            pltpu.VMEM((depth, width), BF16),
            pltpu.VMEM((G * strip, width), F32),
            pltpu.VMEM((strip, width), F32),
            pltpu.VMEM(inv_diag.shape[1:], F32),
            pltpu.VMEM(inv_diag.shape[1:], BF16),
            pltpu.VMEM(inv_diag.shape[1:], BF16),
            pltpu.VMEM(upper.shape, F32),
            pltpu.VMEM(upper.shape, BF16),
            pltpu.VMEM(upper.shape, BF16),
            pltpu.VMEM((strip, tile), F32),
            pltpu.VMEM(((G + 1) * C, rows, width), F32),
            pltpu.VMEM((N,) + trail_list.shape[1:], jnp.int32),
            pltpu.VMEM((2, N, terms, tile), F32),
            pltpu.VMEM((rows, width), F32),
            pltpu.VMEM((2 * nt * rows, tile), BF16),
            pltpu.VMEM((nu, nt * rows, tile), F32),
            pltpu.VMEM((C + H, N, rows, tile), F32),
            pltpu.VMEM((C + H, N, rows, tile), F32),
            pltpu.VMEM((max(H, 1), rows, tile), F32),
            dma((nt + G + 6,)),
            dma((hops,)), dma((hops,)), dma((hops,)), dma((hops,)),
            dma((N,)), dma((N,)),
            dma((C + H, steps)), dma((C + H, steps)),
            dma((2,)), dma((max(H, 1),)), dma((max(H, 1),)),
        ],
        compiler_params=pltpu.CompilerParams(
            collective_id=0, has_side_effects=True, vmem_limit_bytes=60 << 20
        ),
    )(leaf_l, leaf_u, front, inv_diag, send_tiles, counts, trail_list, upper, trailing)
    return write_out(panel, updated)


def copy_kernel(cuts, panel, updated, panel_out, updated_out, sem):
    rows = panel.shape[0] // cuts
    copies = [pltpu.make_async_copy(updated, updated_out.at[0], sem.at[cuts])]
    for i in range(cuts):
        at = pl.ds(i * rows, rows)
        copies.append(pltpu.make_async_copy(panel.at[at], panel_out.at[0, at], sem.at[i]))
    for copy in copies:
        copy.start()
    for copy in copies:
        copy.wait()


def write_out(panel, updated):
    strip = panel.shape[0]
    cuts = next(n for n in (4, 2, 1) if strip % (8 * n) == 0)
    vmem = pl.BlockSpec(memory_space=pltpu.VMEM)
    anywhere = pl.BlockSpec(memory_space=pl.ANY)
    return pl.pallas_call(
        functools.partial(copy_kernel, cuts),
        out_shape=tuple(jax.ShapeDtypeStruct((1,) + x.shape, F32) for x in (panel, updated)),
        in_specs=[vmem, vmem],
        out_specs=(anywhere, anywhere),
        scratch_shapes=[pltpu.SemaphoreType.DMA((cuts + 1,))],
        compiler_params=pltpu.CompilerParams(vmem_limit_bytes=1 << 20),
    )(panel, updated)


def solution(mesh):
    placed = (
        P("sub", "grp", None),
        P("sub", "grp", None),
        P("sub", "grp", None),
        P("sub", None, None, None),
        P("sub", "grp", None, None),
        P("sub", "grp", None),
        P("sub", "grp", None, None),
        P(),
        P("sub", "grp", None),
    )
    return jax.shard_map(
        per_device,
        mesh=mesh,
        in_specs=placed,
        out_specs=(P("sub", "grp", None), P("sub", "grp", None)),
        check_vma=False,
    )
```

```python
import functools

import jax
import jax.numpy as jnp
from jax import lax
from jax.experimental import pallas as pl
from jax.experimental.pallas import tpu as pltpu
from jax.sharding import PartitionSpec as P

MESH = pl.DeviceIdType.MESH
F32 = jnp.float32
BF16 = jnp.bfloat16
ROWS = (32, 16, 8)
AHEAD = 3
LAG = 2


def split(x):
    high = x.astype(BF16)
    return high, (x - high.astype(F32)).astype(BF16)


def dot(a, b):
    return jnp.dot(a, b, preferred_element_type=F32)


def dot3(stacked, high, low):
    m = stacked.shape[0] // 2
    both = dot(stacked, high)
    return both[:m] + both[m:] + dot(stacked[:m], low)


def kernel(
    G, N, C, H, rows, block,
    leaf_l, leaf_u, front, inv_diag, send_tiles, counts, trail_list, upper, trailing,
    pan, upd,
    tiles_buf, counts_buf, l_buf, l_two, u_buf, u_hi, u_lo, s_buf, f_buf, d_buf, d_hi, d_lo, v_buf, v_hi, v_lo, t_buf, mail,
    lists, coef, work, x_buf, prod, part, got, ahead,
    in_sem, send_sem, many_recv, up_recv, dn_recv, list_sem, x_send, x_recv, coef_sem, ahead_sem,
):
    z = lax.axis_index("grp")
    me = lax.axis_index("sub")
    width = front.shape[2]
    tile = upper.shape[1]
    depth = u_buf.shape[0]
    nt = width // tile
    nu = upper.shape[0]
    cap = send_tiles.shape[2]
    strip = C * rows
    per = block // rows
    group = min(4, N // 2)
    steps = N.bit_length() - 1
    top = (G + 1) * C - 1
    low_end, high_end = z == 0, z == G - 1
    helper = (H > 0) & (low_end | high_end)
    helped_up, helped_dn = (H > 0) & (z == 1), (H > 0) & (z == G - 2)
    helped = helped_up | helped_dn
    ally = jnp.where(low_end | (z == G - 2), z + 1, z - 1)
    extra = jnp.where(helper, H, 0)

    def bit(value, s):
        return lax.rem(lax.div(value, 1 << s), 2)

    def partner(s):
        return me + (1 << s) * (1 - 2 * bit(me, s))

    def dest_of(p):
        return sum((1 << s) * lax.rem(bit(me, s) + bit(p, steps - 1 - s), 2) for s in range(steps))

    def load_l(t, first, count, n):
        at = pl.ds(t * strip + first, count)
        return pltpu.make_async_copy(leaf_l.at[0, at], l_buf.at[at], in_sem.at[n])

    def load_u(n):
        cols = pl.ds(pl.multiple_of(n * tile, tile), tile)
        return pltpu.make_async_copy(leaf_u.at[0, :, cols], u_buf.at[:, cols], in_sem.at[n])

    heads = [load_l(G - 1, 0, block, nt), load_l(0, 0, block, nt + 1)]
    tails = [load_l(0, block, (G - 1) * strip - block, nt + 2)]
    if block < strip:
        tails.append(load_l(G - 1, block, strip - block, nt + 3))
    others = [
        pltpu.make_async_copy(front.at[0], f_buf, in_sem.at[nt + 4]),
        pltpu.make_async_copy(inv_diag.at[0], d_buf, in_sem.at[nt + 5]),
        pltpu.make_async_copy(trailing.at[0], t_buf, in_sem.at[nt + 6]),
        pltpu.make_async_copy(upper, v_buf, in_sem.at[nt + 7]),
        pltpu.make_async_copy(send_tiles, tiles_buf, in_sem.at[nt + 8]),
        pltpu.make_async_copy(counts, counts_buf, in_sem.at[nt + 9]),
    ]
    heads[0].start()
    heads[1].start()
    pl.loop(0, nt)(lambda n: load_u(n).start())
    for copy in tails + others:
        copy.start()

    barrier = pltpu.get_barrier_semaphore()

    @pl.loop(1, N)
    def _(p):
        pl.semaphore_signal(barrier, inc=1, device_id={"sub": dest_of(p)}, device_id_type=MESH)

    @pl.when(z > 0)
    def _():
        pl.semaphore_signal(barrier, inc=1, device_id={"grp": z - 1}, device_id_type=MESH)

    @pl.when(z < G - 1)
    def _():
        pl.semaphore_signal(barrier, inc=1, device_id={"grp": z + 1}, device_id_type=MESH)

    def own_list():
        return pltpu.make_async_copy(trail_list.at[0], lists.at[me], in_sem.at[nt + 10])

    def list_copy(p, owner):
        return pltpu.make_async_remote_copy(
            src_ref=trail_list.at[0], dst_ref=lists.at[owner],
            send_sem=list_sem.at[0], recv_sem=list_sem.at[1],
            device_id={"sub": dest_of(p)}, device_id_type=MESH,
        )

    def all_lists():
        return pltpu.make_async_remote_copy(
            src_ref=lists.at[pl.ds(0, N - 1)], dst_ref=lists.at[pl.ds(0, N - 1)],
            send_sem=list_sem.at[0], recv_sem=list_sem.at[1],
            device_id={"sub": dest_of(1)}, device_id_type=MESH,
        )

    def up_move(first, count, recv_sem, cols=slice(None)):
        at = pl.ds(first, count)
        return pltpu.make_async_remote_copy(
            src_ref=mail.at[at, :, cols], dst_ref=mail.at[at, :, cols],
            send_sem=send_sem.at[0], recv_sem=recv_sem,
            device_id={"grp": z + 1}, device_id_type=MESH,
        )

    def dn_move(first, count, recv_sem, cols=slice(None)):
        at = pl.ds(top + 1 - first - count, count)
        return pltpu.make_async_remote_copy(
            src_ref=mail.at[at, :, cols], dst_ref=mail.at[at, :, cols],
            send_sem=send_sem.at[1], recv_sem=recv_sem,
            device_id={"grp": z - 1}, device_id_type=MESH,
        )

    def up_copy(c, k):
        return up_move(k, 1, up_recv.at[c])

    def dn_copy(c, k):
        return dn_move(k, 1, dn_recv.at[c])

    def up_many(b, cols=slice(None)):
        return up_move(b * per, per, many_recv.at[b], cols)

    def dn_many(b, cols=slice(None)):
        return dn_move(b * per, per, many_recv.at[(G - 1) * C // per - 1 - b], cols)

    def coef_copy():
        return pltpu.make_async_remote_copy(
            src_ref=coef.at[0], dst_ref=coef.at[1],
            send_sem=coef_sem.at[0], recv_sem=coef_sem.at[1],
            device_id={"grp": ally}, device_id_type=MESH,
        )

    def ahead_copy(e):
        return pltpu.make_async_remote_copy(
            src_ref=ahead.at[e], dst_ref=ahead.at[e],
            send_sem=ahead_sem.at[0], recv_sem=ahead_sem.at[1],
            device_id={"grp": ally}, device_id_type=MESH,
        )

    def all_ahead():
        return pltpu.make_async_remote_copy(
            src_ref=ahead, dst_ref=ahead,
            send_sem=ahead_sem.at[0], recv_sem=ahead_sem.at[1],
            device_id={"grp": ally}, device_id_type=MESH,
        )

    def halve(row):
        at = pl.ds(pl.multiple_of(row, 8), block)
        high, low = split(l_buf[at, :])
        l_two[:block, :] = high
        l_two[block:, :] = low

    def product(row, n):
        at = pl.ds(pl.multiple_of(row, 8), block)
        cols = pl.ds(pl.multiple_of(n * tile, tile), tile)
        s_buf[at, cols] = dot3(l_two[...], u_hi[:, cols], u_lo[:, cols])

    def schur(row):
        halve(row)
        pl.loop(0, nt)(lambda n: product(row, n))

    def forward(slot, row, first):
        at = pl.ds(pl.multiple_of(row, 8), rows)

        @pl.when(first)
        def _():
            mail[slot] = s_buf[at, :]

        @pl.when(jnp.logical_not(first))
        def _():
            mail[slot] = mail[slot] + s_buf[at, :]

    def begin(n):
        cols = pl.ds(pl.multiple_of(n * tile, tile), tile)
        load_u(n).wait()

        @pl.loop(0, depth, step=16)
        def _(r):
            at = pl.ds(pl.multiple_of(r, 16), 16)
            high, low = split(u_buf[at, cols])
            u_hi[at, cols] = high
            u_lo[at, cols] = low

        @pl.when(low_end)
        def _():
            product((G - 1) * strip, n)

        @pl.when(high_end)
        def _():
            product(0, n)

    def begin_send(n):
        cols = pl.ds(pl.multiple_of(n * tile, tile), tile)

        @pl.when(low_end)
        def _():
            for k in range(per):
                mail[k, :, cols] = s_buf[(G - 1) * strip + k * rows : (G - 1) * strip + (k + 1) * rows, cols]
            up_many(0, cols).start()

        @pl.when(high_end)
        def _():
            for k in range(per):
                mail[top - k, :, cols] = s_buf[k * rows : (k + 1) * rows, cols]
            dn_many(0, cols).start()

    for head in heads:
        head.wait()

    @pl.when(low_end)
    def _():
        halve((G - 1) * strip)

    @pl.when(high_end)
    def _():
        halve(0)

    begin(0)
    pl.semaphore_wait(barrier, N - 1 + jnp.where(z > 0, 1, 0) + jnp.where(z < G - 1, 1, 0))
    begin_send(0)

    @pl.loop(1, nt)
    def _(n):
        begin(n)
        begin_send(n)

    def weigh(p):
        d = dest_of(p)

        source, slot, which = lists[d, 0], lists[d, 1], lists[d, 2]
        pick = jnp.zeros_like(source)
        for c in range(cap):
            pick = jnp.where(slot == c, tiles_buf[0, 0, c, d], pick)
        live = (source == me) & (slot < counts_buf[0, 0, d])
        code = jnp.where(live, pick * nu + which, -1)
        terms = lax.broadcasted_iota(jnp.int32, (coef.shape[2], code.shape[1]), 0)
        total = jnp.sum(jnp.where(code == terms, 1.0, 0.0).astype(F32), axis=1, keepdims=True)
        coef[0, p] = jnp.broadcast_to(total, coef.shape[2:])

    def exchange(e, s):
        h = N >> (s + 1)
        return pltpu.make_async_remote_copy(
            src_ref=part.at[e, pl.ds(h, h)], dst_ref=got.at[e, pl.ds(h, h)],
            send_sem=x_send.at[s], recv_sem=x_recv.at[lax.rem(e, 2 * LAG), s],
            device_id={"sub": partner(s)}, device_id_type=MESH,
        )

    def chunk(e):
        c = jnp.where(helper, e - H, jnp.where(helped, jnp.where(e < H, C - H + e, e - H), e))
        return jnp.maximum(c, 0)

    def strip_rows(c):
        return pl.ds(pl.multiple_of(c * rows, 8), rows)

    def solve(e):
        helping = helper & (e < H)
        late = helped & (e < H)
        c = chunk(e)
        at = strip_rows(c)
        k_late = (G - 1) * C - H + e

        @pl.when(helping)
        def _():
            there = ally * strip + (C - H + e) * rows
            work[...] = s_buf[pl.ds(pl.multiple_of(there, 8), rows), :]

        @pl.when(jnp.logical_not(helping))
        def _():
            work[...] = f_buf[at, :] - s_buf[pl.ds(pl.multiple_of(z * strip + c * rows, 8), rows), :]

            @pl.when((z > 0) & jnp.logical_not(late & helped_up))
            def _():
                k = (G - 1 - z) * C + c
                up_copy(c, k).wait_recv()
                work[...] = work[...] - mail[k]

            @pl.when((z < G - 1) & jnp.logical_not(late & helped_dn))
            def _():
                k = z * C + c
                dn_copy(c, k).wait_recv()
                work[...] = work[...] - mail[top - k]

        half = nt * rows
        for j in range(nt):
            cols = slice(j * tile, (j + 1) * tile)
            high, low = split(work[:, cols])
            solved = dot3(jnp.concatenate([high, low], axis=0), d_hi[j], d_lo[j])
            work[:, cols] = solved
            high, low = split(solved)
            x_buf[j * rows : (j + 1) * rows, :] = high
            x_buf[half + j * rows : half + (j + 1) * rows, :] = low

        @pl.when(jnp.logical_not(helping))
        def _():
            pan[at, :] = work[...]

        @pl.when(helping & low_end)
        def _():
            mail[k_late] = work[...]
            up_copy(C - H + e, k_late).start()

        @pl.when(helping & high_end)
        def _():
            mail[top - k_late] = work[...]
            dn_copy(C - H + e, k_late).start()

        for u in range(nu):
            prod[u] = dot3(x_buf[...], v_hi[u], v_lo[u])

        @pl.when(helping & (e == 0))
        def _():
            coef_copy().wait_recv()

        table = jnp.where(helping, 1, 0)

        def mix(g):
            p0 = g * group

            @pl.loop(0, rows, step=8)
            def _(r):
                r = pl.multiple_of(r, 8)
                sums = [None] * group
                for j in range(nt):
                    for u in range(nu):
                        value = prod[u, pl.ds(j * rows + r, 8), :]
                        for q in range(group):
                            n = j * nu + u
                            term = coef[table, p0 + q, n : n + 1, :] * value
                            sums[q] = term if sums[q] is None else sums[q] + term
                for q in range(group):
                    part[e, p0 + q, pl.ds(r, 8), :] = sums[q]

        groups = N // group
        pl.loop(groups // 2, groups)(mix)
        exchange(e, 0).start()
        pl.loop(0, groups // 2)(mix)

    def stage(e, s):
        h = N >> (s + 1)
        exchange(e, s).wait_recv()
        if s < steps - 1:
            q = h // 2
            part[e, q:h] = part[e, q:h] + got[e, h + q : 2 * h]
            exchange(e, s + 1).start()
            part[e, 0:q] = part[e, 0:q] + got[e, h : h + q]
        else:
            helping = helper & (e < H)

            @pl.when(helping)
            def _():
                ahead[e] = part[e, 0] + got[e, 1]
                ahead_copy(e).start()

            @pl.when(jnp.logical_not(helping))
            def _():
                at = strip_rows(chunk(e))
                upd[at, :] = t_buf[at, :] - (part[e, 0] + got[e, 1])

    lag_up, lag_dn = z * per, (G - 1 - z) * per
    base = jnp.maximum((G - 1 - z) * C + lag_up, z * C + lag_dn)
    last = max(max((G - 1 - i) * C + i * per, i * C + (G - 1 - i) * per) for i in range(G))

    @pl.loop(0, last + C + LAG * steps)
    def _(i):
        up, down, own = i - lag_up, i - lag_dn, i - base
        e = own + extra
        has_up = (up >= jnp.where(low_end, per, 0)) & (up < (G - 1 - z) * C)
        has_dn = (down >= jnp.where(high_end, per, 0)) & (down < z * C)
        plain = (G - 1) * C - extra
        up_row = (G - 1) * strip + lax.rem(jnp.maximum(up, 0), C) * rows - lax.div(jnp.maximum(up, 0), C) * strip

        @pl.loop(0, 3)
        def _(job):
            k = jnp.where(job == 0, up, jnp.where(job == 1, down, own + C))
            has = ((job == 0) & has_up) | ((job == 1) & has_dn) | ((job == 2) & (k >= 0) & (k < C))
            row = jnp.where(job == 0, up_row, jnp.where(job == 1, down * rows, z * strip + k * rows))

            @pl.when(has & (lax.rem(jnp.maximum(k, 0), per) == 0))
            def _():
                schur(row)

        @pl.when(has_up & (up < plain))
        def _():
            place = lax.rem(up, per)
            final = (G - 2 - z) * C

            @pl.when((z > 0) & (place == 0))
            def _():
                up_many(lax.div(up, per)).wait_recv()

            forward(up, up_row, z == 0)

            @pl.when((up < final) & (place == per - 1))
            def _():
                up_many(lax.div(up, per)).start()

            @pl.when(up >= final)
            def _():
                up_copy(up - final, up).start()

        @pl.when(has_dn & (down < plain))
        def _():
            place = lax.rem(down, per)
            final = (z - 1) * C

            @pl.when((z < G - 1) & (place == 0))
            def _():
                dn_many(lax.div(down, per)).wait_recv()

            forward(top - down, down * rows, z == G - 1)

            @pl.when((down < final) & (place == per - 1))
            def _():
                dn_many(lax.div(down, per)).start()

            @pl.when(down >= final)
            def _():
                dn_copy(down - final, down).start()

        @pl.when(i == 1)
        def _():
            own_list().start()

            @pl.loop(1, N)
            def _(p):
                list_copy(p, me).start()

            for copy in tails + others:
                copy.wait()
            for j in range(nt):
                high, low = split(d_buf[j])
                d_hi[j] = high
                d_lo[j] = low
            for u in range(nu):
                high, low = split(v_buf[u])
                v_hi[u] = high
                v_lo[u] = low

        @pl.when(i == 3)
        def _():
            own_list().wait()
            all_lists().wait_recv()
            pl.loop(0, N)(weigh)

            @pl.when(helped)
            def _():
                coef_copy().start()

        for s in reversed(range(steps)):
            old = e - LAG * (s + 1)

            @pl.when((old >= 0) & (old < C + extra))
            def _():
                stage(old, s)

        @pl.when((e >= 0) & (e < C + extra))
        def _():
            solve(e)

    @pl.when(helped)
    def _():
        @pl.loop(0, H)
        def _(e):
            at = strip_rows(C - H + e)
            k = (G - 1) * C - H + e

            @pl.when(helped_up)
            def _():
                up_copy(C - H + e, k).wait_recv()
                pan[at, :] = pan[at, :] - mail[k]

            @pl.when(helped_dn)
            def _():
                dn_copy(C - H + e, k).wait_recv()
                pan[at, :] = pan[at, :] - mail[top - k]

        all_ahead().wait_recv()

        @pl.loop(0, H)
        def _(e):
            at = strip_rows(C - H + e)
            upd[at, :] = upd[at, :] + ahead[e]

        coef_copy().wait_send()

    for g in range(G):
        @pl.when(z == g)
        def _():
            if g < G - 1:
                up_move(0, (G - 1 - g) * C, up_recv.at[0]).wait_send()
            if g > 0:
                dn_move(0, g * C, dn_recv.at[0]).wait_send()
            worked = C + (H if g in (0, G - 1) else 0)
            for s in range(steps):
                h = N >> (s + 1)
                sent = part.at[pl.ds(0, worked), pl.ds(h, h)]
                pltpu.make_async_remote_copy(
                    src_ref=sent, dst_ref=sent, send_sem=x_send.at[s], recv_sem=x_recv.at[0, s],
                    device_id={"sub": partner(s)}, device_id_type=MESH,
                ).wait_send()

    if H:
        @pl.when(helper)
        def _():
            all_ahead().wait_send()

    all_lists().wait_send()


def per_device(leaf_l, leaf_u, front, inv_diag, send_tiles, counts, trail_list, upper, trailing):
    G = lax.axis_size("grp")
    N = lax.axis_size("sub")
    strip, width = front.shape[1:]
    depth = leaf_u.shape[1]
    tile = upper.shape[1]
    rows = next(r for r in ROWS if strip % r == 0)
    C = strip // rows
    H = min(AHEAD, C) if G > 3 else 0
    block = 2 * rows if strip % (2 * rows) == 0 else strip
    nt, nu = width // tile, upper.shape[0]
    terms = -(-nt * nu // 8) * 8
    send_tiles = jnp.transpose(send_tiles, (0, 1, 3, 2))
    trail_list = jnp.transpose(trail_list, (0, 3, 1, 2))
    anywhere = pl.BlockSpec(memory_space=pl.ANY)
    vmem = pl.BlockSpec(memory_space=pltpu.VMEM)
    steps = N.bit_length() - 1
    dma = pltpu.SemaphoreType.DMA
    panel, updated = pl.pallas_call(
        functools.partial(kernel, G, N, C, H, rows, block),
        out_shape=(pltpu.VMEM(front.shape[1:], F32), pltpu.VMEM(trailing.shape[1:], F32)),
        in_specs=[anywhere] * 9,
        out_specs=(vmem, vmem),
        scratch_shapes=[
            pltpu.SMEM(send_tiles.shape, jnp.int32),
            pltpu.SMEM(counts.shape, jnp.int32),
            pltpu.VMEM(leaf_l.shape[1:], F32),
            pltpu.VMEM((2 * block, depth), BF16),
            pltpu.VMEM((depth, width), F32),
            pltpu.VMEM((depth, width), BF16),
            pltpu.VMEM((depth, width), BF16),
            pltpu.VMEM((G * strip, width), F32),
            pltpu.VMEM((strip, width), F32),
            pltpu.VMEM(inv_diag.shape[1:], F32),
            pltpu.VMEM(inv_diag.shape[1:], BF16),
            pltpu.VMEM(inv_diag.shape[1:], BF16),
            pltpu.VMEM(upper.shape, F32),
            pltpu.VMEM(upper.shape, BF16),
            pltpu.VMEM(upper.shape, BF16),
            pltpu.VMEM((strip, tile), F32),
            pltpu.VMEM(((G + 1) * C, rows, width), F32),
            pltpu.VMEM((N,) + trail_list.shape[1:], jnp.int32),
            pltpu.VMEM((2, N, terms, tile), F32),
            pltpu.VMEM((rows, width), F32),
            pltpu.VMEM((2 * nt * rows, tile), BF16),
            pltpu.VMEM((nu, nt * rows, tile), F32),
            pltpu.VMEM((C + H, N, rows, tile), F32),
            pltpu.VMEM((C + H, N, rows, tile), F32),
            pltpu.VMEM((max(H, 1), rows, tile), F32),
            dma((nt + 11,)),
            dma((2,)), dma(((G - 1) * C * rows // block,)), dma((C,)), dma((C,)),
            dma((2,)),
            dma((steps,)), dma((2 * LAG, steps)),
            dma((2,)), dma((2,)),
        ],
        compiler_params=pltpu.CompilerParams(
            collective_id=0, has_side_effects=True, vmem_limit_bytes=60 << 20
        ),
    )(leaf_l, leaf_u, front, inv_diag, send_tiles, counts, trail_list, upper, trailing)
    return write_out(panel, updated)


def copy_kernel(cuts, panel, updated, panel_out, updated_out, sem):
    rows = panel.shape[0] // cuts
    copies = [pltpu.make_async_copy(updated, updated_out.at[0], sem.at[cuts])]
    for i in range(cuts):
        at = pl.ds(i * rows, rows)
        copies.append(pltpu.make_async_copy(panel.at[at], panel_out.at[0, at], sem.at[i]))
    for copy in copies:
        copy.start()
    for copy in copies:
        copy.wait()


def write_out(panel, updated):
    strip = panel.shape[0]
    cuts = next(n for n in (4, 2, 1) if strip % (8 * n) == 0)
    vmem = pl.BlockSpec(memory_space=pltpu.VMEM)
    anywhere = pl.BlockSpec(memory_space=pl.ANY)
    return pl.pallas_call(
        functools.partial(copy_kernel, cuts),
        out_shape=tuple(jax.ShapeDtypeStruct((1,) + x.shape, F32) for x in (panel, updated)),
        in_specs=[vmem, vmem],
        out_specs=(anywhere, anywhere),
        scratch_shapes=[pltpu.SemaphoreType.DMA((cuts + 1,))],
        compiler_params=pltpu.CompilerParams(vmem_limit_bytes=1 << 20),
    )(panel, updated)


def solution(mesh):
    placed = (
        P("sub", "grp", None),
        P("sub", "grp", None),
        P("sub", "grp", None),
        P("sub", None, None, None),
        P("sub", "grp", None, None),
        P("sub", "grp", None),
        P("sub", "grp", None, None),
        P(),
        P("sub", "grp", None),
    )
    return jax.shard_map(
        per_device,
        mesh=mesh,
        in_specs=placed,
        out_specs=(P("sub", "grp", None), P("sub", "grp", None)),
        check_vma=False,
    )
```

```python
import functools

import jax
import jax.numpy as jnp
from jax import lax
from jax.experimental import pallas as pl
from jax.experimental.pallas import tpu as pltpu
from jax.sharding import PartitionSpec as P

MESH = pl.DeviceIdType.MESH
F32 = jnp.float32
BF16 = jnp.bfloat16
ROWS = (32, 16, 8)
AHEAD = 2
LAGS = (2, 4)
RING = 6


def split(x):
    high = x.astype(BF16)
    return high, (x - high.astype(F32)).astype(BF16)


def dot(a, b):
    return jnp.dot(a, b, preferred_element_type=F32)


def dot3(stacked, high, low):
    m = stacked.shape[0] // 2
    both = dot(stacked, high)
    return both[:m] + both[m:] + dot(stacked[:m], low)


def kernel(
    G, N, C, H, rows, block,
    leaf_l, leaf_u, front, inv_diag, send_tiles, counts, trail_list, upper, trailing,
    pan, upd,
    tiles_buf, counts_buf, l_buf, l_two, u_buf, u_hi, u_lo, s_buf, f_buf, d_buf, d_hi, d_lo, v_buf, v_hi, v_lo, t_buf, mail,
    lists, coef, work, x_buf, prod, part, got, ahead,
    in_sem, send_sem, many_recv, up_recv, dn_recv, list_sem, x_send, x_recv, coef_sem, ahead_sem,
):
    z = lax.axis_index("grp")
    me = lax.axis_index("sub")
    width = front.shape[2]
    tile = upper.shape[1]
    depth = u_buf.shape[0]
    nt = width // tile
    nu = upper.shape[0]
    cap = send_tiles.shape[2]
    strip = C * rows
    per = block // rows
    group = min(4, N // 2)
    steps = N.bit_length() - 1
    half_n = N // 2
    top = (G + 1) * C - 1
    low_end, high_end = z == 0, z == G - 1
    helper = (H > 0) & (low_end | high_end)
    helped_up, helped_dn = (H > 0) & (z == 1), (H > 0) & (z == G - 2)
    helped = helped_up | helped_dn
    ally = jnp.where(low_end | (z == G - 2), z + 1, z - 1)
    extra = jnp.where(helper, H, 0)

    def bit(value, s):
        return lax.rem(lax.div(value, 1 << s), 2)

    def dest_of(p):
        return sum((1 << s) * lax.rem(bit(me, s) + bit(p, steps - 1 - s), 2) for s in range(steps))

    def load_l(t, first, count, n):
        at = pl.ds(t * strip + first, count)
        return pltpu.make_async_copy(leaf_l.at[0, at], l_buf.at[at], in_sem.at[n])

    def load_u(n):
        cols = pl.ds(pl.multiple_of(n * tile, tile), tile)
        return pltpu.make_async_copy(leaf_u.at[0, :, cols], u_buf.at[:, cols], in_sem.at[n])

    heads = [load_l(G - 1, 0, block, nt), load_l(0, 0, block, nt + 1)]
    tails = [load_l(0, block, (G - 1) * strip - block, nt + 2)]
    if block < strip:
        tails.append(load_l(G - 1, block, strip - block, nt + 3))
    others = [
        pltpu.make_async_copy(front.at[0], f_buf, in_sem.at[nt + 4]),
        pltpu.make_async_copy(inv_diag.at[0], d_buf, in_sem.at[nt + 5]),
        pltpu.make_async_copy(trailing.at[0], t_buf, in_sem.at[nt + 6]),
        pltpu.make_async_copy(upper, v_buf, in_sem.at[nt + 7]),
        pltpu.make_async_copy(send_tiles, tiles_buf, in_sem.at[nt + 8]),
        pltpu.make_async_copy(counts, counts_buf, in_sem.at[nt + 9]),
    ]
    heads[0].start()
    heads[1].start()
    pl.loop(0, nt)(lambda n: load_u(n).start())
    for copy in tails + others:
        copy.start()

    barrier = pltpu.get_barrier_semaphore()

    @pl.loop(1, N)
    def _(p):
        pl.semaphore_signal(barrier, inc=1, device_id={"sub": dest_of(p)}, device_id_type=MESH)

    @pl.when(z > 0)
    def _():
        pl.semaphore_signal(barrier, inc=1, device_id={"grp": z - 1}, device_id_type=MESH)

    @pl.when(z < G - 1)
    def _():
        pl.semaphore_signal(barrier, inc=1, device_id={"grp": z + 1}, device_id_type=MESH)

    def own_list():
        return pltpu.make_async_copy(trail_list.at[0], lists.at[me], in_sem.at[nt + 10])

    def list_copy(p, owner):
        return pltpu.make_async_remote_copy(
            src_ref=trail_list.at[0], dst_ref=lists.at[owner],
            send_sem=list_sem.at[0], recv_sem=list_sem.at[1],
            device_id={"sub": dest_of(p)}, device_id_type=MESH,
        )

    def all_lists():
        return pltpu.make_async_remote_copy(
            src_ref=lists.at[pl.ds(0, N - 1)], dst_ref=lists.at[pl.ds(0, N - 1)],
            send_sem=list_sem.at[0], recv_sem=list_sem.at[1],
            device_id={"sub": dest_of(1)}, device_id_type=MESH,
        )

    def up_move(first, count, recv_sem, cols=slice(None)):
        at = pl.ds(first, count)
        return pltpu.make_async_remote_copy(
            src_ref=mail.at[at, :, cols], dst_ref=mail.at[at, :, cols],
            send_sem=send_sem.at[0], recv_sem=recv_sem,
            device_id={"grp": z + 1}, device_id_type=MESH,
        )

    def dn_move(first, count, recv_sem, cols=slice(None)):
        at = pl.ds(top + 1 - first - count, count)
        return pltpu.make_async_remote_copy(
            src_ref=mail.at[at, :, cols], dst_ref=mail.at[at, :, cols],
            send_sem=send_sem.at[1], recv_sem=recv_sem,
            device_id={"grp": z - 1}, device_id_type=MESH,
        )

    def up_copy(c, k):
        return up_move(k, 1, up_recv.at[c])

    def dn_copy(c, k):
        return dn_move(k, 1, dn_recv.at[c])

    def up_many(b, cols=slice(None)):
        return up_move(b * per, per, many_recv.at[b], cols)

    def dn_many(b, cols=slice(None)):
        return dn_move(b * per, per, many_recv.at[(G - 1) * C // per - 1 - b], cols)

    def coef_copy():
        return pltpu.make_async_remote_copy(
            src_ref=coef.at[0], dst_ref=coef.at[1],
            send_sem=coef_sem.at[0], recv_sem=coef_sem.at[1],
            device_id={"grp": ally}, device_id_type=MESH,
        )

    def ahead_copy(e):
        return pltpu.make_async_remote_copy(
            src_ref=ahead.at[e], dst_ref=ahead.at[e],
            send_sem=ahead_sem.at[0], recv_sem=ahead_sem.at[1],
            device_id={"grp": ally}, device_id_type=MESH,
        )

    def all_ahead():
        return pltpu.make_async_remote_copy(
            src_ref=ahead, dst_ref=ahead,
            send_sem=ahead_sem.at[0], recv_sem=ahead_sem.at[1],
            device_id={"grp": ally}, device_id_type=MESH,
        )

    def halve(row):
        at = pl.ds(pl.multiple_of(row, 8), block)
        high, low = split(l_buf[at, :])
        l_two[:block, :] = high
        l_two[block:, :] = low

    def product(row, n):
        at = pl.ds(pl.multiple_of(row, 8), block)
        cols = pl.ds(pl.multiple_of(n * tile, tile), tile)
        s_buf[at, cols] = dot3(l_two[...], u_hi[:, cols], u_lo[:, cols])

    def schur(row):
        halve(row)
        pl.loop(0, nt)(lambda n: product(row, n))

    def forward(slot, row, first):
        at = pl.ds(pl.multiple_of(row, 8), rows)

        @pl.when(first)
        def _():
            mail[slot] = s_buf[at, :]

        @pl.when(jnp.logical_not(first))
        def _():
            mail[slot] = mail[slot] + s_buf[at, :]

    def begin(n):
        cols = pl.ds(pl.multiple_of(n * tile, tile), tile)
        load_u(n).wait()

        @pl.loop(0, depth, step=16)
        def _(r):
            at = pl.ds(pl.multiple_of(r, 16), 16)
            high, low = split(u_buf[at, cols])
            u_hi[at, cols] = high
            u_lo[at, cols] = low

        @pl.when(low_end)
        def _():
            product((G - 1) * strip, n)

        @pl.when(high_end)
        def _():
            product(0, n)

    def begin_send(n):
        cols = pl.ds(pl.multiple_of(n * tile, tile), tile)

        @pl.when(low_end)
        def _():
            for k in range(per):
                mail[k, :, cols] = s_buf[(G - 1) * strip + k * rows : (G - 1) * strip + (k + 1) * rows, cols]
            up_many(0, cols).start()

        @pl.when(high_end)
        def _():
            for k in range(per):
                mail[top - k, :, cols] = s_buf[k * rows : (k + 1) * rows, cols]
            dn_many(0, cols).start()

    for head in heads:
        head.wait()

    @pl.when(low_end)
    def _():
        halve((G - 1) * strip)

    @pl.when(high_end)
    def _():
        halve(0)

    begin(0)
    pl.semaphore_wait(barrier, N - 1 + jnp.where(z > 0, 1, 0) + jnp.where(z < G - 1, 1, 0))
    begin_send(0)

    @pl.loop(1, nt)
    def _(n):
        begin(n)
        begin_send(n)

    def weigh(p):
        d = dest_of(p)

        source, slot, which = lists[d, 0], lists[d, 1], lists[d, 2]
        pick = jnp.zeros_like(source)
        for c in range(cap):
            pick = jnp.where(slot == c, tiles_buf[0, 0, c, d], pick)
        live = (source == me) & (slot < counts_buf[0, 0, d])
        code = jnp.where(live, pick * nu + which, -1)
        terms = lax.broadcasted_iota(jnp.int32, (coef.shape[2], code.shape[1]), 0)
        total = jnp.sum(jnp.where(code == terms, 1.0, 0.0).astype(F32), axis=1, keepdims=True)
        coef[0, p] = jnp.broadcast_to(total, coef.shape[2:])

    def exchange(e):
        return pltpu.make_async_remote_copy(
            src_ref=part.at[e, pl.ds(half_n, half_n)], dst_ref=got.at[e, pl.ds(half_n, half_n)],
            send_sem=x_send.at[0], recv_sem=x_recv.at[lax.rem(e, RING), 0],
            device_id={"sub": dest_of(half_n)}, device_id_type=MESH,
        )

    def scatter(e, p, count=1):
        return pltpu.make_async_remote_copy(
            src_ref=part.at[e, pl.ds(p, count)], dst_ref=got.at[e, pl.ds(p, count)],
            send_sem=x_send.at[1], recv_sem=x_recv.at[lax.rem(e, RING), 1],
            device_id={"sub": dest_of(p)}, device_id_type=MESH,
        )

    def chunk(e):
        c = jnp.where(helper, e - H, jnp.where(helped, jnp.where(e < H, C - H + e, e - H), e))
        return jnp.maximum(c, 0)

    def strip_rows(c):
        return pl.ds(pl.multiple_of(c * rows, 8), rows)

    def solve(e):
        helping = helper & (e < H)
        late = helped & (e < H)
        c = chunk(e)
        at = strip_rows(c)
        k_late = (G - 1) * C - H + e

        @pl.when(helping)
        def _():
            there = ally * strip + (C - H + e) * rows
            work[...] = s_buf[pl.ds(pl.multiple_of(there, 8), rows), :]

        @pl.when(jnp.logical_not(helping))
        def _():
            work[...] = f_buf[at, :] - s_buf[pl.ds(pl.multiple_of(z * strip + c * rows, 8), rows), :]

            @pl.when((z > 0) & jnp.logical_not(late & helped_up))
            def _():
                k = (G - 1 - z) * C + c
                up_copy(c, k).wait_recv()
                work[...] = work[...] - mail[k]

            @pl.when((z < G - 1) & jnp.logical_not(late & helped_dn))
            def _():
                k = z * C + c
                dn_copy(c, k).wait_recv()
                work[...] = work[...] - mail[top - k]

        half = nt * rows
        for j in range(nt):
            cols = slice(j * tile, (j + 1) * tile)
            high, low = split(work[:, cols])
            solved = dot3(jnp.concatenate([high, low], axis=0), d_hi[j], d_lo[j])
            work[:, cols] = solved
            high, low = split(solved)
            x_buf[j * rows : (j + 1) * rows, :] = high
            x_buf[half + j * rows : half + (j + 1) * rows, :] = low

        @pl.when(jnp.logical_not(helping))
        def _():
            pan[at, :] = work[...]

        @pl.when(helping & low_end)
        def _():
            mail[k_late] = work[...]
            up_copy(C - H + e, k_late).start()

        @pl.when(helping & high_end)
        def _():
            mail[top - k_late] = work[...]
            dn_copy(C - H + e, k_late).start()

        for u in range(nu):
            prod[u] = dot3(x_buf[...], v_hi[u], v_lo[u])

        @pl.when(helping & (e == 0))
        def _():
            coef_copy().wait_recv()

        table = jnp.where(helping, 1, 0)

        def mix(g):
            p0 = g * group

            @pl.loop(0, rows, step=8)
            def _(r):
                r = pl.multiple_of(r, 8)
                sums = [None] * group
                for j in range(nt):
                    for u in range(nu):
                        value = prod[u, pl.ds(j * rows + r, 8), :]
                        for q in range(group):
                            n = j * nu + u
                            term = coef[table, p0 + q, n : n + 1, :] * value
                            sums[q] = term if sums[q] is None else sums[q] + term
                for q in range(group):
                    part[e, p0 + q, pl.ds(r, 8), :] = sums[q]

        groups = N // group
        pl.loop(groups // 2, groups)(mix)
        exchange(e).start()
        pl.loop(0, groups // 2)(mix)

    def stage(e, s):
        if s == 0:
            exchange(e).wait_recv()
            if half_n > 1:
                part[e, 1:half_n] = part[e, 1:half_n] + got[e, half_n + 1 :]
                pl.loop(1, half_n)(lambda p: scatter(e, p).start())
            part[e, 0] = part[e, 0] + got[e, half_n]
        else:
            total = part[e, 0]
            if half_n > 1:
                scatter(e, 1, half_n - 1).wait_recv()
                for p in range(1, half_n):
                    total = total + got[e, p]
            helping = helper & (e < H)

            @pl.when(helping)
            def _():
                ahead[e] = total
                ahead_copy(e).start()

            @pl.when(jnp.logical_not(helping))
            def _():
                at = strip_rows(chunk(e))
                upd[at, :] = t_buf[at, :] - total

    lag_up, lag_dn = z * per, (G - 1 - z) * per
    base = jnp.maximum((G - 1 - z) * C + lag_up, z * C + lag_dn)
    last = max(max((G - 1 - i) * C + i * per, i * C + (G - 1 - i) * per) for i in range(G))

    @pl.loop(0, last + C + LAGS[1])
    def _(i):
        up, down, own = i - lag_up, i - lag_dn, i - base
        e = own + extra
        has_up = (up >= jnp.where(low_end, per, 0)) & (up < (G - 1 - z) * C)
        has_dn = (down >= jnp.where(high_end, per, 0)) & (down < z * C)
        plain = (G - 1) * C - extra
        up_row = (G - 1) * strip + lax.rem(jnp.maximum(up, 0), C) * rows - lax.div(jnp.maximum(up, 0), C) * strip

        @pl.loop(0, 3)
        def _(job):
            k = jnp.where(job == 0, up, jnp.where(job == 1, down, own + C))
            has = ((job == 0) & has_up) | ((job == 1) & has_dn) | ((job == 2) & (k >= 0) & (k < C))
            row = jnp.where(job == 0, up_row, jnp.where(job == 1, down * rows, z * strip + k * rows))

            @pl.when(has & (lax.rem(jnp.maximum(k, 0), per) == 0))
            def _():
                schur(row)

        @pl.when(has_up & (up < plain))
        def _():
            place = lax.rem(up, per)
            final = (G - 2 - z) * C

            @pl.when((z > 0) & (place == 0))
            def _():
                up_many(lax.div(up, per)).wait_recv()

            forward(up, up_row, z == 0)

            @pl.when((up < final) & (place == per - 1))
            def _():
                up_many(lax.div(up, per)).start()

            @pl.when(up >= final)
            def _():
                up_copy(up - final, up).start()

        @pl.when(has_dn & (down < plain))
        def _():
            place = lax.rem(down, per)
            final = (z - 1) * C

            @pl.when((z < G - 1) & (place == 0))
            def _():
                dn_many(lax.div(down, per)).wait_recv()

            forward(top - down, down * rows, z == G - 1)

            @pl.when((down < final) & (place == per - 1))
            def _():
                dn_many(lax.div(down, per)).start()

            @pl.when(down >= final)
            def _():
                dn_copy(down - final, down).start()

        @pl.when(i == 1)
        def _():
            own_list().start()

            @pl.loop(1, N)
            def _(p):
                list_copy(p, me).start()

            for copy in tails + others:
                copy.wait()
            for j in range(nt):
                high, low = split(d_buf[j])
                d_hi[j] = high
                d_lo[j] = low
            for u in range(nu):
                high, low = split(v_buf[u])
                v_hi[u] = high
                v_lo[u] = low

        @pl.when(i == 3)
        def _():
            own_list().wait()
            all_lists().wait_recv()
            pl.loop(0, N)(weigh)

            @pl.when(helped)
            def _():
                coef_copy().start()

        turn = C + extra - 2
        ready = jnp.where(e < turn, e - LAGS[0] + 1, e)

        @pl.when((e >= LAGS[1]) & (e - LAGS[1] < C + extra))
        def _():
            stage(e - LAGS[1], 1)

        @pl.loop(jnp.where(e <= turn, e - LAGS[0], e - 1), ready)
        def _(old):
            @pl.when((old >= 0) & (old < C + extra))
            def _():
                stage(old, 0)

        @pl.when((e >= 0) & (e < C + extra))
        def _():
            solve(e)

    @pl.when(helped)
    def _():
        @pl.loop(0, H)
        def _(e):
            at = strip_rows(C - H + e)
            k = (G - 1) * C - H + e

            @pl.when(helped_up)
            def _():
                up_copy(C - H + e, k).wait_recv()
                pan[at, :] = pan[at, :] - mail[k]

            @pl.when(helped_dn)
            def _():
                dn_copy(C - H + e, k).wait_recv()
                pan[at, :] = pan[at, :] - mail[top - k]

        all_ahead().wait_recv()

        @pl.loop(0, H)
        def _(e):
            at = strip_rows(C - H + e)
            upd[at, :] = upd[at, :] + ahead[e]

        coef_copy().wait_send()

    for g in range(G):
        @pl.when(z == g)
        def _():
            if g < G - 1:
                up_move(0, (G - 1 - g) * C, up_recv.at[0]).wait_send()
            if g > 0:
                dn_move(0, g * C, dn_recv.at[0]).wait_send()
            worked = C + (H if g in (0, G - 1) else 0)
            for s, first, count in ((0, half_n, half_n), (1, 1, half_n - 1)):
                if count:
                    sent = part.at[pl.ds(0, worked), pl.ds(first, count)]
                    pltpu.make_async_remote_copy(
                        src_ref=sent, dst_ref=sent, send_sem=x_send.at[s], recv_sem=x_recv.at[0, s],
                        device_id={"sub": dest_of(half_n)}, device_id_type=MESH,
                    ).wait_send()

    if H:
        @pl.when(helper)
        def _():
            all_ahead().wait_send()

    all_lists().wait_send()


def per_device(leaf_l, leaf_u, front, inv_diag, send_tiles, counts, trail_list, upper, trailing):
    G = lax.axis_size("grp")
    N = lax.axis_size("sub")
    strip, width = front.shape[1:]
    depth = leaf_u.shape[1]
    tile = upper.shape[1]
    rows = next(r for r in ROWS if strip % r == 0)
    C = strip // rows
    H = min(AHEAD, C) if G > 3 else 0
    block = 2 * rows if strip % (2 * rows) == 0 else strip
    nt, nu = width // tile, upper.shape[0]
    terms = -(-nt * nu // 8) * 8
    send_tiles = jnp.transpose(send_tiles, (0, 1, 3, 2))
    trail_list = jnp.transpose(trail_list, (0, 3, 1, 2))
    anywhere = pl.BlockSpec(memory_space=pl.ANY)
    vmem = pl.BlockSpec(memory_space=pltpu.VMEM)
    steps = N.bit_length() - 1
    dma = pltpu.SemaphoreType.DMA
    panel, updated = pl.pallas_call(
        functools.partial(kernel, G, N, C, H, rows, block),
        out_shape=(pltpu.VMEM(front.shape[1:], F32), pltpu.VMEM(trailing.shape[1:], F32)),
        in_specs=[anywhere] * 9,
        out_specs=(vmem, vmem),
        scratch_shapes=[
            pltpu.SMEM(send_tiles.shape, jnp.int32),
            pltpu.SMEM(counts.shape, jnp.int32),
            pltpu.VMEM(leaf_l.shape[1:], F32),
            pltpu.VMEM((2 * block, depth), BF16),
            pltpu.VMEM((depth, width), F32),
            pltpu.VMEM((depth, width), BF16),
            pltpu.VMEM((depth, width), BF16),
            pltpu.VMEM((G * strip, width), F32),
            pltpu.VMEM((strip, width), F32),
            pltpu.VMEM(inv_diag.shape[1:], F32),
            pltpu.VMEM(inv_diag.shape[1:], BF16),
            pltpu.VMEM(inv_diag.shape[1:], BF16),
            pltpu.VMEM(upper.shape, F32),
            pltpu.VMEM(upper.shape, BF16),
            pltpu.VMEM(upper.shape, BF16),
            pltpu.VMEM((strip, tile), F32),
            pltpu.VMEM(((G + 1) * C, rows, width), F32),
            pltpu.VMEM((N,) + trail_list.shape[1:], jnp.int32),
            pltpu.VMEM((2, N, terms, tile), F32),
            pltpu.VMEM((rows, width), F32),
            pltpu.VMEM((2 * nt * rows, tile), BF16),
            pltpu.VMEM((nu, nt * rows, tile), F32),
            pltpu.VMEM((C + H, N, rows, tile), F32),
            pltpu.VMEM((C + H, N, rows, tile), F32),
            pltpu.VMEM((max(H, 1), rows, tile), F32),
            dma((nt + 11,)),
            dma((2,)), dma(((G - 1) * C * rows // block,)), dma((C,)), dma((C,)),
            dma((2,)),
            dma((2,)), dma((RING, 2)),
            dma((2,)), dma((2,)),
        ],
        compiler_params=pltpu.CompilerParams(
            collective_id=0, has_side_effects=True, vmem_limit_bytes=60 << 20
        ),
    )(leaf_l, leaf_u, front, inv_diag, send_tiles, counts, trail_list, upper, trailing)
    return write_out(panel, updated)


def copy_kernel(cuts, panel, updated, panel_out, updated_out, sem):
    rows = panel.shape[0] // cuts
    copies = [pltpu.make_async_copy(updated, updated_out.at[0], sem.at[cuts])]
    for i in range(cuts):
        at = pl.ds(i * rows, rows)
        copies.append(pltpu.make_async_copy(panel.at[at], panel_out.at[0, at], sem.at[i]))
    for copy in copies:
        copy.start()
    for copy in copies:
        copy.wait()


def write_out(panel, updated):
    strip = panel.shape[0]
    cuts = next(n for n in (4, 2, 1) if strip % (8 * n) == 0)
    vmem = pl.BlockSpec(memory_space=pltpu.VMEM)
    anywhere = pl.BlockSpec(memory_space=pl.ANY)
    return pl.pallas_call(
        functools.partial(copy_kernel, cuts),
        out_shape=tuple(jax.ShapeDtypeStruct((1,) + x.shape, F32) for x in (panel, updated)),
        in_specs=[vmem, vmem],
        out_specs=(anywhere, anywhere),
        scratch_shapes=[pltpu.SemaphoreType.DMA((cuts + 1,))],
        compiler_params=pltpu.CompilerParams(vmem_limit_bytes=1 << 20),
    )(panel, updated)


def solution(mesh):
    placed = (
        P("sub", "grp", None),
        P("sub", "grp", None),
        P("sub", "grp", None),
        P("sub", None, None, None),
        P("sub", "grp", None, None),
        P("sub", "grp", None),
        P("sub", "grp", None, None),
        P(),
        P("sub", "grp", None),
    )
    return jax.shard_map(
        per_device,
        mesh=mesh,
        in_specs=placed,
        out_specs=(P("sub", "grp", None), P("sub", "grp", None)),
        check_vma=False,
    )
```

```python
import functools

import jax
import jax.numpy as jnp
from jax import lax
from jax.experimental import pallas as pl
from jax.experimental.pallas import tpu as pltpu
from jax.sharding import PartitionSpec as P

MESH = pl.DeviceIdType.MESH
F32 = jnp.float32
BF16 = jnp.bfloat16
ROWS = (32, 16, 8)
AHEAD = 2
LAGS = (2, 4)
RING = 6


def split(x):
    high = x.astype(BF16)
    return high, (x - high.astype(F32)).astype(BF16)


def dot(a, b):
    return jnp.dot(a, b, preferred_element_type=F32)


def dot3(stacked, high, low):
    m = stacked.shape[0] // 2
    both = dot(stacked, high)
    return both[:m] + both[m:] + dot(stacked[:m], low)


def kernel(
    G, N, C, H, rows, block,
    leaf_l, leaf_u, front, inv_diag, send_tiles, counts, trail_list, upper, trailing,
    pan, upd,
    tiles_buf, counts_buf, l_buf, l_two, u_buf, u_hi, u_lo, s_buf, f_buf, d_buf, d_hi, d_lo, v_buf, v_hi, v_lo, t_buf, mail,
    lists, coef, work, x_buf, prod, part, got, ahead,
    in_sem, send_sem, many_recv, up_recv, dn_recv, list_sem, x_send, x_recv, coef_sem, ahead_sem,
):
    z = lax.axis_index("grp")
    me = lax.axis_index("sub")
    width = front.shape[2]
    tile = upper.shape[1]
    depth = u_buf.shape[0]
    nt = width // tile
    nu = upper.shape[0]
    cap = send_tiles.shape[2]
    strip = C * rows
    per = block // rows
    group = min(4, N // 2)
    steps = N.bit_length() - 1
    half_n = N // 2
    step = next(n for n in (64, 32, 16) if depth % n == 0)
    top = (G + 1) * C - 1
    low_end, high_end = z == 0, z == G - 1
    helper = (H > 0) & (low_end | high_end)
    helped_up, helped_dn = (H > 0) & (z == 1), (H > 0) & (z == G - 2)
    helped = helped_up | helped_dn
    ally = jnp.where(low_end | (z == G - 2), z + 1, z - 1)
    extra = jnp.where(helper, H, 0)

    def bit(value, s):
        return lax.rem(lax.div(value, 1 << s), 2)

    shifts = [(1 << s) * (1 - 2 * bit(me, s)) for s in range(steps)]

    def dest_of(p):
        if isinstance(p, int):
            return me + sum(shifts[s] for s in range(steps) if p >> (steps - 1 - s) & 1)
        return me + sum(bit(p, steps - 1 - s) * shifts[s] for s in range(steps))

    def load_l(t, first, count, n):
        at = pl.ds(t * strip + first, count)
        return pltpu.make_async_copy(leaf_l.at[0, at], l_buf.at[at], in_sem.at[n])

    def load_u(n):
        cols = pl.ds(pl.multiple_of(n * tile, tile), tile)
        return pltpu.make_async_copy(leaf_u.at[0, :, cols], u_buf.at[:, cols], in_sem.at[n])

    heads = [load_l(G - 1, 0, block, nt), load_l(0, 0, block, nt + 1)]
    tails = [load_l(0, block, (G - 1) * strip - block, nt + 2)]
    if block < strip:
        tails.append(load_l(G - 1, block, strip - block, nt + 3))
    others = [
        pltpu.make_async_copy(front.at[0], f_buf, in_sem.at[nt + 4]),
        pltpu.make_async_copy(inv_diag.at[0], d_buf, in_sem.at[nt + 5]),
        pltpu.make_async_copy(trailing.at[0], t_buf, in_sem.at[nt + 6]),
        pltpu.make_async_copy(upper, v_buf, in_sem.at[nt + 7]),
        pltpu.make_async_copy(send_tiles, tiles_buf, in_sem.at[nt + 8]),
        pltpu.make_async_copy(counts, counts_buf, in_sem.at[nt + 9]),
    ]
    cuts = 3 if depth % 24 == 0 else 1
    for q in range(cuts):
        at = pl.ds(q * (depth // cuts), depth // cuts)
        pltpu.make_async_copy(leaf_u.at[0, at, :tile], u_buf.at[at, :tile], in_sem.at[0]).start()
    heads[0].start()
    heads[1].start()

    barrier = pltpu.get_barrier_semaphore()

    for p in reversed(range(1, N)):
        pl.semaphore_signal(barrier, inc=1, device_id={"sub": dest_of(p)}, device_id_type=MESH)

    @pl.when(z > 0)
    def _():
        pl.semaphore_signal(barrier, inc=1, device_id={"grp": z - 1}, device_id_type=MESH)

    @pl.when(z < G - 1)
    def _():
        pl.semaphore_signal(barrier, inc=1, device_id={"grp": z + 1}, device_id_type=MESH)

    pl.loop(1, nt)(lambda n: load_u(n).start())
    for copy in tails + others:
        copy.start()

    def own_list():
        return pltpu.make_async_copy(trail_list.at[0], lists.at[me], in_sem.at[nt + 10])

    def list_copy(p, owner):
        return pltpu.make_async_remote_copy(
            src_ref=trail_list.at[0], dst_ref=lists.at[owner],
            send_sem=list_sem.at[0], recv_sem=list_sem.at[1],
            device_id={"sub": dest_of(p)}, device_id_type=MESH,
        )

    def all_lists():
        return pltpu.make_async_remote_copy(
            src_ref=lists.at[pl.ds(0, N - 1)], dst_ref=lists.at[pl.ds(0, N - 1)],
            send_sem=list_sem.at[0], recv_sem=list_sem.at[1],
            device_id={"sub": dest_of(1)}, device_id_type=MESH,
        )

    def up_move(first, count, recv_sem, cols=slice(None)):
        at = pl.ds(first, count)
        return pltpu.make_async_remote_copy(
            src_ref=mail.at[at, :, cols], dst_ref=mail.at[at, :, cols],
            send_sem=send_sem.at[0], recv_sem=recv_sem,
            device_id={"grp": z + 1}, device_id_type=MESH,
        )

    def dn_move(first, count, recv_sem, cols=slice(None)):
        at = pl.ds(top + 1 - first - count, count)
        return pltpu.make_async_remote_copy(
            src_ref=mail.at[at, :, cols], dst_ref=mail.at[at, :, cols],
            send_sem=send_sem.at[1], recv_sem=recv_sem,
            device_id={"grp": z - 1}, device_id_type=MESH,
        )

    def up_copy(c, k):
        return up_move(k, 1, up_recv.at[c])

    def dn_copy(c, k):
        return dn_move(k, 1, dn_recv.at[c])

    def up_many(b, cols=slice(None)):
        return up_move(b * per, per, many_recv.at[b], cols)

    def dn_many(b, cols=slice(None)):
        return dn_move(b * per, per, many_recv.at[(G - 1) * C // per - 1 - b], cols)

    def coef_copy():
        return pltpu.make_async_remote_copy(
            src_ref=coef.at[0], dst_ref=coef.at[1],
            send_sem=coef_sem.at[0], recv_sem=coef_sem.at[1],
            device_id={"grp": ally}, device_id_type=MESH,
        )

    def ahead_copy(e):
        return pltpu.make_async_remote_copy(
            src_ref=ahead.at[e], dst_ref=ahead.at[e],
            send_sem=ahead_sem.at[0], recv_sem=ahead_sem.at[1],
            device_id={"grp": ally}, device_id_type=MESH,
        )

    def all_ahead():
        return pltpu.make_async_remote_copy(
            src_ref=ahead, dst_ref=ahead,
            send_sem=ahead_sem.at[0], recv_sem=ahead_sem.at[1],
            device_id={"grp": ally}, device_id_type=MESH,
        )

    def halve(row):
        at = pl.ds(pl.multiple_of(row, 8), block)
        high, low = split(l_buf[at, :])
        l_two[:block, :] = high
        l_two[block:, :] = low

    def product(row, n):
        at = pl.ds(pl.multiple_of(row, 8), block)
        cols = pl.ds(pl.multiple_of(n * tile, tile), tile)
        s_buf[at, cols] = dot3(l_two[...], u_hi[:, cols], u_lo[:, cols])

    def schur(row):
        halve(row)
        pl.loop(0, nt)(lambda n: product(row, n))

    def forward(slot, row, first):
        at = pl.ds(pl.multiple_of(row, 8), rows)

        @pl.when(first)
        def _():
            mail[slot] = s_buf[at, :]

        @pl.when(jnp.logical_not(first))
        def _():
            mail[slot] = mail[slot] + s_buf[at, :]

    def begin(n):
        cols = pl.ds(pl.multiple_of(n * tile, tile), tile)
        load_u(n).wait()

        @pl.loop(0, depth, step=step)
        def _(r):
            at = pl.ds(pl.multiple_of(r, step), step)
            high, low = split(u_buf[at, cols])
            u_hi[at, cols] = high
            u_lo[at, cols] = low

        @pl.when(low_end)
        def _():
            product((G - 1) * strip, n)

        @pl.when(high_end)
        def _():
            product(0, n)

    def begin_send(n):
        cols = pl.ds(pl.multiple_of(n * tile, tile), tile)

        @pl.when(low_end)
        def _():
            for k in range(per):
                mail[k, :, cols] = s_buf[(G - 1) * strip + k * rows : (G - 1) * strip + (k + 1) * rows, cols]
            up_many(0, cols).start()

        @pl.when(high_end)
        def _():
            for k in range(per):
                mail[top - k, :, cols] = s_buf[k * rows : (k + 1) * rows, cols]
            dn_many(0, cols).start()

    for head in heads:
        head.wait()

    @pl.when(low_end)
    def _():
        halve((G - 1) * strip)

    @pl.when(high_end)
    def _():
        halve(0)

    begin(0)
    pl.semaphore_wait(barrier, N - 1 + jnp.where(z > 0, 1, 0) + jnp.where(z < G - 1, 1, 0))
    begin_send(0)

    @pl.loop(1, nt)
    def _(n):
        begin(n)
        begin_send(n)

    def weigh(p):
        d = dest_of(p)

        source, slot, which = lists[d, 0], lists[d, 1], lists[d, 2]
        pick = jnp.zeros_like(source)
        for c in range(cap):
            pick = jnp.where(slot == c, tiles_buf[0, 0, c, d], pick)
        live = (source == me) & (slot < counts_buf[0, 0, d])
        code = jnp.where(live, pick * nu + which, -1)
        terms = lax.broadcasted_iota(jnp.int32, (coef.shape[2], code.shape[1]), 0)
        total = jnp.sum(jnp.where(code == terms, 1.0, 0.0).astype(F32), axis=1, keepdims=True)
        coef[0, p] = jnp.broadcast_to(total, coef.shape[2:])

    def exchange(e):
        return pltpu.make_async_remote_copy(
            src_ref=part.at[e, pl.ds(half_n, half_n)], dst_ref=got.at[e, pl.ds(half_n, half_n)],
            send_sem=x_send.at[0], recv_sem=x_recv.at[lax.rem(e, RING), 0],
            device_id={"sub": dest_of(half_n)}, device_id_type=MESH,
        )

    def scatter(e, p, count=1):
        return pltpu.make_async_remote_copy(
            src_ref=part.at[e, pl.ds(p, count)], dst_ref=got.at[e, pl.ds(p, count)],
            send_sem=x_send.at[1], recv_sem=x_recv.at[lax.rem(e, RING), 1],
            device_id={"sub": dest_of(p)}, device_id_type=MESH,
        )

    def chunk(e):
        c = jnp.where(helper, e - H, jnp.where(helped, jnp.where(e < H, C - H + e, e - H), e))
        return jnp.maximum(c, 0)

    def strip_rows(c):
        return pl.ds(pl.multiple_of(c * rows, 8), rows)

    def solve(e):
        helping = helper & (e < H)
        late = helped & (e < H)
        c = chunk(e)
        at = strip_rows(c)
        k_late = (G - 1) * C - H + e

        @pl.when(helping)
        def _():
            there = ally * strip + (C - H + e) * rows
            work[...] = s_buf[pl.ds(pl.multiple_of(there, 8), rows), :]

        @pl.when(jnp.logical_not(helping))
        def _():
            work[...] = f_buf[at, :] - s_buf[pl.ds(pl.multiple_of(z * strip + c * rows, 8), rows), :]

            @pl.when((z > 0) & jnp.logical_not(late & helped_up))
            def _():
                k = (G - 1 - z) * C + c
                up_copy(c, k).wait_recv()
                work[...] = work[...] - mail[k]

            @pl.when((z < G - 1) & jnp.logical_not(late & helped_dn))
            def _():
                k = z * C + c
                dn_copy(c, k).wait_recv()
                work[...] = work[...] - mail[top - k]

        half = nt * rows
        for j in range(nt):
            cols = slice(j * tile, (j + 1) * tile)
            high, low = split(work[:, cols])
            solved = dot3(jnp.concatenate([high, low], axis=0), d_hi[j], d_lo[j])
            work[:, cols] = solved
            high, low = split(solved)
            x_buf[j * rows : (j + 1) * rows, :] = high
            x_buf[half + j * rows : half + (j + 1) * rows, :] = low

        @pl.when(jnp.logical_not(helping))
        def _():
            pan[at, :] = work[...]

        @pl.when(helping & low_end)
        def _():
            mail[k_late] = work[...]
            up_copy(C - H + e, k_late).start()

        @pl.when(helping & high_end)
        def _():
            mail[top - k_late] = work[...]
            dn_copy(C - H + e, k_late).start()

        for u in range(nu):
            prod[u] = dot3(x_buf[...], v_hi[u], v_lo[u])

        @pl.when(helping & (e == 0))
        def _():
            coef_copy().wait_recv()

        table = jnp.where(helping, 1, 0)

        def mix(g):
            p0 = g * group

            @pl.loop(0, rows, step=8)
            def _(r):
                r = pl.multiple_of(r, 8)
                sums = [None] * group
                for j in range(nt):
                    for u in range(nu):
                        value = prod[u, pl.ds(j * rows + r, 8), :]
                        for q in range(group):
                            n = j * nu + u
                            term = coef[table, p0 + q, n : n + 1, :] * value
                            sums[q] = term if sums[q] is None else sums[q] + term
                for q in range(group):
                    part[e, p0 + q, pl.ds(r, 8), :] = sums[q]

        groups = N // group
        pl.loop(groups // 2, groups)(mix)
        exchange(e).start()
        pl.loop(0, groups // 2)(mix)

    def stage(e, s):
        if s == 0:
            exchange(e).wait_recv()
            if half_n > 1:
                part[e, 1:half_n] = part[e, 1:half_n] + got[e, half_n + 1 :]
                for p in reversed(range(1, half_n)):
                    scatter(e, p).start()
            part[e, 0] = part[e, 0] + got[e, half_n]
        else:
            total = part[e, 0]
            if half_n > 1:
                scatter(e, 1, half_n - 1).wait_recv()
                for p in range(1, half_n):
                    total = total + got[e, p]
            helping = helper & (e < H)

            @pl.when(helping)
            def _():
                ahead[e] = total
                ahead_copy(e).start()

            @pl.when(jnp.logical_not(helping))
            def _():
                at = strip_rows(chunk(e))
                upd[at, :] = t_buf[at, :] - total

    lag_up, lag_dn = z * per, (G - 1 - z) * per
    base = jnp.maximum((G - 1 - z) * C + lag_up, z * C + lag_dn)
    last = max(max((G - 1 - i) * C + i * per, i * C + (G - 1 - i) * per) for i in range(G))

    @pl.loop(0, last + C + LAGS[1])
    def _(i):
        up, down, own = i - lag_up, i - lag_dn, i - base
        e = own + extra
        has_up = (up >= jnp.where(low_end, per, 0)) & (up < (G - 1 - z) * C)
        has_dn = (down >= jnp.where(high_end, per, 0)) & (down < z * C)
        plain = (G - 1) * C - extra
        up_row = (G - 1) * strip + lax.rem(jnp.maximum(up, 0), C) * rows - lax.div(jnp.maximum(up, 0), C) * strip

        @pl.loop(0, 3)
        def _(job):
            k = jnp.where(job == 0, up, jnp.where(job == 1, down, own + C))
            has = ((job == 0) & has_up) | ((job == 1) & has_dn) | ((job == 2) & (k >= 0) & (k < C))
            row = jnp.where(job == 0, up_row, jnp.where(job == 1, down * rows, z * strip + k * rows))

            @pl.when(has & (lax.rem(jnp.maximum(k, 0), per) == 0))
            def _():
                schur(row)

        @pl.when(has_up & (up < plain))
        def _():
            place = lax.rem(up, per)
            final = (G - 2 - z) * C

            @pl.when((z > 0) & (place == 0))
            def _():
                up_many(lax.div(up, per)).wait_recv()

            forward(up, up_row, z == 0)

            @pl.when((up < final) & (place == per - 1))
            def _():
                up_many(lax.div(up, per)).start()

            @pl.when(up >= final)
            def _():
                up_copy(up - final, up).start()

        @pl.when(has_dn & (down < plain))
        def _():
            place = lax.rem(down, per)
            final = (z - 1) * C

            @pl.when((z < G - 1) & (place == 0))
            def _():
                dn_many(lax.div(down, per)).wait_recv()

            forward(top - down, down * rows, z == G - 1)

            @pl.when((down < final) & (place == per - 1))
            def _():
                dn_many(lax.div(down, per)).start()

            @pl.when(down >= final)
            def _():
                dn_copy(down - final, down).start()

        @pl.when(i == 1)
        def _():
            own_list().start()

            @pl.loop(1, N)
            def _(p):
                list_copy(p, me).start()

            for copy in tails + others:
                copy.wait()
            for j in range(nt):
                high, low = split(d_buf[j])
                d_hi[j] = high
                d_lo[j] = low
            for u in range(nu):
                high, low = split(v_buf[u])
                v_hi[u] = high
                v_lo[u] = low

        @pl.when(i == 3)
        def _():
            own_list().wait()
            all_lists().wait_recv()
            pl.loop(0, N)(weigh)

            @pl.when(helped)
            def _():
                coef_copy().start()

        turn = C + extra - 2
        ready = jnp.where(e < turn, e - LAGS[0] + 1, e)

        @pl.when((e >= LAGS[1]) & (e - LAGS[1] < C + extra))
        def _():
            stage(e - LAGS[1], 1)

        @pl.loop(jnp.where(e <= turn, e - LAGS[0], e - 1), ready)
        def _(old):
            @pl.when((old >= 0) & (old < C + extra))
            def _():
                stage(old, 0)

        @pl.when((e >= 0) & (e < C + extra))
        def _():
            solve(e)

    @pl.when(helped)
    def _():
        @pl.loop(0, H)
        def _(e):
            at = strip_rows(C - H + e)
            k = (G - 1) * C - H + e

            @pl.when(helped_up)
            def _():
                up_copy(C - H + e, k).wait_recv()
                pan[at, :] = pan[at, :] - mail[k]

            @pl.when(helped_dn)
            def _():
                dn_copy(C - H + e, k).wait_recv()
                pan[at, :] = pan[at, :] - mail[top - k]

        all_ahead().wait_recv()

        @pl.loop(0, H)
        def _(e):
            at = strip_rows(C - H + e)
            upd[at, :] = upd[at, :] + ahead[e]

        coef_copy().wait_send()

    for g in range(G):
        @pl.when(z == g)
        def _():
            if g < G - 1:
                up_move(0, (G - 1 - g) * C, up_recv.at[0]).wait_send()
            if g > 0:
                dn_move(0, g * C, dn_recv.at[0]).wait_send()
            worked = C + (H if g in (0, G - 1) else 0)
            for s, first, count in ((0, half_n, half_n), (1, 1, half_n - 1)):
                if count:
                    sent = part.at[pl.ds(0, worked), pl.ds(first, count)]
                    pltpu.make_async_remote_copy(
                        src_ref=sent, dst_ref=sent, send_sem=x_send.at[s], recv_sem=x_recv.at[0, s],
                        device_id={"sub": dest_of(half_n)}, device_id_type=MESH,
                    ).wait_send()

    if H:
        @pl.when(helper)
        def _():
            all_ahead().wait_send()

    all_lists().wait_send()


def per_device(leaf_l, leaf_u, front, inv_diag, send_tiles, counts, trail_list, upper, trailing):
    G = lax.axis_size("grp")
    N = lax.axis_size("sub")
    strip, width = front.shape[1:]
    depth = leaf_u.shape[1]
    tile = upper.shape[1]
    rows = next(r for r in ROWS if strip % r == 0)
    C = strip // rows
    H = min(AHEAD, C) if G > 3 else 0
    block = 2 * rows if strip % (2 * rows) == 0 else strip
    nt, nu = width // tile, upper.shape[0]
    terms = -(-nt * nu // 8) * 8
    send_tiles = jnp.transpose(send_tiles, (0, 1, 3, 2))
    trail_list = jnp.transpose(trail_list, (0, 3, 1, 2))
    anywhere = pl.BlockSpec(memory_space=pl.ANY)
    vmem = pl.BlockSpec(memory_space=pltpu.VMEM)
    steps = N.bit_length() - 1
    dma = pltpu.SemaphoreType.DMA
    panel, updated = pl.pallas_call(
        functools.partial(kernel, G, N, C, H, rows, block),
        out_shape=(pltpu.VMEM(front.shape[1:], F32), pltpu.VMEM(trailing.shape[1:], F32)),
        in_specs=[anywhere] * 9,
        out_specs=(vmem, vmem),
        scratch_shapes=[
            pltpu.SMEM(send_tiles.shape, jnp.int32),
            pltpu.SMEM(counts.shape, jnp.int32),
            pltpu.VMEM(leaf_l.shape[1:], F32),
            pltpu.VMEM((2 * block, depth), BF16),
            pltpu.VMEM((depth, width), F32),
            pltpu.VMEM((depth, width), BF16),
            pltpu.VMEM((depth, width), BF16),
            pltpu.VMEM((G * strip, width), F32),
            pltpu.VMEM((strip, width), F32),
            pltpu.VMEM(inv_diag.shape[1:], F32),
            pltpu.VMEM(inv_diag.shape[1:], BF16),
            pltpu.VMEM(inv_diag.shape[1:], BF16),
            pltpu.VMEM(upper.shape, F32),
            pltpu.VMEM(upper.shape, BF16),
            pltpu.VMEM(upper.shape, BF16),
            pltpu.VMEM((strip, tile), F32),
            pltpu.VMEM(((G + 1) * C, rows, width), F32),
            pltpu.VMEM((N,) + trail_list.shape[1:], jnp.int32),
            pltpu.VMEM((2, N, terms, tile), F32),
            pltpu.VMEM((rows, width), F32),
            pltpu.VMEM((2 * nt * rows, tile), BF16),
            pltpu.VMEM((nu, nt * rows, tile), F32),
            pltpu.VMEM((C + H, N, rows, tile), F32),
            pltpu.VMEM((C + H, N, rows, tile), F32),
            pltpu.VMEM((max(H, 1), rows, tile), F32),
            dma((nt + 11,)),
            dma((2,)), dma(((G - 1) * C * rows // block,)), dma((C,)), dma((C,)),
            dma((2,)),
            dma((2,)), dma((RING, 2)),
            dma((2,)), dma((2,)),
        ],
        compiler_params=pltpu.CompilerParams(
            collective_id=0, has_side_effects=True, vmem_limit_bytes=60 << 20
        ),
    )(leaf_l, leaf_u, front, inv_diag, send_tiles, counts, trail_list, upper, trailing)
    return write_out(panel, updated)


def copy_kernel(cuts, panel, updated, panel_out, updated_out, sem):
    rows = panel.shape[0] // cuts
    copies = [pltpu.make_async_copy(updated, updated_out.at[0], sem.at[cuts])]
    for i in range(cuts):
        at = pl.ds(i * rows, rows)
        copies.append(pltpu.make_async_copy(panel.at[at], panel_out.at[0, at], sem.at[i]))
    for copy in copies:
        copy.start()
    for copy in copies:
        copy.wait()


def write_out(panel, updated):
    strip = panel.shape[0]
    cuts = next(n for n in (4, 2, 1) if strip % (8 * n) == 0)
    vmem = pl.BlockSpec(memory_space=pltpu.VMEM)
    anywhere = pl.BlockSpec(memory_space=pl.ANY)
    return pl.pallas_call(
        functools.partial(copy_kernel, cuts),
        out_shape=tuple(jax.ShapeDtypeStruct((1,) + x.shape, F32) for x in (panel, updated)),
        in_specs=[vmem, vmem],
        out_specs=(anywhere, anywhere),
        scratch_shapes=[pltpu.SemaphoreType.DMA((cuts + 1,))],
        compiler_params=pltpu.CompilerParams(vmem_limit_bytes=1 << 20),
    )(panel, updated)


def solution(mesh):
    placed = (
        P("sub", "grp", None),
        P("sub", "grp", None),
        P("sub", "grp", None),
        P("sub", None, None, None),
        P("sub", "grp", None, None),
        P("sub", "grp", None),
        P("sub", "grp", None, None),
        P(),
        P("sub", "grp", None),
    )
    return jax.shard_map(
        per_device,
        mesh=mesh,
        in_specs=placed,
        out_specs=(P("sub", "grp", None), P("sub", "grp", None)),
        check_vma=False,
    )
```

```python
import functools

import jax
import jax.numpy as jnp
from jax import lax
from jax.experimental import pallas as pl
from jax.experimental.pallas import tpu as pltpu
from jax.sharding import PartitionSpec as P

MESH = pl.DeviceIdType.MESH
F32 = jnp.float32
BF16 = jnp.bfloat16
ROWS = (32, 16, 8)
AHEAD = 2
LAGS = (2, 4)
RING = 6


def split(x):
    high = x.astype(BF16)
    return high, (x - high.astype(F32)).astype(BF16)


def dot(a, b):
    return jnp.dot(a, b, preferred_element_type=F32)


def dot3(stacked, high, low):
    m = stacked.shape[0] // 2
    both = dot(stacked, high)
    return both[:m] + both[m:] + dot(stacked[:m], low)


def kernel(
    G, N, C, H, rows, block,
    leaf_l, leaf_u, front, inv_diag, send_tiles, counts, trail_list, upper, trailing,
    pan, upd,
    tiles_buf, counts_buf, l_buf, l_two, u_buf, u_hi, u_lo, s_buf, f_buf, d_buf, d_hi, d_lo, v_buf, v_hi, v_lo, t_buf, mail,
    lists, coef, work, x_buf, prod, part, got, ahead,
    in_sem, send_sem, many_recv, up_recv, dn_recv, list_sem, x_send, x_recv, coef_sem, ahead_sem, relay,
):
    z = lax.axis_index("grp")
    me = lax.axis_index("sub")
    width = front.shape[2]
    tile = upper.shape[1]
    depth = u_buf.shape[0]
    nt = width // tile
    nu = upper.shape[0]
    cap = send_tiles.shape[2]
    strip = C * rows
    per = block // rows
    group = min(4, N // 2)
    steps = N.bit_length() - 1
    half_n = N // 2
    step = next(n for n in (64, 32, 16) if depth % n == 0)
    top = (G + 1) * C - 1
    low_end, high_end = z == 0, z == G - 1
    helper = (H > 0) & (low_end | high_end)
    helped_up, helped_dn = (H > 0) & (z == 1), (H > 0) & (z == G - 2)
    helped = helped_up | helped_dn
    ally = jnp.where(low_end | (z == G - 2), z + 1, z - 1)
    extra = jnp.where(helper, H, 0)

    def bit(value, s):
        return lax.rem(lax.div(value, 1 << s), 2)

    shifts = [(1 << s) * (1 - 2 * bit(me, s)) for s in range(steps)]

    def dest_of(p):
        if isinstance(p, int):
            return me + sum(shifts[s] for s in range(steps) if p >> (steps - 1 - s) & 1)
        return me + sum(bit(p, steps - 1 - s) * shifts[s] for s in range(steps))

    def load_l(t, first, count, n):
        at = pl.ds(t * strip + first, count)
        return pltpu.make_async_copy(leaf_l.at[0, at], l_buf.at[at], in_sem.at[n])

    def load_u(n):
        cols = pl.ds(pl.multiple_of(n * tile, tile), tile)
        return pltpu.make_async_copy(leaf_u.at[0, :, cols], u_buf.at[:, cols], in_sem.at[n])

    heads = [load_l(G - 1, 0, block, nt), load_l(0, 0, block, nt + 1)]
    tails = [load_l(0, block, (G - 1) * strip - block, nt + 2)]
    if block < strip:
        tails.append(load_l(G - 1, block, strip - block, nt + 3))
    others = [
        pltpu.make_async_copy(front.at[0], f_buf, in_sem.at[nt + 4]),
        pltpu.make_async_copy(inv_diag.at[0], d_buf, in_sem.at[nt + 5]),
        pltpu.make_async_copy(trailing.at[0], t_buf, in_sem.at[nt + 6]),
        pltpu.make_async_copy(upper, v_buf, in_sem.at[nt + 7]),
        pltpu.make_async_copy(send_tiles, tiles_buf, in_sem.at[nt + 8]),
        pltpu.make_async_copy(counts, counts_buf, in_sem.at[nt + 9]),
    ]
    cuts = 3 if depth % 24 == 0 else 1
    for q in range(cuts):
        at = pl.ds(q * (depth // cuts), depth // cuts)
        pltpu.make_async_copy(leaf_u.at[0, at, :tile], u_buf.at[at, :tile], in_sem.at[0]).start()
    heads[0].start()
    heads[1].start()

    barrier = pltpu.get_barrier_semaphore()

    relayed = H > 0
    plane = jnp.logical_not(low_end | high_end) if relayed else z >= 0

    @pl.when(z > 0)
    def _():
        pl.semaphore_signal(barrier, inc=1, device_id={"grp": z - 1}, device_id_type=MESH)

    @pl.when(z < G - 1)
    def _():
        pl.semaphore_signal(barrier, inc=1, device_id={"grp": z + 1}, device_id_type=MESH)

    @pl.when(plane)
    def _():
        for p in reversed(range(1, N)):
            pl.semaphore_signal(barrier, inc=1, device_id={"sub": dest_of(p)}, device_id_type=MESH)

    pl.loop(1, nt)(lambda n: load_u(n).start())
    for copy in tails + others:
        copy.start()

    def own_list():
        return pltpu.make_async_copy(trail_list.at[0], lists.at[me], in_sem.at[nt + 10])

    def list_copy(p, owner):
        return pltpu.make_async_remote_copy(
            src_ref=trail_list.at[0], dst_ref=lists.at[owner],
            send_sem=list_sem.at[0], recv_sem=list_sem.at[1],
            device_id={"sub": dest_of(p)}, device_id_type=MESH,
        )

    def all_lists():
        return pltpu.make_async_remote_copy(
            src_ref=lists.at[pl.ds(0, N - 1)], dst_ref=lists.at[pl.ds(0, N - 1)],
            send_sem=list_sem.at[0], recv_sem=list_sem.at[1],
            device_id={"sub": dest_of(1)}, device_id_type=MESH,
        )

    def up_move(first, count, recv_sem, cols=slice(None)):
        at = pl.ds(first, count)
        return pltpu.make_async_remote_copy(
            src_ref=mail.at[at, :, cols], dst_ref=mail.at[at, :, cols],
            send_sem=send_sem.at[0], recv_sem=recv_sem,
            device_id={"grp": z + 1}, device_id_type=MESH,
        )

    def dn_move(first, count, recv_sem, cols=slice(None)):
        at = pl.ds(top + 1 - first - count, count)
        return pltpu.make_async_remote_copy(
            src_ref=mail.at[at, :, cols], dst_ref=mail.at[at, :, cols],
            send_sem=send_sem.at[1], recv_sem=recv_sem,
            device_id={"grp": z - 1}, device_id_type=MESH,
        )

    def up_copy(c, k):
        return up_move(k, 1, up_recv.at[c])

    def dn_copy(c, k):
        return dn_move(k, 1, dn_recv.at[c])

    def up_many(b, cols=slice(None)):
        return up_move(b * per, per, many_recv.at[b], cols)

    def dn_many(b, cols=slice(None)):
        return dn_move(b * per, per, many_recv.at[(G - 1) * C // per - 1 - b], cols)

    def coef_copy():
        return pltpu.make_async_remote_copy(
            src_ref=coef.at[0], dst_ref=coef.at[1],
            send_sem=coef_sem.at[0], recv_sem=coef_sem.at[1],
            device_id={"grp": ally}, device_id_type=MESH,
        )

    def ahead_copy(e):
        return pltpu.make_async_remote_copy(
            src_ref=ahead.at[e], dst_ref=ahead.at[e],
            send_sem=ahead_sem.at[0], recv_sem=ahead_sem.at[1],
            device_id={"grp": ally}, device_id_type=MESH,
        )

    def all_ahead():
        return pltpu.make_async_remote_copy(
            src_ref=ahead, dst_ref=ahead,
            send_sem=ahead_sem.at[0], recv_sem=ahead_sem.at[1],
            device_id={"grp": ally}, device_id_type=MESH,
        )

    def halve(row):
        at = pl.ds(pl.multiple_of(row, 8), block)
        high, low = split(l_buf[at, :])
        l_two[:block, :] = high
        l_two[block:, :] = low

    def product(row, n):
        at = pl.ds(pl.multiple_of(row, 8), block)
        cols = pl.ds(pl.multiple_of(n * tile, tile), tile)
        s_buf[at, cols] = dot3(l_two[...], u_hi[:, cols], u_lo[:, cols])

    def schur(row):
        halve(row)
        pl.loop(0, nt)(lambda n: product(row, n))

    def forward(slot, row, first):
        at = pl.ds(pl.multiple_of(row, 8), rows)

        @pl.when(first)
        def _():
            mail[slot] = s_buf[at, :]

        @pl.when(jnp.logical_not(first))
        def _():
            mail[slot] = mail[slot] + s_buf[at, :]

    def begin(n):
        cols = pl.ds(pl.multiple_of(n * tile, tile), tile)
        load_u(n).wait()

        @pl.loop(0, depth, step=step)
        def _(r):
            at = pl.ds(pl.multiple_of(r, step), step)
            high, low = split(u_buf[at, cols])
            u_hi[at, cols] = high
            u_lo[at, cols] = low

        @pl.when(low_end)
        def _():
            product((G - 1) * strip, n)

        @pl.when(high_end)
        def _():
            product(0, n)

    def begin_send(n):
        cols = pl.ds(pl.multiple_of(n * tile, tile), tile)

        @pl.when(low_end)
        def _():
            for k in range(per):
                mail[k, :, cols] = s_buf[(G - 1) * strip + k * rows : (G - 1) * strip + (k + 1) * rows, cols]
            up_many(0, cols).start()

        @pl.when(high_end)
        def _():
            for k in range(per):
                mail[top - k, :, cols] = s_buf[k * rows : (k + 1) * rows, cols]
            dn_many(0, cols).start()

    for head in heads:
        head.wait()

    @pl.when(low_end)
    def _():
        halve((G - 1) * strip)

    @pl.when(high_end)
    def _():
        halve(0)

    begin(0)
    pl.semaphore_wait(barrier, jnp.where(plane, N - 1, 0) + jnp.where(z > 0, 1, 0) + jnp.where(z < G - 1, 1, 0))
    begin_send(0)

    @pl.when(helped)
    def _():
        for p in reversed(range(1, N)):
            pl.semaphore_signal(relay.at[0], inc=1, device_id={"sub": dest_of(p)}, device_id_type=MESH)

    @pl.loop(1, nt)
    def _(n):
        begin(n)
        begin_send(n)

    @pl.when(helped)
    def _():
        pl.semaphore_wait(relay.at[0], N - 1)
        pl.semaphore_signal(relay.at[1], inc=1, device_id={"grp": ally}, device_id_type=MESH)

    def weigh(p):
        d = dest_of(p)

        source, slot, which = lists[d, 0], lists[d, 1], lists[d, 2]
        pick = jnp.zeros_like(source)
        for c in range(cap):
            pick = jnp.where(slot == c, tiles_buf[0, 0, c, d], pick)
        live = (source == me) & (slot < counts_buf[0, 0, d])
        code = jnp.where(live, pick * nu + which, -1)
        terms = lax.broadcasted_iota(jnp.int32, (coef.shape[2], code.shape[1]), 0)
        total = jnp.sum(jnp.where(code == terms, 1.0, 0.0).astype(F32), axis=1, keepdims=True)
        coef[0, p] = jnp.broadcast_to(total, coef.shape[2:])

    def exchange(e):
        return pltpu.make_async_remote_copy(
            src_ref=part.at[e, pl.ds(half_n, half_n)], dst_ref=got.at[e, pl.ds(half_n, half_n)],
            send_sem=x_send.at[0], recv_sem=x_recv.at[lax.rem(e, RING), 0],
            device_id={"sub": dest_of(half_n)}, device_id_type=MESH,
        )

    def scatter(e, p, count=1):
        return pltpu.make_async_remote_copy(
            src_ref=part.at[e, pl.ds(p, count)], dst_ref=got.at[e, pl.ds(p, count)],
            send_sem=x_send.at[1], recv_sem=x_recv.at[lax.rem(e, RING), 1],
            device_id={"sub": dest_of(p)}, device_id_type=MESH,
        )

    def chunk(e):
        c = jnp.where(helper, e - H, jnp.where(helped, jnp.where(e < H, C - H + e, e - H), e))
        return jnp.maximum(c, 0)

    def strip_rows(c):
        return pl.ds(pl.multiple_of(c * rows, 8), rows)

    def solve(e):
        helping = helper & (e < H)
        late = helped & (e < H)
        c = chunk(e)
        at = strip_rows(c)
        k_late = (G - 1) * C - H + e

        @pl.when(helping)
        def _():
            there = ally * strip + (C - H + e) * rows
            work[...] = s_buf[pl.ds(pl.multiple_of(there, 8), rows), :]

        @pl.when(jnp.logical_not(helping))
        def _():
            work[...] = f_buf[at, :] - s_buf[pl.ds(pl.multiple_of(z * strip + c * rows, 8), rows), :]

            @pl.when((z > 0) & jnp.logical_not(late & helped_up))
            def _():
                k = (G - 1 - z) * C + c
                up_copy(c, k).wait_recv()
                work[...] = work[...] - mail[k]

            @pl.when((z < G - 1) & jnp.logical_not(late & helped_dn))
            def _():
                k = z * C + c
                dn_copy(c, k).wait_recv()
                work[...] = work[...] - mail[top - k]

        half = nt * rows
        for j in range(nt):
            cols = slice(j * tile, (j + 1) * tile)
            high, low = split(work[:, cols])
            solved = dot3(jnp.concatenate([high, low], axis=0), d_hi[j], d_lo[j])
            work[:, cols] = solved
            high, low = split(solved)
            x_buf[j * rows : (j + 1) * rows, :] = high
            x_buf[half + j * rows : half + (j + 1) * rows, :] = low

        @pl.when(jnp.logical_not(helping))
        def _():
            pan[at, :] = work[...]

        @pl.when(helping & low_end)
        def _():
            mail[k_late] = work[...]
            up_copy(C - H + e, k_late).start()

        @pl.when(helping & high_end)
        def _():
            mail[top - k_late] = work[...]
            dn_copy(C - H + e, k_late).start()

        for u in range(nu):
            prod[u] = dot3(x_buf[...], v_hi[u], v_lo[u])

        @pl.when(helping & (e == 0))
        def _():
            coef_copy().wait_recv()

        table = jnp.where(helping, 1, 0)

        def mix(g):
            p0 = g * group

            @pl.loop(0, rows, step=8)
            def _(r):
                r = pl.multiple_of(r, 8)
                sums = [None] * group
                for j in range(nt):
                    for u in range(nu):
                        value = prod[u, pl.ds(j * rows + r, 8), :]
                        for q in range(group):
                            n = j * nu + u
                            term = coef[table, p0 + q, n : n + 1, :] * value
                            sums[q] = term if sums[q] is None else sums[q] + term
                for q in range(group):
                    part[e, p0 + q, pl.ds(r, 8), :] = sums[q]

        groups = N // group
        pl.loop(groups // 2, groups)(mix)
        exchange(e).start()
        pl.loop(0, groups // 2)(mix)

    def stage(e, s):
        if s == 0:
            exchange(e).wait_recv()
            if half_n > 1:
                part[e, 1:half_n] = part[e, 1:half_n] + got[e, half_n + 1 :]
                for p in reversed(range(1, half_n)):
                    scatter(e, p).start()
            part[e, 0] = part[e, 0] + got[e, half_n]
        else:
            total = part[e, 0]
            if half_n > 1:
                scatter(e, 1, half_n - 1).wait_recv()
                for p in range(1, half_n):
                    total = total + got[e, p]
            helping = helper & (e < H)

            @pl.when(helping)
            def _():
                ahead[e] = total
                ahead_copy(e).start()

            @pl.when(jnp.logical_not(helping))
            def _():
                at = strip_rows(chunk(e))
                upd[at, :] = t_buf[at, :] - total

    lag_up, lag_dn = z * per, (G - 1 - z) * per
    base = jnp.maximum((G - 1 - z) * C + lag_up, z * C + lag_dn)

    @pl.loop(0, base + C + LAGS[1])
    def _(i):
        up, down, own = i - lag_up, i - lag_dn, i - base
        e = own + extra
        has_up = (up >= jnp.where(low_end, per, 0)) & (up < (G - 1 - z) * C)
        has_dn = (down >= jnp.where(high_end, per, 0)) & (down < z * C)
        plain = (G - 1) * C - extra
        up_row = (G - 1) * strip + lax.rem(jnp.maximum(up, 0), C) * rows - lax.div(jnp.maximum(up, 0), C) * strip

        @pl.loop(0, 3)
        def _(job):
            k = jnp.where(job == 0, up, jnp.where(job == 1, down, own + C))
            has = ((job == 0) & has_up) | ((job == 1) & has_dn) | ((job == 2) & (k >= 0) & (k < C))
            row = jnp.where(job == 0, up_row, jnp.where(job == 1, down * rows, z * strip + k * rows))

            @pl.when(has & (lax.rem(jnp.maximum(k, 0), per) == 0))
            def _():
                schur(row)

        @pl.when(has_up & (up < plain))
        def _():
            place = lax.rem(up, per)
            final = (G - 2 - z) * C

            @pl.when((z > 0) & (place == 0))
            def _():
                up_many(lax.div(up, per)).wait_recv()

            forward(up, up_row, z == 0)

            @pl.when((up < final) & (place == per - 1))
            def _():
                up_many(lax.div(up, per)).start()

            @pl.when(up >= final)
            def _():
                up_copy(up - final, up).start()

        @pl.when(has_dn & (down < plain))
        def _():
            place = lax.rem(down, per)
            final = (z - 1) * C

            @pl.when((z < G - 1) & (place == 0))
            def _():
                dn_many(lax.div(down, per)).wait_recv()

            forward(top - down, down * rows, z == G - 1)

            @pl.when((down < final) & (place == per - 1))
            def _():
                dn_many(lax.div(down, per)).start()

            @pl.when(down >= final)
            def _():
                dn_copy(down - final, down).start()

        @pl.when(i == 1)
        def _():
            own_list().start()
            for copy in tails + others:
                copy.wait()

            @pl.when(helper)
            def _():
                pl.semaphore_wait(relay.at[1], 1)

            @pl.loop(1, N)
            def _(p):
                list_copy(p, me).start()

            for j in range(nt):
                high, low = split(d_buf[j])
                d_hi[j] = high
                d_lo[j] = low
            for u in range(nu):
                high, low = split(v_buf[u])
                v_hi[u] = high
                v_lo[u] = low

        @pl.when(i == 3)
        def _():
            own_list().wait()
            all_lists().wait_recv()
            pl.loop(0, N)(weigh)

            @pl.when(helped)
            def _():
                coef_copy().start()

        turn = C + extra - 2
        ready = jnp.where(e < turn, e - LAGS[0] + 1, e)

        @pl.when((e >= LAGS[1]) & (e - LAGS[1] < C + extra))
        def _():
            stage(e - LAGS[1], 1)

        @pl.loop(jnp.where(e <= turn, e - LAGS[0], e - 1), ready)
        def _(old):
            @pl.when((old >= 0) & (old < C + extra))
            def _():
                stage(old, 0)

        @pl.when((e >= 0) & (e < C + extra))
        def _():
            solve(e)

    @pl.when(helped)
    def _():
        @pl.loop(0, H)
        def _(e):
            at = strip_rows(C - H + e)
            k = (G - 1) * C - H + e

            @pl.when(helped_up)
            def _():
                up_copy(C - H + e, k).wait_recv()
                pan[at, :] = pan[at, :] - mail[k]

            @pl.when(helped_dn)
            def _():
                dn_copy(C - H + e, k).wait_recv()
                pan[at, :] = pan[at, :] - mail[top - k]

        all_ahead().wait_recv()

        @pl.loop(0, H)
        def _(e):
            at = strip_rows(C - H + e)
            upd[at, :] = upd[at, :] + ahead[e]

        coef_copy().wait_send()

    for g in range(G):
        @pl.when(z == g)
        def _():
            if g < G - 1:
                up_move(0, (G - 1 - g) * C, up_recv.at[0]).wait_send()
            if g > 0:
                dn_move(0, g * C, dn_recv.at[0]).wait_send()
            worked = C + (H if g in (0, G - 1) else 0)
            for s, first, count in ((0, half_n, half_n), (1, 1, half_n - 1)):
                if count:
                    sent = part.at[pl.ds(0, worked), pl.ds(first, count)]
                    pltpu.make_async_remote_copy(
                        src_ref=sent, dst_ref=sent, send_sem=x_send.at[s], recv_sem=x_recv.at[0, s],
                        device_id={"sub": dest_of(half_n)}, device_id_type=MESH,
                    ).wait_send()

    if H:
        @pl.when(helper)
        def _():
            all_ahead().wait_send()

    all_lists().wait_send()


def per_device(leaf_l, leaf_u, front, inv_diag, send_tiles, counts, trail_list, upper, trailing):
    G = lax.axis_size("grp")
    N = lax.axis_size("sub")
    strip, width = front.shape[1:]
    depth = leaf_u.shape[1]
    tile = upper.shape[1]
    rows = next(r for r in ROWS if strip % r == 0)
    C = strip // rows
    H = min(AHEAD, C) if G > 3 else 0
    block = 2 * rows if strip % (2 * rows) == 0 else strip
    nt, nu = width // tile, upper.shape[0]
    terms = -(-nt * nu // 8) * 8
    send_tiles = jnp.transpose(send_tiles, (0, 1, 3, 2))
    trail_list = jnp.transpose(trail_list, (0, 3, 1, 2))
    anywhere = pl.BlockSpec(memory_space=pl.ANY)
    vmem = pl.BlockSpec(memory_space=pltpu.VMEM)
    steps = N.bit_length() - 1
    dma = pltpu.SemaphoreType.DMA
    panel, updated = pl.pallas_call(
        functools.partial(kernel, G, N, C, H, rows, block),
        out_shape=(pltpu.VMEM(front.shape[1:], F32), pltpu.VMEM(trailing.shape[1:], F32)),
        in_specs=[anywhere] * 9,
        out_specs=(vmem, vmem),
        scratch_shapes=[
            pltpu.SMEM(send_tiles.shape, jnp.int32),
            pltpu.SMEM(counts.shape, jnp.int32),
            pltpu.VMEM(leaf_l.shape[1:], F32),
            pltpu.VMEM((2 * block, depth), BF16),
            pltpu.VMEM((depth, width), F32),
            pltpu.VMEM((depth, width), BF16),
            pltpu.VMEM((depth, width), BF16),
            pltpu.VMEM((G * strip, width), F32),
            pltpu.VMEM((strip, width), F32),
            pltpu.VMEM(inv_diag.shape[1:], F32),
            pltpu.VMEM(inv_diag.shape[1:], BF16),
            pltpu.VMEM(inv_diag.shape[1:], BF16),
            pltpu.VMEM(upper.shape, F32),
            pltpu.VMEM(upper.shape, BF16),
            pltpu.VMEM(upper.shape, BF16),
            pltpu.VMEM((strip, tile), F32),
            pltpu.VMEM(((G + 1) * C, rows, width), F32),
            pltpu.VMEM((N,) + trail_list.shape[1:], jnp.int32),
            pltpu.VMEM((2, N, terms, tile), F32),
            pltpu.VMEM((rows, width), F32),
            pltpu.VMEM((2 * nt * rows, tile), BF16),
            pltpu.VMEM((nu, nt * rows, tile), F32),
            pltpu.VMEM((C + H, N, rows, tile), F32),
            pltpu.VMEM((C + H, N, rows, tile), F32),
            pltpu.VMEM((max(H, 1), rows, tile), F32),
            dma((nt + 11,)),
            dma((2,)), dma(((G - 1) * C * rows // block,)), dma((C,)), dma((C,)),
            dma((2,)),
            dma((2,)), dma((RING, 2)),
            dma((2,)), dma((2,)),
            pltpu.SemaphoreType.REGULAR((2,)),
        ],
        compiler_params=pltpu.CompilerParams(
            collective_id=0, has_side_effects=True, vmem_limit_bytes=60 << 20
        ),
    )(leaf_l, leaf_u, front, inv_diag, send_tiles, counts, trail_list, upper, trailing)
    return write_out(panel, updated)


def copy_kernel(cuts, panel, updated, panel_out, updated_out, sem):
    rows = panel.shape[0] // cuts
    copies = [pltpu.make_async_copy(updated, updated_out.at[0], sem.at[cuts])]
    for i in range(cuts):
        at = pl.ds(i * rows, rows)
        copies.append(pltpu.make_async_copy(panel.at[at], panel_out.at[0, at], sem.at[i]))
    for copy in copies:
        copy.start()
    for copy in copies:
        copy.wait()


def write_out(panel, updated):
    strip = panel.shape[0]
    cuts = next(n for n in (4, 2, 1) if strip % (8 * n) == 0)
    vmem = pl.BlockSpec(memory_space=pltpu.VMEM)
    anywhere = pl.BlockSpec(memory_space=pl.ANY)
    return pl.pallas_call(
        functools.partial(copy_kernel, cuts),
        out_shape=tuple(jax.ShapeDtypeStruct((1,) + x.shape, F32) for x in (panel, updated)),
        in_specs=[vmem, vmem],
        out_specs=(anywhere, anywhere),
        scratch_shapes=[pltpu.SemaphoreType.DMA((cuts + 1,))],
        compiler_params=pltpu.CompilerParams(vmem_limit_bytes=1 << 20),
    )(panel, updated)


def solution(mesh):
    placed = (
        P("sub", "grp", None),
        P("sub", "grp", None),
        P("sub", "grp", None),
        P("sub", None, None, None),
        P("sub", "grp", None, None),
        P("sub", "grp", None),
        P("sub", "grp", None, None),
        P(),
        P("sub", "grp", None),
    )
    return jax.shard_map(
        per_device,
        mesh=mesh,
        in_specs=placed,
        out_specs=(P("sub", "grp", None), P("sub", "grp", None)),
        check_vma=False,
    )
```

```python
import functools

import jax
import jax.numpy as jnp
from jax import lax
from jax.experimental import pallas as pl
from jax.experimental.pallas import tpu as pltpu
from jax.sharding import PartitionSpec as P

MESH = pl.DeviceIdType.MESH
F32 = jnp.float32
BF16 = jnp.bfloat16
ROWS = (32, 16, 8)
AHEAD = 2
LAGS = (2, 4)
RING = 6


def split(x):
    high = x.astype(BF16)
    return high, (x - high.astype(F32)).astype(BF16)


def dot(a, b):
    return jnp.dot(a, b, preferred_element_type=F32)


def dot3(stacked, high, low):
    m = stacked.shape[0] // 2
    both = dot(stacked, high)
    return both[:m] + both[m:] + dot(stacked[:m], low)


def kernel(
    G, N, C, H, rows, block,
    leaf_l, leaf_u, front, inv_diag, send_tiles, counts, trail_list, upper, trailing,
    pan, upd,
    tiles_buf, counts_buf, l_buf, l_two, u_buf, u_hi, u_lo, s_buf, f_buf, d_buf, d_hi, d_lo, v_buf, v_hi, v_lo, t_buf, mail,
    lists, coef, work, x_buf, prod, part, got, ahead,
    in_sem, send_sem, many_recv, up_recv, dn_recv, list_sem, x_send, x_recv, coef_sem, ahead_sem, relay,
):
    z = lax.axis_index("grp")
    me = lax.axis_index("sub")
    width = front.shape[2]
    tile = upper.shape[1]
    depth = u_buf.shape[0]
    nt = width // tile
    nu = upper.shape[0]
    cap = send_tiles.shape[2]
    strip = C * rows
    per = block // rows
    group = min(4, N // 2)
    steps = N.bit_length() - 1
    half_n = N // 2
    step = next(n for n in (64, 32, 16) if depth % n == 0)
    top = (G + 1) * C - 1
    low_end, high_end = z == 0, z == G - 1
    helper = (H > 0) & (low_end | high_end)
    helped_up, helped_dn = (H > 0) & (z == 1), (H > 0) & (z == G - 2)
    helped = helped_up | helped_dn
    ally = jnp.where(low_end | (z == G - 2), z + 1, z - 1)
    extra = jnp.where(helper, H, 0)

    def bit(value, s):
        return lax.rem(lax.div(value, 1 << s), 2)

    shifts = [(1 << s) * (1 - 2 * bit(me, s)) for s in range(steps)]

    def dest_of(p):
        if isinstance(p, int):
            return me + sum(shifts[s] for s in range(steps) if p >> (steps - 1 - s) & 1)
        return me + sum(bit(p, steps - 1 - s) * shifts[s] for s in range(steps))

    def load_l(t, first, count, n):
        at = pl.ds(t * strip + first, count)
        return pltpu.make_async_copy(leaf_l.at[0, at], l_buf.at[at], in_sem.at[n])

    def load_u(n):
        cols = pl.ds(pl.multiple_of(n * tile, tile), tile)
        return pltpu.make_async_copy(leaf_u.at[0, :, cols], u_buf.at[:, cols], in_sem.at[n])

    def load_head(row, n):
        at = pl.ds(pl.multiple_of(row, 8), block)
        return pltpu.make_async_copy(leaf_l.at[0, at], l_buf.at[at], in_sem.at[n])

    row_far = (G - 1) * strip
    head_row = jnp.where(high_end, 0, row_far)
    head = load_head(head_row, nt)
    tails = [load_head(row_far - head_row, nt + 1), load_l(0, block, (G - 1) * strip - block, nt + 2)]
    if block < strip:
        tails.append(load_l(G - 1, block, strip - block, nt + 3))
    others = [
        pltpu.make_async_copy(front.at[0], f_buf, in_sem.at[nt + 4]),
        pltpu.make_async_copy(inv_diag.at[0], d_buf, in_sem.at[nt + 5]),
        pltpu.make_async_copy(trailing.at[0], t_buf, in_sem.at[nt + 6]),
        pltpu.make_async_copy(upper, v_buf, in_sem.at[nt + 7]),
        pltpu.make_async_copy(send_tiles, tiles_buf, in_sem.at[nt + 8]),
        pltpu.make_async_copy(counts, counts_buf, in_sem.at[nt + 9]),
    ]
    small = tile // 2
    halves = [
        pltpu.make_async_copy(leaf_u.at[0, :, cols], u_buf.at[:, cols], in_sem.at[n])
        for n, cols in ((0, slice(0, small)), (nt + 11, slice(small, tile)))
    ]
    halves[0].start()
    head.start()
    halves[1].start()

    barrier = pltpu.get_barrier_semaphore()

    relayed = H > 0
    plane = jnp.logical_not(low_end | high_end) if relayed else z >= 0

    @pl.when(z > 0)
    def _():
        pl.semaphore_signal(barrier, inc=1, device_id={"grp": z - 1}, device_id_type=MESH)

    @pl.when(z < G - 1)
    def _():
        pl.semaphore_signal(barrier, inc=1, device_id={"grp": z + 1}, device_id_type=MESH)

    @pl.when(plane)
    def _():
        for p in reversed(range(1, N)):
            pl.semaphore_signal(barrier, inc=1, device_id={"sub": dest_of(p)}, device_id_type=MESH)

    pl.loop(1, nt)(lambda n: load_u(n).start())
    for copy in tails + others:
        copy.start()

    def own_list():
        return pltpu.make_async_copy(trail_list.at[0], lists.at[me], in_sem.at[nt + 10])

    def list_copy(p, owner):
        return pltpu.make_async_remote_copy(
            src_ref=trail_list.at[0], dst_ref=lists.at[owner],
            send_sem=list_sem.at[0], recv_sem=list_sem.at[1],
            device_id={"sub": dest_of(p)}, device_id_type=MESH,
        )

    def all_lists():
        return pltpu.make_async_remote_copy(
            src_ref=lists.at[pl.ds(0, N - 1)], dst_ref=lists.at[pl.ds(0, N - 1)],
            send_sem=list_sem.at[0], recv_sem=list_sem.at[1],
            device_id={"sub": dest_of(1)}, device_id_type=MESH,
        )

    def up_move(first, count, recv_sem, cols=slice(None)):
        at = pl.ds(first, count)
        return pltpu.make_async_remote_copy(
            src_ref=mail.at[at, :, cols], dst_ref=mail.at[at, :, cols],
            send_sem=send_sem.at[0], recv_sem=recv_sem,
            device_id={"grp": z + 1}, device_id_type=MESH,
        )

    def dn_move(first, count, recv_sem, cols=slice(None)):
        at = pl.ds(top + 1 - first - count, count)
        return pltpu.make_async_remote_copy(
            src_ref=mail.at[at, :, cols], dst_ref=mail.at[at, :, cols],
            send_sem=send_sem.at[1], recv_sem=recv_sem,
            device_id={"grp": z - 1}, device_id_type=MESH,
        )

    def up_copy(c, k):
        return up_move(k, 1, up_recv.at[c])

    def dn_copy(c, k):
        return dn_move(k, 1, dn_recv.at[c])

    def up_many(b, cols=slice(None)):
        return up_move(b * per, per, many_recv.at[b], cols)

    def dn_many(b, cols=slice(None)):
        return dn_move(b * per, per, many_recv.at[(G - 1) * C // per - 1 - b], cols)

    def coef_copy():
        return pltpu.make_async_remote_copy(
            src_ref=coef.at[0], dst_ref=coef.at[1],
            send_sem=coef_sem.at[0], recv_sem=coef_sem.at[1],
            device_id={"grp": ally}, device_id_type=MESH,
        )

    def ahead_copy(e):
        return pltpu.make_async_remote_copy(
            src_ref=ahead.at[e], dst_ref=ahead.at[e],
            send_sem=ahead_sem.at[0], recv_sem=ahead_sem.at[1],
            device_id={"grp": ally}, device_id_type=MESH,
        )

    def all_ahead():
        return pltpu.make_async_remote_copy(
            src_ref=ahead, dst_ref=ahead,
            send_sem=ahead_sem.at[0], recv_sem=ahead_sem.at[1],
            device_id={"grp": ally}, device_id_type=MESH,
        )

    def halve(row):
        at = pl.ds(pl.multiple_of(row, 8), block)
        high, low = split(l_buf[at, :])
        l_two[:block, :] = high
        l_two[block:, :] = low

    def tile_cols(n):
        return pl.ds(pl.multiple_of(n * tile, tile), tile)

    def product(row, cols):
        at = pl.ds(pl.multiple_of(row, 8), block)
        s_buf[at, cols] = dot3(l_two[...], u_hi[:, cols], u_lo[:, cols])

    def schur(row):
        halve(row)
        pl.loop(0, nt)(lambda n: product(row, tile_cols(n)))

    def forward(slot, row, first):
        at = pl.ds(pl.multiple_of(row, 8), rows)

        @pl.when(first)
        def _():
            mail[slot] = s_buf[at, :]

        @pl.when(jnp.logical_not(first))
        def _():
            mail[slot] = mail[slot] + s_buf[at, :]

    def begin(copy, cols):
        copy.wait()

        @pl.loop(0, depth, step=step)
        def _(r):
            at = pl.ds(pl.multiple_of(r, step), step)
            high, low = split(u_buf[at, cols])
            u_hi[at, cols] = high
            u_lo[at, cols] = low

        @pl.when(low_end | high_end)
        def _():
            product(head_row, cols)

    def begin_send(cols):
        @pl.when(low_end)
        def _():
            for k in range(per):
                mail[k, :, cols] = s_buf[(G - 1) * strip + k * rows : (G - 1) * strip + (k + 1) * rows, cols]
            up_many(0, cols).start()

        @pl.when(high_end)
        def _():
            for k in range(per):
                mail[top - k, :, cols] = s_buf[k * rows : (k + 1) * rows, cols]
            dn_many(0, cols).start()

    head.wait()

    @pl.when(low_end | high_end)
    def _():
        halve(head_row)

    begin(halves[0], slice(0, small))
    pl.semaphore_wait(barrier, jnp.where(plane, N - 1, 0) + jnp.where(z > 0, 1, 0) + jnp.where(z < G - 1, 1, 0))
    begin_send(slice(0, small))
    begin(halves[1], slice(small, tile))
    begin_send(slice(small, tile))

    @pl.when(helped)
    def _():
        for p in reversed(range(1, N)):
            pl.semaphore_signal(relay.at[0], inc=1, device_id={"sub": dest_of(p)}, device_id_type=MESH)

    @pl.loop(1, nt)
    def _(n):
        begin(load_u(n), tile_cols(n))
        begin_send(tile_cols(n))

    @pl.when(helped)
    def _():
        pl.semaphore_wait(relay.at[0], N - 1)
        pl.semaphore_signal(relay.at[1], inc=1, device_id={"grp": ally}, device_id_type=MESH)

    def weigh(p):
        d = dest_of(p)

        source, slot, which = lists[d, 0], lists[d, 1], lists[d, 2]
        pick = jnp.zeros_like(source)
        for c in range(cap):
            pick = jnp.where(slot == c, tiles_buf[0, 0, c, d], pick)
        live = (source == me) & (slot < counts_buf[0, 0, d])
        code = jnp.where(live, pick * nu + which, -1)
        terms = lax.broadcasted_iota(jnp.int32, (coef.shape[2], code.shape[1]), 0)
        total = jnp.sum(jnp.where(code == terms, 1.0, 0.0).astype(F32), axis=1, keepdims=True)
        coef[0, p] = jnp.broadcast_to(total, coef.shape[2:])

    def exchange(e):
        return pltpu.make_async_remote_copy(
            src_ref=part.at[e, pl.ds(half_n, half_n)], dst_ref=got.at[e, pl.ds(half_n, half_n)],
            send_sem=x_send.at[0], recv_sem=x_recv.at[lax.rem(e, RING), 0],
            device_id={"sub": dest_of(half_n)}, device_id_type=MESH,
        )

    def scatter(e, p, count=1):
        return pltpu.make_async_remote_copy(
            src_ref=part.at[e, pl.ds(p, count)], dst_ref=got.at[e, pl.ds(p, count)],
            send_sem=x_send.at[1], recv_sem=x_recv.at[lax.rem(e, RING), 1],
            device_id={"sub": dest_of(p)}, device_id_type=MESH,
        )

    def chunk(e):
        c = jnp.where(helper, e - H, jnp.where(helped, jnp.where(e < H, C - H + e, e - H), e))
        return jnp.maximum(c, 0)

    def strip_rows(c):
        return pl.ds(pl.multiple_of(c * rows, 8), rows)

    def solve(e):
        helping = helper & (e < H)
        late = helped & (e < H)
        c = chunk(e)
        at = strip_rows(c)
        k_late = (G - 1) * C - H + e

        @pl.when(helping)
        def _():
            there = ally * strip + (C - H + e) * rows
            work[...] = s_buf[pl.ds(pl.multiple_of(there, 8), rows), :]

        @pl.when(jnp.logical_not(helping))
        def _():
            work[...] = f_buf[at, :] - s_buf[pl.ds(pl.multiple_of(z * strip + c * rows, 8), rows), :]

            @pl.when((z > 0) & jnp.logical_not(late & helped_up))
            def _():
                k = (G - 1 - z) * C + c
                up_copy(c, k).wait_recv()
                work[...] = work[...] - mail[k]

            @pl.when((z < G - 1) & jnp.logical_not(late & helped_dn))
            def _():
                k = z * C + c
                dn_copy(c, k).wait_recv()
                work[...] = work[...] - mail[top - k]

        half = nt * rows
        for j in range(nt):
            cols = slice(j * tile, (j + 1) * tile)
            high, low = split(work[:, cols])
            solved = dot3(jnp.concatenate([high, low], axis=0), d_hi[j], d_lo[j])
            work[:, cols] = solved
            high, low = split(solved)
            x_buf[j * rows : (j + 1) * rows, :] = high
            x_buf[half + j * rows : half + (j + 1) * rows, :] = low

        @pl.when(jnp.logical_not(helping))
        def _():
            pan[at, :] = work[...]

        @pl.when(helping & low_end)
        def _():
            mail[k_late] = work[...]
            up_copy(C - H + e, k_late).start()

        @pl.when(helping & high_end)
        def _():
            mail[top - k_late] = work[...]
            dn_copy(C - H + e, k_late).start()

        for u in range(nu):
            prod[u] = dot3(x_buf[...], v_hi[u], v_lo[u])

        @pl.when(helping & (e == 0))
        def _():
            coef_copy().wait_recv()

        table = jnp.where(helping, 1, 0)

        def mix(g):
            p0 = g * group

            @pl.loop(0, rows, step=8)
            def _(r):
                r = pl.multiple_of(r, 8)
                sums = [None] * group
                for j in range(nt):
                    for u in range(nu):
                        value = prod[u, pl.ds(j * rows + r, 8), :]
                        for q in range(group):
                            n = j * nu + u
                            term = coef[table, p0 + q, n : n + 1, :] * value
                            sums[q] = term if sums[q] is None else sums[q] + term
                for q in range(group):
                    part[e, p0 + q, pl.ds(r, 8), :] = sums[q]

        groups = N // group
        pl.loop(groups // 2, groups)(mix)
        exchange(e).start()
        pl.loop(0, groups // 2)(mix)

    def stage(e, s):
        if s == 0:
            exchange(e).wait_recv()
            if half_n > 1:
                part[e, 1:half_n] = part[e, 1:half_n] + got[e, half_n + 1 :]
                for p in reversed(range(1, half_n)):
                    scatter(e, p).start()
            part[e, 0] = part[e, 0] + got[e, half_n]
        else:
            total = part[e, 0]
            if half_n > 1:
                scatter(e, 1, half_n - 1).wait_recv()
                for p in range(1, half_n):
                    total = total + got[e, p]
            helping = helper & (e < H)

            @pl.when(helping)
            def _():
                ahead[e] = total
                ahead_copy(e).start()

            @pl.when(jnp.logical_not(helping))
            def _():
                at = strip_rows(chunk(e))
                upd[at, :] = t_buf[at, :] - total

    lag_up, lag_dn = z * per, (G - 1 - z) * per
    base = jnp.maximum((G - 1 - z) * C + lag_up, z * C + lag_dn)

    @pl.loop(0, base + C + LAGS[1])
    def _(i):
        up, down, own = i - lag_up, i - lag_dn, i - base
        e = own + extra
        has_up = (up >= jnp.where(low_end, per, 0)) & (up < (G - 1 - z) * C)
        has_dn = (down >= jnp.where(high_end, per, 0)) & (down < z * C)
        plain = (G - 1) * C - extra
        up_row = (G - 1) * strip + lax.rem(jnp.maximum(up, 0), C) * rows - lax.div(jnp.maximum(up, 0), C) * strip

        @pl.loop(0, 3)
        def _(job):
            k = jnp.where(job == 0, up, jnp.where(job == 1, down, own + C))
            has = ((job == 0) & has_up) | ((job == 1) & has_dn) | ((job == 2) & (k >= 0) & (k < C))
            row = jnp.where(job == 0, up_row, jnp.where(job == 1, down * rows, z * strip + k * rows))

            @pl.when(has & (lax.rem(jnp.maximum(k, 0), per) == 0))
            def _():
                schur(row)

        @pl.when(has_up & (up < plain))
        def _():
            place = lax.rem(up, per)
            final = (G - 2 - z) * C

            @pl.when((z > 0) & (place == 0))
            def _():
                up_many(lax.div(up, per)).wait_recv()

            forward(up, up_row, z == 0)

            @pl.when((up < final) & (place == per - 1))
            def _():
                up_many(lax.div(up, per)).start()

            @pl.when(up >= final)
            def _():
                up_copy(up - final, up).start()

        @pl.when(has_dn & (down < plain))
        def _():
            place = lax.rem(down, per)
            final = (z - 1) * C

            @pl.when((z < G - 1) & (place == 0))
            def _():
                dn_many(lax.div(down, per)).wait_recv()

            forward(top - down, down * rows, z == G - 1)

            @pl.when((down < final) & (place == per - 1))
            def _():
                dn_many(lax.div(down, per)).start()

            @pl.when(down >= final)
            def _():
                dn_copy(down - final, down).start()

        @pl.when(i == 1)
        def _():
            own_list().start()
            for copy in tails + others:
                copy.wait()

            @pl.when(helper)
            def _():
                pl.semaphore_wait(relay.at[1], 1)

            @pl.loop(1, N)
            def _(p):
                list_copy(p, me).start()

            for j in range(nt):
                high, low = split(d_buf[j])
                d_hi[j] = high
                d_lo[j] = low
            for u in range(nu):
                high, low = split(v_buf[u])
                v_hi[u] = high
                v_lo[u] = low

        @pl.when(i == 3)
        def _():
            own_list().wait()
            all_lists().wait_recv()
            pl.loop(0, N)(weigh)

            @pl.when(helped)
            def _():
                coef_copy().start()

        turn = C + extra - 2
        ready = jnp.where(e < turn, e - LAGS[0] + 1, e)

        @pl.when((e >= LAGS[1]) & (e - LAGS[1] < C + extra))
        def _():
            stage(e - LAGS[1], 1)

        @pl.loop(jnp.where(e <= turn, e - LAGS[0], e - 1), ready)
        def _(old):
            @pl.when((old >= 0) & (old < C + extra))
            def _():
                stage(old, 0)

        @pl.when((e >= 0) & (e < C + extra))
        def _():
            solve(e)

    @pl.when(helped)
    def _():
        @pl.loop(0, H)
        def _(e):
            at = strip_rows(C - H + e)
            k = (G - 1) * C - H + e

            @pl.when(helped_up)
            def _():
                up_copy(C - H + e, k).wait_recv()
                pan[at, :] = pan[at, :] - mail[k]

            @pl.when(helped_dn)
            def _():
                dn_copy(C - H + e, k).wait_recv()
                pan[at, :] = pan[at, :] - mail[top - k]

        all_ahead().wait_recv()

        @pl.loop(0, H)
        def _(e):
            at = strip_rows(C - H + e)
            upd[at, :] = upd[at, :] + ahead[e]

        coef_copy().wait_send()

    for g in range(G):
        @pl.when(z == g)
        def _():
            if g < G - 1:
                up_move(0, (G - 1 - g) * C, up_recv.at[0]).wait_send()
            if g > 0:
                dn_move(0, g * C, dn_recv.at[0]).wait_send()
            worked = C + (H if g in (0, G - 1) else 0)
            for s, first, count in ((0, half_n, half_n), (1, 1, half_n - 1)):
                if count:
                    sent = part.at[pl.ds(0, worked), pl.ds(first, count)]
                    pltpu.make_async_remote_copy(
                        src_ref=sent, dst_ref=sent, send_sem=x_send.at[s], recv_sem=x_recv.at[0, s],
                        device_id={"sub": dest_of(half_n)}, device_id_type=MESH,
                    ).wait_send()

    if H:
        @pl.when(helper)
        def _():
            all_ahead().wait_send()

    all_lists().wait_send()


def per_device(leaf_l, leaf_u, front, inv_diag, send_tiles, counts, trail_list, upper, trailing):
    G = lax.axis_size("grp")
    N = lax.axis_size("sub")
    strip, width = front.shape[1:]
    depth = leaf_u.shape[1]
    tile = upper.shape[1]
    rows = next(r for r in ROWS if strip % r == 0)
    C = strip // rows
    H = min(AHEAD, C) if G > 3 else 0
    block = 2 * rows if strip % (2 * rows) == 0 else strip
    nt, nu = width // tile, upper.shape[0]
    terms = -(-nt * nu // 8) * 8
    send_tiles = jnp.transpose(send_tiles, (0, 1, 3, 2))
    trail_list = jnp.transpose(trail_list, (0, 3, 1, 2))
    anywhere = pl.BlockSpec(memory_space=pl.ANY)
    vmem = pl.BlockSpec(memory_space=pltpu.VMEM)
    steps = N.bit_length() - 1
    dma = pltpu.SemaphoreType.DMA
    panel, updated = pl.pallas_call(
        functools.partial(kernel, G, N, C, H, rows, block),
        out_shape=(pltpu.VMEM(front.shape[1:], F32), pltpu.VMEM(trailing.shape[1:], F32)),
        in_specs=[anywhere] * 9,
        out_specs=(vmem, vmem),
        scratch_shapes=[
            pltpu.SMEM(send_tiles.shape, jnp.int32),
            pltpu.SMEM(counts.shape, jnp.int32),
            pltpu.VMEM(leaf_l.shape[1:], F32),
            pltpu.VMEM((2 * block, depth), BF16),
            pltpu.VMEM((depth, width), F32),
            pltpu.VMEM((depth, width), BF16),
            pltpu.VMEM((depth, width), BF16),
            pltpu.VMEM((G * strip, width), F32),
            pltpu.VMEM((strip, width), F32),
            pltpu.VMEM(inv_diag.shape[1:], F32),
            pltpu.VMEM(inv_diag.shape[1:], BF16),
            pltpu.VMEM(inv_diag.shape[1:], BF16),
            pltpu.VMEM(upper.shape, F32),
            pltpu.VMEM(upper.shape, BF16),
            pltpu.VMEM(upper.shape, BF16),
            pltpu.VMEM((strip, tile), F32),
            pltpu.VMEM(((G + 1) * C, rows, width), F32),
            pltpu.VMEM((N,) + trail_list.shape[1:], jnp.int32),
            pltpu.VMEM((2, N, terms, tile), F32),
            pltpu.VMEM((rows, width), F32),
            pltpu.VMEM((2 * nt * rows, tile), BF16),
            pltpu.VMEM((nu, nt * rows, tile), F32),
            pltpu.VMEM((C + H, N, rows, tile), F32),
            pltpu.VMEM((C + H, N, rows, tile), F32),
            pltpu.VMEM((max(H, 1), rows, tile), F32),
            dma((nt + 12,)),
            dma((2,)), dma(((G - 1) * C * rows // block,)), dma((C,)), dma((C,)),
            dma((2,)),
            dma((2,)), dma((RING, 2)),
            dma((2,)), dma((2,)),
            pltpu.SemaphoreType.REGULAR((2,)),
        ],
        compiler_params=pltpu.CompilerParams(
            collective_id=0, has_side_effects=True, vmem_limit_bytes=60 << 20
        ),
    )(leaf_l, leaf_u, front, inv_diag, send_tiles, counts, trail_list, upper, trailing)
    return write_out(panel, updated)


def copy_kernel(cuts, panel, updated, panel_out, updated_out, sem):
    rows = panel.shape[0] // cuts
    copies = [pltpu.make_async_copy(updated, updated_out.at[0], sem.at[cuts])]
    for i in range(cuts):
        at = pl.ds(i * rows, rows)
        copies.append(pltpu.make_async_copy(panel.at[at], panel_out.at[0, at], sem.at[i]))
    for copy in copies:
        copy.start()
    for copy in copies:
        copy.wait()


def write_out(panel, updated):
    strip = panel.shape[0]
    cuts = next(n for n in (4, 2, 1) if strip % (8 * n) == 0)
    vmem = pl.BlockSpec(memory_space=pltpu.VMEM)
    anywhere = pl.BlockSpec(memory_space=pl.ANY)
    return pl.pallas_call(
        functools.partial(copy_kernel, cuts),
        out_shape=tuple(jax.ShapeDtypeStruct((1,) + x.shape, F32) for x in (panel, updated)),
        in_specs=[vmem, vmem],
        out_specs=(anywhere, anywhere),
        scratch_shapes=[pltpu.SemaphoreType.DMA((cuts + 1,))],
        compiler_params=pltpu.CompilerParams(vmem_limit_bytes=1 << 20),
    )(panel, updated)


def solution(mesh):
    placed = (
        P("sub", "grp", None),
        P("sub", "grp", None),
        P("sub", "grp", None),
        P("sub", None, None, None),
        P("sub", "grp", None, None),
        P("sub", "grp", None),
        P("sub", "grp", None, None),
        P(),
        P("sub", "grp", None),
    )
    return jax.shard_map(
        per_device,
        mesh=mesh,
        in_specs=placed,
        out_specs=(P("sub", "grp", None), P("sub", "grp", None)),
        check_vma=False,
    )
```

```python
import functools

import jax
import jax.numpy as jnp
from jax import lax
from jax.experimental import pallas as pl
from jax.experimental.pallas import tpu as pltpu
from jax.sharding import PartitionSpec as P

MESH = pl.DeviceIdType.MESH
F32 = jnp.float32
BF16 = jnp.bfloat16
ROWS = (32, 16, 8)
AHEAD = 2
LAGS = (2, 4)
RING = 6


def split(x):
    high = x.astype(BF16)
    return high, (x - high.astype(F32)).astype(BF16)


def dot(a, b):
    return jnp.dot(a, b, preferred_element_type=F32)


def dot3(stacked, high, low):
    m = stacked.shape[0] // 2
    both = dot(stacked, high)
    return both[:m] + both[m:] + dot(stacked[:m], low)


def kernel(
    G, N, C, H, rows, block,
    leaf_l, leaf_u, front, inv_diag, send_tiles, counts, trail_list, upper, trailing,
    pan, upd,
    tiles_buf, counts_buf, l_buf, l_two, u_buf, u_hi, u_lo, s_buf, f_buf, d_buf, d_hi, d_lo, v_buf, v_hi, v_lo, t_buf, mail,
    lists, coef, work, x_buf, prod, part, got, ahead,
    in_sem, send_sem, many_recv, up_recv, dn_recv, list_sem, x_send, x_recv, coef_sem, ahead_sem, relay,
):
    z = lax.axis_index("grp")
    me = lax.axis_index("sub")
    width = front.shape[2]
    tile = upper.shape[1]
    depth = u_buf.shape[0]
    nt = width // tile
    nu = upper.shape[0]
    cap = send_tiles.shape[2]
    strip = C * rows
    per = block // rows
    group = min(4, N // 2)
    steps = N.bit_length() - 1
    half_n = N // 2
    step = next(n for n in (256, 128, 64, 32, 16) if depth % n == 0)
    top = (G + 1) * C - 1
    low_end, high_end = z == 0, z == G - 1
    helper = (H > 0) & (low_end | high_end)
    helped_up, helped_dn = (H > 0) & (z == 1), (H > 0) & (z == G - 2)
    helped = helped_up | helped_dn
    ally = jnp.where(low_end | (z == G - 2), z + 1, z - 1)
    extra = jnp.where(helper, H, 0)

    def bit(value, s):
        return lax.rem(lax.div(value, 1 << s), 2)

    shifts = [(1 << s) * (1 - 2 * bit(me, s)) for s in range(steps)]

    def dest_of(p):
        if isinstance(p, int):
            return me + sum(shifts[s] for s in range(steps) if p >> (steps - 1 - s) & 1)
        return me + sum(bit(p, steps - 1 - s) * shifts[s] for s in range(steps))

    def load_l(t, first, count, n):
        at = pl.ds(t * strip + first, count)
        return pltpu.make_async_copy(leaf_l.at[0, at], l_buf.at[at], in_sem.at[n])

    def load_u(n):
        cols = pl.ds(pl.multiple_of(n * tile, tile), tile)
        return pltpu.make_async_copy(leaf_u.at[0, :, cols], u_buf.at[:, cols], in_sem.at[n])

    def load_head(row, n):
        at = pl.ds(pl.multiple_of(row, 8), block)
        return pltpu.make_async_copy(leaf_l.at[0, at], l_buf.at[at], in_sem.at[n])

    row_far = (G - 1) * strip
    head_row = jnp.where(high_end, 0, row_far)
    head = load_head(head_row, nt)
    tails = [load_head(row_far - head_row, nt + 1), load_l(0, block, (G - 1) * strip - block, nt + 2)]
    if block < strip:
        tails.append(load_l(G - 1, block, strip - block, nt + 3))
    others = [
        pltpu.make_async_copy(front.at[0], f_buf, in_sem.at[nt + 4]),
        pltpu.make_async_copy(inv_diag.at[0], d_buf, in_sem.at[nt + 5]),
        pltpu.make_async_copy(trailing.at[0], t_buf, in_sem.at[nt + 6]),
        pltpu.make_async_copy(upper, v_buf, in_sem.at[nt + 7]),
        pltpu.make_async_copy(send_tiles, tiles_buf, in_sem.at[nt + 8]),
        pltpu.make_async_copy(counts, counts_buf, in_sem.at[nt + 9]),
    ]
    small = tile // 2
    halves = [
        pltpu.make_async_copy(leaf_u.at[0, :, cols], u_buf.at[:, cols], in_sem.at[n])
        for n, cols in ((0, slice(0, small)), (nt + 11, slice(small, tile)))
    ]
    head.start()
    halves[0].start()
    halves[1].start()

    barrier = pltpu.get_barrier_semaphore()

    relayed = H > 0
    plane = jnp.logical_not(low_end | high_end) if relayed else z >= 0

    @pl.when(z > 0)
    def _():
        pl.semaphore_signal(barrier, inc=1, device_id={"grp": z - 1}, device_id_type=MESH)

    @pl.when(z < G - 1)
    def _():
        pl.semaphore_signal(barrier, inc=1, device_id={"grp": z + 1}, device_id_type=MESH)

    @pl.when(plane)
    def _():
        for p in reversed(range(1, N)):
            pl.semaphore_signal(barrier, inc=1, device_id={"sub": dest_of(p)}, device_id_type=MESH)

    pl.loop(1, nt)(lambda n: load_u(n).start())
    for copy in tails + others:
        copy.start()

    def own_list():
        return pltpu.make_async_copy(trail_list.at[0], lists.at[me], in_sem.at[nt + 10])

    def list_copy(p, owner):
        return pltpu.make_async_remote_copy(
            src_ref=trail_list.at[0], dst_ref=lists.at[owner],
            send_sem=list_sem.at[0], recv_sem=list_sem.at[1],
            device_id={"sub": dest_of(p)}, device_id_type=MESH,
        )

    def all_lists():
        return pltpu.make_async_remote_copy(
            src_ref=lists.at[pl.ds(0, N - 1)], dst_ref=lists.at[pl.ds(0, N - 1)],
            send_sem=list_sem.at[0], recv_sem=list_sem.at[1],
            device_id={"sub": dest_of(1)}, device_id_type=MESH,
        )

    def up_move(first, count, recv_sem, cols=slice(None)):
        at = pl.ds(first, count)
        return pltpu.make_async_remote_copy(
            src_ref=mail.at[at, :, cols], dst_ref=mail.at[at, :, cols],
            send_sem=send_sem.at[0], recv_sem=recv_sem,
            device_id={"grp": z + 1}, device_id_type=MESH,
        )

    def dn_move(first, count, recv_sem, cols=slice(None)):
        at = pl.ds(top + 1 - first - count, count)
        return pltpu.make_async_remote_copy(
            src_ref=mail.at[at, :, cols], dst_ref=mail.at[at, :, cols],
            send_sem=send_sem.at[1], recv_sem=recv_sem,
            device_id={"grp": z - 1}, device_id_type=MESH,
        )

    def up_copy(c, k):
        return up_move(k, 1, up_recv.at[c])

    def dn_copy(c, k):
        return dn_move(k, 1, dn_recv.at[c])

    def up_many(b, cols=slice(None)):
        return up_move(b * per, per, many_recv.at[b], cols)

    def dn_many(b, cols=slice(None)):
        return dn_move(b * per, per, many_recv.at[(G - 1) * C // per - 1 - b], cols)

    def coef_copy():
        return pltpu.make_async_remote_copy(
            src_ref=coef.at[0], dst_ref=coef.at[1],
            send_sem=coef_sem.at[0], recv_sem=coef_sem.at[1],
            device_id={"grp": ally}, device_id_type=MESH,
        )

    def ahead_copy(e):
        return pltpu.make_async_remote_copy(
            src_ref=ahead.at[e], dst_ref=ahead.at[e],
            send_sem=ahead_sem.at[0], recv_sem=ahead_sem.at[1],
            device_id={"grp": ally}, device_id_type=MESH,
        )

    def all_ahead():
        return pltpu.make_async_remote_copy(
            src_ref=ahead, dst_ref=ahead,
            send_sem=ahead_sem.at[0], recv_sem=ahead_sem.at[1],
            device_id={"grp": ally}, device_id_type=MESH,
        )

    def halve(row):
        at = pl.ds(pl.multiple_of(row, 8), block)
        high, low = split(l_buf[at, :])
        l_two[:block, :] = high
        l_two[block:, :] = low

    def tile_cols(n):
        return pl.ds(pl.multiple_of(n * tile, tile), tile)

    def product(row, cols):
        at = pl.ds(pl.multiple_of(row, 8), block)
        s_buf[at, cols] = dot3(l_two[...], u_hi[:, cols], u_lo[:, cols])

    def schur(row):
        halve(row)
        pl.loop(0, nt)(lambda n: product(row, tile_cols(n)))

    def forward(slot, row, first):
        at = pl.ds(pl.multiple_of(row, 8), rows)

        @pl.when(first)
        def _():
            mail[slot] = s_buf[at, :]

        @pl.when(jnp.logical_not(first))
        def _():
            mail[slot] = mail[slot] + s_buf[at, :]

    def begin(copy, cols):
        copy.wait()

        @pl.loop(0, depth, step=step)
        def _(r):
            at = pl.ds(pl.multiple_of(r, step), step)
            high, low = split(u_buf[at, cols])
            u_hi[at, cols] = high
            u_lo[at, cols] = low

        @pl.when(low_end | high_end)
        def _():
            product(head_row, cols)

    def begin_send(cols):
        @pl.when(low_end)
        def _():
            for k in range(per):
                mail[k, :, cols] = s_buf[(G - 1) * strip + k * rows : (G - 1) * strip + (k + 1) * rows, cols]
            up_many(0, cols).start()

        @pl.when(high_end)
        def _():
            for k in range(per):
                mail[top - k, :, cols] = s_buf[k * rows : (k + 1) * rows, cols]
            dn_many(0, cols).start()

    head.wait()

    @pl.when(low_end | high_end)
    def _():
        halve(head_row)

    begin(halves[0], slice(0, small))
    pl.semaphore_wait(barrier, jnp.where(plane, N - 1, 0) + jnp.where(z > 0, 1, 0) + jnp.where(z < G - 1, 1, 0))
    begin_send(slice(0, small))
    begin(halves[1], slice(small, tile))
    begin_send(slice(small, tile))

    @pl.when(helped)
    def _():
        for p in reversed(range(1, N)):
            pl.semaphore_signal(relay.at[0], inc=1, device_id={"sub": dest_of(p)}, device_id_type=MESH)

    @pl.loop(1, nt)
    def _(n):
        begin(load_u(n), tile_cols(n))
        begin_send(tile_cols(n))

    @pl.when(helped)
    def _():
        pl.semaphore_wait(relay.at[0], N - 1)
        pl.semaphore_signal(relay.at[1], inc=1, device_id={"grp": ally}, device_id_type=MESH)

    def weigh(p):
        d = dest_of(p)

        source, slot, which = lists[d, 0], lists[d, 1], lists[d, 2]
        pick = jnp.zeros_like(source)
        for c in range(cap):
            pick = jnp.where(slot == c, tiles_buf[0, 0, c, d], pick)
        live = (source == me) & (slot < counts_buf[0, 0, d])
        code = jnp.where(live, pick * nu + which, -1)
        terms = lax.broadcasted_iota(jnp.int32, (coef.shape[2], code.shape[1]), 0)
        total = jnp.sum(jnp.where(code == terms, 1.0, 0.0).astype(F32), axis=1, keepdims=True)
        coef[0, p] = jnp.broadcast_to(total, coef.shape[2:])

    def exchange(e):
        return pltpu.make_async_remote_copy(
            src_ref=part.at[e, pl.ds(half_n, half_n)], dst_ref=got.at[e, pl.ds(half_n, half_n)],
            send_sem=x_send.at[0], recv_sem=x_recv.at[lax.rem(e, RING), 0],
            device_id={"sub": dest_of(half_n)}, device_id_type=MESH,
        )

    def scatter(e, p, count=1):
        return pltpu.make_async_remote_copy(
            src_ref=part.at[e, pl.ds(p, count)], dst_ref=got.at[e, pl.ds(p, count)],
            send_sem=x_send.at[1], recv_sem=x_recv.at[lax.rem(e, RING), 1],
            device_id={"sub": dest_of(p)}, device_id_type=MESH,
        )

    def chunk(e):
        c = jnp.where(helper, e - H, jnp.where(helped, jnp.where(e < H, C - H + e, e - H), e))
        return jnp.maximum(c, 0)

    def strip_rows(c):
        return pl.ds(pl.multiple_of(c * rows, 8), rows)

    def solve(e):
        helping = helper & (e < H)
        late = helped & (e < H)
        c = chunk(e)
        at = strip_rows(c)
        k_late = (G - 1) * C - H + e

        @pl.when(helping)
        def _():
            there = ally * strip + (C - H + e) * rows
            work[...] = s_buf[pl.ds(pl.multiple_of(there, 8), rows), :]

        @pl.when(jnp.logical_not(helping))
        def _():
            work[...] = f_buf[at, :] - s_buf[pl.ds(pl.multiple_of(z * strip + c * rows, 8), rows), :]

            @pl.when((z > 0) & jnp.logical_not(late & helped_up))
            def _():
                k = (G - 1 - z) * C + c
                up_copy(c, k).wait_recv()
                work[...] = work[...] - mail[k]

            @pl.when((z < G - 1) & jnp.logical_not(late & helped_dn))
            def _():
                k = z * C + c
                dn_copy(c, k).wait_recv()
                work[...] = work[...] - mail[top - k]

        half = nt * rows
        for j in range(nt):
            cols = slice(j * tile, (j + 1) * tile)
            high, low = split(work[:, cols])
            solved = dot3(jnp.concatenate([high, low], axis=0), d_hi[j], d_lo[j])
            work[:, cols] = solved
            high, low = split(solved)
            x_buf[j * rows : (j + 1) * rows, :] = high
            x_buf[half + j * rows : half + (j + 1) * rows, :] = low

        @pl.when(jnp.logical_not(helping))
        def _():
            pan[at, :] = work[...]

        @pl.when(helping & low_end)
        def _():
            mail[k_late] = work[...]
            up_copy(C - H + e, k_late).start()

        @pl.when(helping & high_end)
        def _():
            mail[top - k_late] = work[...]
            dn_copy(C - H + e, k_late).start()

        for u in range(nu):
            prod[u] = dot3(x_buf[...], v_hi[u], v_lo[u])

        @pl.when(helping & (e == 0))
        def _():
            coef_copy().wait_recv()

        table = jnp.where(helping, 1, 0)

        def mix(g):
            p0 = g * group

            @pl.loop(0, rows, step=8)
            def _(r):
                r = pl.multiple_of(r, 8)
                sums = [None] * group
                for j in range(nt):
                    for u in range(nu):
                        value = prod[u, pl.ds(j * rows + r, 8), :]
                        for q in range(group):
                            n = j * nu + u
                            term = coef[table, p0 + q, n : n + 1, :] * value
                            sums[q] = term if sums[q] is None else sums[q] + term
                for q in range(group):
                    part[e, p0 + q, pl.ds(r, 8), :] = sums[q]

        groups = N // group
        pl.loop(groups // 2, groups)(mix)
        exchange(e).start()
        pl.loop(0, groups // 2)(mix)

    def stage(e, s):
        if s == 0:
            exchange(e).wait_recv()
            if half_n > 1:
                part[e, 1:half_n] = part[e, 1:half_n] + got[e, half_n + 1 :]
                for p in reversed(range(1, half_n)):
                    scatter(e, p).start()
            part[e, 0] = part[e, 0] + got[e, half_n]
        else:
            total = part[e, 0]
            if half_n > 1:
                scatter(e, 1, half_n - 1).wait_recv()
                for p in range(1, half_n):
                    total = total + got[e, p]
            helping = helper & (e < H)

            @pl.when(helping)
            def _():
                ahead[e] = total
                ahead_copy(e).start()

            @pl.when(jnp.logical_not(helping))
            def _():
                at = strip_rows(chunk(e))
                upd[at, :] = t_buf[at, :] - total

    lag_up, lag_dn = z * per, (G - 1 - z) * per
    base = jnp.maximum((G - 1 - z) * C + lag_up, z * C + lag_dn)

    @pl.loop(0, base + C + LAGS[1])
    def _(i):
        up, down, own = i - lag_up, i - lag_dn, i - base
        e = own + extra
        has_up = (up >= jnp.where(low_end, per, 0)) & (up < (G - 1 - z) * C)
        has_dn = (down >= jnp.where(high_end, per, 0)) & (down < z * C)
        plain = (G - 1) * C - extra
        up_row = (G - 1) * strip + lax.rem(jnp.maximum(up, 0), C) * rows - lax.div(jnp.maximum(up, 0), C) * strip

        @pl.loop(0, 3)
        def _(job):
            k = jnp.where(job == 0, up, jnp.where(job == 1, down, own + C))
            has = ((job == 0) & has_up) | ((job == 1) & has_dn) | ((job == 2) & (k >= 0) & (k < C))
            row = jnp.where(job == 0, up_row, jnp.where(job == 1, down * rows, z * strip + k * rows))

            @pl.when(has & (lax.rem(jnp.maximum(k, 0), per) == 0))
            def _():
                schur(row)

        @pl.when(has_up & (up < plain))
        def _():
            place = lax.rem(up, per)
            final = (G - 2 - z) * C

            @pl.when((z > 0) & (place == 0))
            def _():
                up_many(lax.div(up, per)).wait_recv()

            forward(up, up_row, z == 0)

            @pl.when((up < final) & (place == per - 1))
            def _():
                up_many(lax.div(up, per)).start()

            @pl.when(up >= final)
            def _():
                up_copy(up - final, up).start()

        @pl.when(has_dn & (down < plain))
        def _():
            place = lax.rem(down, per)
            final = (z - 1) * C

            @pl.when((z < G - 1) & (place == 0))
            def _():
                dn_many(lax.div(down, per)).wait_recv()

            forward(top - down, down * rows, z == G - 1)

            @pl.when((down < final) & (place == per - 1))
            def _():
                dn_many(lax.div(down, per)).start()

            @pl.when(down >= final)
            def _():
                dn_copy(down - final, down).start()

        @pl.when(i == 1)
        def _():
            own_list().start()
            for copy in tails + others:
                copy.wait()

            @pl.when(helper)
            def _():
                pl.semaphore_wait(relay.at[1], 1)

            @pl.loop(1, N)
            def _(p):
                list_copy(p, me).start()

            for j in range(nt):
                high, low = split(d_buf[j])
                d_hi[j] = high
                d_lo[j] = low
            for u in range(nu):
                high, low = split(v_buf[u])
                v_hi[u] = high
                v_lo[u] = low

        @pl.when(i == 3)
        def _():
            own_list().wait()
            all_lists().wait_recv()
            pl.loop(0, N)(weigh)

            @pl.when(helped)
            def _():
                coef_copy().start()

        turn = C + extra - 2
        ready = jnp.where(e < turn, e - LAGS[0] + 1, e)

        @pl.when((e >= LAGS[1]) & (e - LAGS[1] < C + extra))
        def _():
            stage(e - LAGS[1], 1)

        @pl.loop(jnp.where(e <= turn, e - LAGS[0], e - 1), ready)
        def _(old):
            @pl.when((old >= 0) & (old < C + extra))
            def _():
                stage(old, 0)

        @pl.when((e >= 0) & (e < C + extra))
        def _():
            solve(e)

    @pl.when(helped)
    def _():
        @pl.loop(0, H)
        def _(e):
            at = strip_rows(C - H + e)
            k = (G - 1) * C - H + e

            @pl.when(helped_up)
            def _():
                up_copy(C - H + e, k).wait_recv()
                pan[at, :] = pan[at, :] - mail[k]

            @pl.when(helped_dn)
            def _():
                dn_copy(C - H + e, k).wait_recv()
                pan[at, :] = pan[at, :] - mail[top - k]

        all_ahead().wait_recv()

        @pl.loop(0, H)
        def _(e):
            at = strip_rows(C - H + e)
            upd[at, :] = upd[at, :] + ahead[e]

        coef_copy().wait_send()

    for g in range(G):
        @pl.when(z == g)
        def _():
            if g < G - 1:
                up_move(0, (G - 1 - g) * C, up_recv.at[0]).wait_send()
            if g > 0:
                dn_move(0, g * C, dn_recv.at[0]).wait_send()
            worked = C + (H if g in (0, G - 1) else 0)
            for s, first, count in ((0, half_n, half_n), (1, 1, half_n - 1)):
                if count:
                    sent = part.at[pl.ds(0, worked), pl.ds(first, count)]
                    pltpu.make_async_remote_copy(
                        src_ref=sent, dst_ref=sent, send_sem=x_send.at[s], recv_sem=x_recv.at[0, s],
                        device_id={"sub": dest_of(half_n)}, device_id_type=MESH,
                    ).wait_send()

    if H:
        @pl.when(helper)
        def _():
            all_ahead().wait_send()

    all_lists().wait_send()


def per_device(leaf_l, leaf_u, front, inv_diag, send_tiles, counts, trail_list, upper, trailing):
    G = lax.axis_size("grp")
    N = lax.axis_size("sub")
    strip, width = front.shape[1:]
    depth = leaf_u.shape[1]
    tile = upper.shape[1]
    rows = next(r for r in ROWS if strip % r == 0)
    C = strip // rows
    H = min(AHEAD, C) if G > 3 else 0
    block = 2 * rows if strip % (2 * rows) == 0 else strip
    nt, nu = width // tile, upper.shape[0]
    terms = -(-nt * nu // 8) * 8
    send_tiles = jnp.transpose(send_tiles, (0, 1, 3, 2))
    trail_list = jnp.transpose(trail_list, (0, 3, 1, 2))
    anywhere = pl.BlockSpec(memory_space=pl.ANY)
    vmem = pl.BlockSpec(memory_space=pltpu.VMEM)
    steps = N.bit_length() - 1
    dma = pltpu.SemaphoreType.DMA
    panel, updated = pl.pallas_call(
        functools.partial(kernel, G, N, C, H, rows, block),
        out_shape=(pltpu.VMEM(front.shape[1:], F32), pltpu.VMEM(trailing.shape[1:], F32)),
        in_specs=[anywhere] * 9,
        out_specs=(vmem, vmem),
        scratch_shapes=[
            pltpu.SMEM(send_tiles.shape, jnp.int32),
            pltpu.SMEM(counts.shape, jnp.int32),
            pltpu.VMEM(leaf_l.shape[1:], F32),
            pltpu.VMEM((2 * block, depth), BF16),
            pltpu.VMEM((depth, width), F32),
            pltpu.VMEM((depth, width), BF16),
            pltpu.VMEM((depth, width), BF16),
            pltpu.VMEM((G * strip, width), F32),
            pltpu.VMEM((strip, width), F32),
            pltpu.VMEM(inv_diag.shape[1:], F32),
            pltpu.VMEM(inv_diag.shape[1:], BF16),
            pltpu.VMEM(inv_diag.shape[1:], BF16),
            pltpu.VMEM(upper.shape, F32),
            pltpu.VMEM(upper.shape, BF16),
            pltpu.VMEM(upper.shape, BF16),
            pltpu.VMEM((strip, tile), F32),
            pltpu.VMEM(((G + 1) * C, rows, width), F32),
            pltpu.VMEM((N,) + trail_list.shape[1:], jnp.int32),
            pltpu.VMEM((2, N, terms, tile), F32),
            pltpu.VMEM((rows, width), F32),
            pltpu.VMEM((2 * nt * rows, tile), BF16),
            pltpu.VMEM((nu, nt * rows, tile), F32),
            pltpu.VMEM((C + H, N, rows, tile), F32),
            pltpu.VMEM((C + H, N, rows, tile), F32),
            pltpu.VMEM((max(H, 1), rows, tile), F32),
            dma((nt + 12,)),
            dma((2,)), dma(((G - 1) * C * rows // block,)), dma((C,)), dma((C,)),
            dma((2,)),
            dma((2,)), dma((RING, 2)),
            dma((2,)), dma((2,)),
            pltpu.SemaphoreType.REGULAR((2,)),
        ],
        compiler_params=pltpu.CompilerParams(
            collective_id=0, has_side_effects=True, vmem_limit_bytes=60 << 20
        ),
    )(leaf_l, leaf_u, front, inv_diag, send_tiles, counts, trail_list, upper, trailing)
    return write_out(panel, updated)


def copy_kernel(cuts, panel, updated, panel_out, updated_out, sem):
    rows = panel.shape[0] // cuts
    copies = [pltpu.make_async_copy(updated, updated_out.at[0], sem.at[cuts])]
    for i in range(cuts):
        at = pl.ds(i * rows, rows)
        copies.append(pltpu.make_async_copy(panel.at[at], panel_out.at[0, at], sem.at[i]))
    for copy in copies:
        copy.start()
    for copy in copies:
        copy.wait()


def write_out(panel, updated):
    strip = panel.shape[0]
    cuts = next(n for n in (4, 2, 1) if strip % (8 * n) == 0)
    vmem = pl.BlockSpec(memory_space=pltpu.VMEM)
    anywhere = pl.BlockSpec(memory_space=pl.ANY)
    return pl.pallas_call(
        functools.partial(copy_kernel, cuts),
        out_shape=tuple(jax.ShapeDtypeStruct((1,) + x.shape, F32) for x in (panel, updated)),
        in_specs=[vmem, vmem],
        out_specs=(anywhere, anywhere),
        scratch_shapes=[pltpu.SemaphoreType.DMA((cuts + 1,))],
        compiler_params=pltpu.CompilerParams(vmem_limit_bytes=1 << 20),
    )(panel, updated)


def solution(mesh):
    placed = (
        P("sub", "grp", None),
        P("sub", "grp", None),
        P("sub", "grp", None),
        P("sub", None, None, None),
        P("sub", "grp", None, None),
        P("sub", "grp", None),
        P("sub", "grp", None, None),
        P(),
        P("sub", "grp", None),
    )
    return jax.shard_map(
        per_device,
        mesh=mesh,
        in_specs=placed,
        out_specs=(P("sub", "grp", None), P("sub", "grp", None)),
        check_vma=False,
    )
```

```python
import functools

import jax
import jax.numpy as jnp
from jax import lax
from jax.experimental import pallas as pl
from jax.experimental.pallas import tpu as pltpu
from jax.sharding import PartitionSpec as P

MESH = pl.DeviceIdType.MESH
F32 = jnp.float32
BF16 = jnp.bfloat16
ROWS = (32, 16, 8)
AHEAD = 2
LAGS = (2, 4)
RING = 6


def split(x):
    high = x.astype(BF16)
    return high, (x - high.astype(F32)).astype(BF16)


def dot(a, b):
    return jnp.dot(a, b, preferred_element_type=F32)


def dot3(stacked, high, low):
    m = stacked.shape[0] // 2
    both = dot(stacked, high)
    return both[:m] + both[m:] + dot(stacked[:m], low)


def kernel(
    G, N, C, H, rows, block,
    leaf_l, leaf_u, front, inv_diag, send_tiles, counts, trail_list, upper, trailing,
    pan, upd,
    tiles_buf, counts_buf, l_buf, l_two, u_buf, u_hi, u_lo, s_buf, f_buf, d_buf, d_hi, d_lo, v_buf, v_hi, v_lo, t_buf, mail,
    lists, coef, work, x_buf, prod, part, got, ahead,
    in_sem, send_sem, many_recv, up_recv, dn_recv, list_sem, x_send, x_recv, role_sem, relay,
):
    z = lax.axis_index("grp")
    me = lax.axis_index("sub")
    width = front.shape[2]
    tile = upper.shape[1]
    depth = u_buf.shape[0]
    nt = width // tile
    nu = upper.shape[0]
    cap = send_tiles.shape[2]
    strip = C * rows
    per = block // rows
    group = min(4, N // 2)
    steps = N.bit_length() - 1
    half_n = N // 2
    step = next(n for n in (256, 128, 64, 32, 16) if depth % n == 0)
    top = (G + 1) * C - 1
    low_end, high_end = z == 0, z == G - 1
    helper = (H > 0) & (low_end | high_end)
    helped_up, helped_dn = (H > 0) & (z == 1), (H > 0) & (z == G - 2)
    helped = helped_up | helped_dn
    ally = jnp.where(low_end | (z == G - 2), z + 1, z - 1)
    extra = jnp.where(helper, H, 0)

    def bit(value, s):
        return lax.rem(lax.div(value, 1 << s), 2)

    shifts = [(1 << s) * (1 - 2 * bit(me, s)) for s in range(steps)]

    def dest_of(p):
        if isinstance(p, int):
            return me + sum(shifts[s] for s in range(steps) if p >> (steps - 1 - s) & 1)
        return me + sum(bit(p, steps - 1 - s) * shifts[s] for s in range(steps))

    def load_l(t, first, count, n):
        at = pl.ds(t * strip + first, count)
        return pltpu.make_async_copy(leaf_l.at[0, at], l_buf.at[at], in_sem.at[n])

    def load_u(n):
        cols = pl.ds(pl.multiple_of(n * tile, tile), tile)
        return pltpu.make_async_copy(leaf_u.at[0, :, cols], u_buf.at[:, cols], in_sem.at[n])

    def load_head(row, n):
        at = pl.ds(pl.multiple_of(row, 8), block)
        return pltpu.make_async_copy(leaf_l.at[0, at], l_buf.at[at], in_sem.at[n])

    row_far = (G - 1) * strip
    head_row = jnp.where(high_end, 0, row_far)
    head = load_head(head_row, nt)
    tails = [load_head(row_far - head_row, nt + 1), load_l(0, block, (G - 1) * strip - block, nt + 2)]
    if block < strip:
        tails.append(load_l(G - 1, block, strip - block, nt + 3))
    others = [
        pltpu.make_async_copy(front.at[0], f_buf, in_sem.at[nt + 4]),
        pltpu.make_async_copy(inv_diag.at[0], d_buf, in_sem.at[nt + 5]),
        pltpu.make_async_copy(trailing.at[0], t_buf, in_sem.at[nt + 6]),
        pltpu.make_async_copy(upper, v_buf, in_sem.at[nt + 7]),
        pltpu.make_async_copy(send_tiles, tiles_buf, in_sem.at[nt + 8]),
        pltpu.make_async_copy(counts, counts_buf, in_sem.at[nt + 9]),
    ]
    small = tile // 2
    halves = [
        pltpu.make_async_copy(leaf_u.at[0, :, cols], u_buf.at[:, cols], in_sem.at[n])
        for n, cols in ((0, slice(0, small)), (nt + 11, slice(small, tile)))
    ]
    head.start()
    halves[0].start()
    halves[1].start()

    barrier = pltpu.get_barrier_semaphore()

    relayed = H > 0
    plane = jnp.logical_not(low_end | high_end) if relayed else z >= 0

    @pl.when(z > 0)
    def _():
        pl.semaphore_signal(barrier, inc=1, device_id={"grp": z - 1}, device_id_type=MESH)

    @pl.when(z < G - 1)
    def _():
        pl.semaphore_signal(barrier, inc=1, device_id={"grp": z + 1}, device_id_type=MESH)

    @pl.when(plane)
    def _():
        for p in reversed(range(1, N)):
            pl.semaphore_signal(barrier, inc=1, device_id={"sub": dest_of(p)}, device_id_type=MESH)

    pl.loop(1, nt)(lambda n: load_u(n).start())
    for copy in tails + others:
        copy.start()

    def own_list():
        return pltpu.make_async_copy(trail_list.at[0], lists.at[me], in_sem.at[nt + 10])

    def list_copy(p, owner):
        return pltpu.make_async_remote_copy(
            src_ref=trail_list.at[0], dst_ref=lists.at[owner],
            send_sem=list_sem.at[0], recv_sem=list_sem.at[1],
            device_id={"sub": dest_of(p)}, device_id_type=MESH,
        )

    def all_lists():
        return pltpu.make_async_remote_copy(
            src_ref=lists.at[pl.ds(0, N - 1)], dst_ref=lists.at[pl.ds(0, N - 1)],
            send_sem=list_sem.at[0], recv_sem=list_sem.at[1],
            device_id={"sub": dest_of(1)}, device_id_type=MESH,
        )

    def up_move(first, count, recv_sem, cols=slice(None)):
        at = pl.ds(first, count)
        return pltpu.make_async_remote_copy(
            src_ref=mail.at[at, :, cols], dst_ref=mail.at[at, :, cols],
            send_sem=send_sem.at[0], recv_sem=recv_sem,
            device_id={"grp": z + 1}, device_id_type=MESH,
        )

    def dn_move(first, count, recv_sem, cols=slice(None)):
        at = pl.ds(top + 1 - first - count, count)
        return pltpu.make_async_remote_copy(
            src_ref=mail.at[at, :, cols], dst_ref=mail.at[at, :, cols],
            send_sem=send_sem.at[1], recv_sem=recv_sem,
            device_id={"grp": z - 1}, device_id_type=MESH,
        )

    def up_copy(c, k):
        return up_move(k, 1, up_recv.at[c])

    def dn_copy(c, k):
        return dn_move(k, 1, dn_recv.at[c])

    def up_many(b, cols=slice(None)):
        return up_move(b * per, per, many_recv.at[b], cols)

    def dn_many(b, cols=slice(None)):
        return dn_move(b * per, per, many_recv.at[(G - 1) * C // per - 1 - b], cols)

    def coef_copy():
        return pltpu.make_async_remote_copy(
            src_ref=coef.at[0], dst_ref=coef.at[1],
            send_sem=role_sem.at[0], recv_sem=role_sem.at[0],
            device_id={"grp": ally}, device_id_type=MESH,
        )

    def ahead_copy(e):
        return pltpu.make_async_remote_copy(
            src_ref=ahead.at[e], dst_ref=ahead.at[e],
            send_sem=role_sem.at[1], recv_sem=role_sem.at[1],
            device_id={"grp": ally}, device_id_type=MESH,
        )

    def all_ahead():
        return pltpu.make_async_remote_copy(
            src_ref=ahead, dst_ref=ahead,
            send_sem=role_sem.at[1], recv_sem=role_sem.at[1],
            device_id={"grp": ally}, device_id_type=MESH,
        )

    def halve(row):
        at = pl.ds(pl.multiple_of(row, 8), block)
        high, low = split(l_buf[at, :])
        l_two[:block, :] = high
        l_two[block:, :] = low

    def tile_cols(n):
        return pl.ds(pl.multiple_of(n * tile, tile), tile)

    def product(row, cols):
        at = pl.ds(pl.multiple_of(row, 8), block)
        s_buf[at, cols] = dot3(l_two[...], u_hi[:, cols], u_lo[:, cols])

    def schur(row):
        halve(row)
        pl.loop(0, nt)(lambda n: product(row, tile_cols(n)))

    def forward(slot, row, first):
        at = pl.ds(pl.multiple_of(row, 8), rows)

        @pl.when(first)
        def _():
            mail[slot] = s_buf[at, :]

        @pl.when(jnp.logical_not(first))
        def _():
            mail[slot] = mail[slot] + s_buf[at, :]

    def begin(copy, cols):
        copy.wait()

        @pl.loop(0, depth, step=step)
        def _(r):
            at = pl.ds(pl.multiple_of(r, step), step)
            high, low = split(u_buf[at, cols])
            u_hi[at, cols] = high
            u_lo[at, cols] = low

        @pl.when(low_end | high_end)
        def _():
            product(head_row, cols)

    def begin_send(cols):
        @pl.when(low_end)
        def _():
            for k in range(per):
                mail[k, :, cols] = s_buf[(G - 1) * strip + k * rows : (G - 1) * strip + (k + 1) * rows, cols]
            up_many(0, cols).start()

        @pl.when(high_end)
        def _():
            for k in range(per):
                mail[top - k, :, cols] = s_buf[k * rows : (k + 1) * rows, cols]
            dn_many(0, cols).start()

    head.wait()

    @pl.when(low_end | high_end)
    def _():
        halve(head_row)

    begin(halves[0], slice(0, small))
    pl.semaphore_wait(barrier, jnp.where(plane, N - 1, 0) + jnp.where(z > 0, 1, 0) + jnp.where(z < G - 1, 1, 0))
    begin_send(slice(0, small))
    begin(halves[1], slice(small, tile))
    begin_send(slice(small, tile))

    @pl.when(helped)
    def _():
        for p in reversed(range(1, N)):
            pl.semaphore_signal(relay.at[0], inc=1, device_id={"sub": dest_of(p)}, device_id_type=MESH)

    @pl.loop(1, nt)
    def _(n):
        begin(load_u(n), tile_cols(n))
        begin_send(tile_cols(n))

    @pl.when(helped)
    def _():
        pl.semaphore_wait(relay.at[0], N - 1)
        pl.semaphore_signal(relay.at[1], inc=1, device_id={"grp": ally}, device_id_type=MESH)

    def weigh(p):
        d = dest_of(p)

        source, slot, which = lists[d, 0], lists[d, 1], lists[d, 2]
        pick = jnp.zeros_like(source)
        for c in range(cap):
            pick = jnp.where(slot == c, tiles_buf[0, 0, c, d], pick)
        live = (source == me) & (slot < counts_buf[0, 0, d])
        code = jnp.where(live, pick * nu + which, -1)
        terms = lax.broadcasted_iota(jnp.int32, (coef.shape[2], code.shape[1]), 0)
        total = jnp.sum(jnp.where(code == terms, 1.0, 0.0).astype(F32), axis=1, keepdims=True)
        coef[0, p] = jnp.broadcast_to(total, coef.shape[2:])

    def exchange(e):
        return pltpu.make_async_remote_copy(
            src_ref=part.at[e, pl.ds(half_n, half_n)], dst_ref=got.at[e, pl.ds(half_n, half_n)],
            send_sem=x_send.at[0], recv_sem=x_recv.at[lax.rem(e, RING), 0],
            device_id={"sub": dest_of(half_n)}, device_id_type=MESH,
        )

    def scatter(e, p, count=1):
        return pltpu.make_async_remote_copy(
            src_ref=part.at[e, pl.ds(p, count)], dst_ref=got.at[e, pl.ds(p, count)],
            send_sem=x_send.at[1], recv_sem=x_recv.at[lax.rem(e, RING), 1],
            device_id={"sub": dest_of(p)}, device_id_type=MESH,
        )

    def chunk(e):
        c = jnp.where(helper, e - H, jnp.where(helped, jnp.where(e < H, C - H + e, e - H), e))
        return jnp.maximum(c, 0)

    def strip_rows(c):
        return pl.ds(pl.multiple_of(c * rows, 8), rows)

    def solve(e):
        helping = helper & (e < H)
        late = helped & (e < H)
        c = chunk(e)
        at = strip_rows(c)
        k_late = (G - 1) * C - H + e

        @pl.when(helping)
        def _():
            there = ally * strip + (C - H + e) * rows
            work[...] = s_buf[pl.ds(pl.multiple_of(there, 8), rows), :]

        @pl.when(jnp.logical_not(helping))
        def _():
            work[...] = f_buf[at, :] - s_buf[pl.ds(pl.multiple_of(z * strip + c * rows, 8), rows), :]

            @pl.when((z > 0) & jnp.logical_not(late & helped_up))
            def _():
                k = (G - 1 - z) * C + c
                up_copy(c, k).wait_recv()
                work[...] = work[...] - mail[k]

            @pl.when((z < G - 1) & jnp.logical_not(late & helped_dn))
            def _():
                k = z * C + c
                dn_copy(c, k).wait_recv()
                work[...] = work[...] - mail[top - k]

        half = nt * rows
        for j in range(nt):
            cols = slice(j * tile, (j + 1) * tile)
            high, low = split(work[:, cols])
            solved = dot3(jnp.concatenate([high, low], axis=0), d_hi[j], d_lo[j])
            work[:, cols] = solved
            high, low = split(solved)
            x_buf[j * rows : (j + 1) * rows, :] = high
            x_buf[half + j * rows : half + (j + 1) * rows, :] = low

        @pl.when(jnp.logical_not(helping))
        def _():
            pan[at, :] = work[...]

        @pl.when(helping & low_end)
        def _():
            mail[k_late] = work[...]
            up_copy(C - H + e, k_late).start()

        @pl.when(helping & high_end)
        def _():
            mail[top - k_late] = work[...]
            dn_copy(C - H + e, k_late).start()

        for u in range(nu):
            prod[u] = dot3(x_buf[...], v_hi[u], v_lo[u])

        @pl.when(helping & (e == 0))
        def _():
            coef_copy().wait_recv()

        table = jnp.where(helping, 1, 0)

        def mix(g):
            p0 = g * group

            @pl.loop(0, rows, step=8)
            def _(r):
                r = pl.multiple_of(r, 8)
                sums = [None] * group
                for j in range(nt):
                    for u in range(nu):
                        value = prod[u, pl.ds(j * rows + r, 8), :]
                        for q in range(group):
                            n = j * nu + u
                            term = coef[table, p0 + q, n : n + 1, :] * value
                            sums[q] = term if sums[q] is None else sums[q] + term
                for q in range(group):
                    part[e, p0 + q, pl.ds(r, 8), :] = sums[q]

        groups = N // group
        pl.loop(groups // 2, groups)(mix)
        exchange(e).start()
        pl.loop(0, groups // 2)(mix)

    def stage(e, s):
        if s == 0:
            exchange(e).wait_recv()
            if half_n > 1:
                part[e, 1:half_n] = part[e, 1:half_n] + got[e, half_n + 1 :]
                for p in reversed(range(1, half_n)):
                    scatter(e, p).start()
            part[e, 0] = part[e, 0] + got[e, half_n]
        else:
            total = part[e, 0]
            if half_n > 1:
                scatter(e, 1, half_n - 1).wait_recv()
                for p in range(1, half_n):
                    total = total + got[e, p]
            helping = helper & (e < H)

            @pl.when(helping)
            def _():
                ahead[e] = total
                ahead_copy(e).start()

            @pl.when(jnp.logical_not(helping))
            def _():
                at = strip_rows(chunk(e))
                upd[at, :] = t_buf[at, :] - total

    lag_up, lag_dn = z * per, (G - 1 - z) * per
    base = jnp.maximum((G - 1 - z) * C + lag_up, z * C + lag_dn)

    @pl.loop(0, base + C + LAGS[1])
    def _(i):
        up, down, own = i - lag_up, i - lag_dn, i - base
        e = own + extra
        has_up = (up >= jnp.where(low_end, per, 0)) & (up < (G - 1 - z) * C)
        has_dn = (down >= jnp.where(high_end, per, 0)) & (down < z * C)
        plain = (G - 1) * C - extra
        up_row = (G - 1) * strip + lax.rem(jnp.maximum(up, 0), C) * rows - lax.div(jnp.maximum(up, 0), C) * strip

        @pl.loop(0, 3)
        def _(job):
            k = jnp.where(job == 0, up, jnp.where(job == 1, down, own + C))
            has = ((job == 0) & has_up) | ((job == 1) & has_dn) | ((job == 2) & (k >= 0) & (k < C))
            row = jnp.where(job == 0, up_row, jnp.where(job == 1, down * rows, z * strip + k * rows))

            @pl.when(has & (lax.rem(jnp.maximum(k, 0), per) == 0))
            def _():
                schur(row)

        @pl.when(has_up & (up < plain))
        def _():
            place = lax.rem(up, per)
            final = (G - 2 - z) * C

            @pl.when((z > 0) & (place == 0))
            def _():
                up_many(lax.div(up, per)).wait_recv()

            forward(up, up_row, z == 0)

            @pl.when((up < final) & (place == per - 1))
            def _():
                up_many(lax.div(up, per)).start()

            @pl.when(up >= final)
            def _():
                up_copy(up - final, up).start()

        @pl.when(has_dn & (down < plain))
        def _():
            place = lax.rem(down, per)
            final = (z - 1) * C

            @pl.when((z < G - 1) & (place == 0))
            def _():
                dn_many(lax.div(down, per)).wait_recv()

            forward(top - down, down * rows, z == G - 1)

            @pl.when((down < final) & (place == per - 1))
            def _():
                dn_many(lax.div(down, per)).start()

            @pl.when(down >= final)
            def _():
                dn_copy(down - final, down).start()

        @pl.when(i == 1)
        def _():
            own_list().start()
            for copy in tails + others:
                copy.wait()

            @pl.when(helper)
            def _():
                pl.semaphore_wait(relay.at[1], 1)

            @pl.loop(1, N)
            def _(p):
                list_copy(p, me).start()

            for j in range(nt):
                high, low = split(d_buf[j])
                d_hi[j] = high
                d_lo[j] = low
            for u in range(nu):
                high, low = split(v_buf[u])
                v_hi[u] = high
                v_lo[u] = low

        @pl.when(i == 3)
        def _():
            own_list().wait()
            all_lists().wait_recv()
            pl.loop(0, N)(weigh)

            @pl.when(helped)
            def _():
                coef_copy().start()

        turn = C + extra - 2
        ready = jnp.where(e < turn, e - LAGS[0] + 1, e)

        @pl.when((e >= LAGS[1]) & (e - LAGS[1] < C + extra))
        def _():
            stage(e - LAGS[1], 1)

        @pl.loop(jnp.where(e <= turn, e - LAGS[0], e - 1), ready)
        def _(old):
            @pl.when((old >= 0) & (old < C + extra))
            def _():
                stage(old, 0)

        @pl.when((e >= 0) & (e < C + extra))
        def _():
            solve(e)

    @pl.when(helped)
    def _():
        @pl.loop(0, H)
        def _(e):
            at = strip_rows(C - H + e)
            k = (G - 1) * C - H + e

            @pl.when(helped_up)
            def _():
                up_copy(C - H + e, k).wait_recv()
                pan[at, :] = pan[at, :] - mail[k]

            @pl.when(helped_dn)
            def _():
                dn_copy(C - H + e, k).wait_recv()
                pan[at, :] = pan[at, :] - mail[top - k]

        all_ahead().wait_recv()

        @pl.loop(0, H)
        def _(e):
            at = strip_rows(C - H + e)
            upd[at, :] = upd[at, :] + ahead[e]

        coef_copy().wait_send()

    for g in range(G):
        @pl.when(z == g)
        def _():
            if g < G - 1:
                up_move(0, (G - 1 - g) * C, up_recv.at[0]).wait_send()
            if g > 0:
                dn_move(0, g * C, dn_recv.at[0]).wait_send()
            worked = C + (H if g in (0, G - 1) else 0)
            for s, first, count in ((0, half_n, half_n), (1, 1, half_n - 1)):
                if count:
                    sent = part.at[pl.ds(0, worked), pl.ds(first, count)]
                    pltpu.make_async_remote_copy(
                        src_ref=sent, dst_ref=sent, send_sem=x_send.at[s], recv_sem=x_recv.at[0, s],
                        device_id={"sub": dest_of(half_n)}, device_id_type=MESH,
                    ).wait_send()

    if H:
        @pl.when(helper)
        def _():
            all_ahead().wait_send()

    all_lists().wait_send()


def per_device(leaf_l, leaf_u, front, inv_diag, send_tiles, counts, trail_list, upper, trailing):
    G = lax.axis_size("grp")
    N = lax.axis_size("sub")
    strip, width = front.shape[1:]
    depth = leaf_u.shape[1]
    tile = upper.shape[1]
    rows = next(r for r in ROWS if strip % r == 0)
    C = strip // rows
    H = min(AHEAD, C) if G > 3 else 0
    block = 2 * rows if strip % (2 * rows) == 0 else strip
    nt, nu = width // tile, upper.shape[0]
    terms = -(-nt * nu // 8) * 8
    send_tiles = jnp.transpose(send_tiles, (0, 1, 3, 2))
    trail_list = jnp.transpose(trail_list, (0, 3, 1, 2))
    anywhere = pl.BlockSpec(memory_space=pl.ANY)
    vmem = pl.BlockSpec(memory_space=pltpu.VMEM)
    steps = N.bit_length() - 1
    dma = pltpu.SemaphoreType.DMA
    panel, updated = pl.pallas_call(
        functools.partial(kernel, G, N, C, H, rows, block),
        out_shape=(pltpu.VMEM(front.shape[1:], F32), pltpu.VMEM(trailing.shape[1:], F32)),
        in_specs=[anywhere] * 9,
        out_specs=(vmem, vmem),
        scratch_shapes=[
            pltpu.SMEM(send_tiles.shape, jnp.int32),
            pltpu.SMEM(counts.shape, jnp.int32),
            pltpu.VMEM(leaf_l.shape[1:], F32),
            pltpu.VMEM((2 * block, depth), BF16),
            pltpu.VMEM((depth, width), F32),
            pltpu.VMEM((depth, width), BF16),
            pltpu.VMEM((depth, width), BF16),
            pltpu.VMEM((G * strip, width), F32),
            pltpu.VMEM((strip, width), F32),
            pltpu.VMEM(inv_diag.shape[1:], F32),
            pltpu.VMEM(inv_diag.shape[1:], BF16),
            pltpu.VMEM(inv_diag.shape[1:], BF16),
            pltpu.VMEM(upper.shape, F32),
            pltpu.VMEM(upper.shape, BF16),
            pltpu.VMEM(upper.shape, BF16),
            pltpu.VMEM((strip, tile), F32),
            pltpu.VMEM(((G + 1) * C, rows, width), F32),
            pltpu.VMEM((N,) + trail_list.shape[1:], jnp.int32),
            pltpu.VMEM((2, N, terms, tile), F32),
            pltpu.VMEM((rows, width), F32),
            pltpu.VMEM((2 * nt * rows, tile), BF16),
            pltpu.VMEM((nu, nt * rows, tile), F32),
            pltpu.VMEM((C + H, N, rows, tile), F32),
            pltpu.VMEM((C + H, N, rows, tile), F32),
            pltpu.VMEM((max(H, 1), rows, tile), F32),
            dma((nt + 12,)),
            dma((2,)), dma(((G - 1) * C * rows // block,)), dma((C,)), dma((C,)),
            dma((2,)),
            dma((2,)), dma((RING, 2)),
            dma((2,)),
            pltpu.SemaphoreType.REGULAR((2,)),
        ],
        compiler_params=pltpu.CompilerParams(
            collective_id=0, has_side_effects=True, vmem_limit_bytes=60 << 20
        ),
    )(leaf_l, leaf_u, front, inv_diag, send_tiles, counts, trail_list, upper, trailing)
    return write_out(panel, updated)


def copy_kernel(cuts, panel, updated, panel_out, updated_out, sem):
    rows = panel.shape[0] // cuts
    copies = [pltpu.make_async_copy(updated, updated_out.at[0], sem.at[cuts])]
    for i in range(cuts):
        at = pl.ds(i * rows, rows)
        copies.append(pltpu.make_async_copy(panel.at[at], panel_out.at[0, at], sem.at[i]))
    for copy in copies:
        copy.start()
    for copy in copies:
        copy.wait()


def write_out(panel, updated):
    strip = panel.shape[0]
    cuts = next(n for n in (4, 2, 1) if strip % (8 * n) == 0)
    vmem = pl.BlockSpec(memory_space=pltpu.VMEM)
    anywhere = pl.BlockSpec(memory_space=pl.ANY)
    return pl.pallas_call(
        functools.partial(copy_kernel, cuts),
        out_shape=tuple(jax.ShapeDtypeStruct((1,) + x.shape, F32) for x in (panel, updated)),
        in_specs=[vmem, vmem],
        out_specs=(anywhere, anywhere),
        scratch_shapes=[pltpu.SemaphoreType.DMA((cuts + 1,))],
        compiler_params=pltpu.CompilerParams(vmem_limit_bytes=1 << 20),
    )(panel, updated)


def solution(mesh):
    placed = (
        P("sub", "grp", None),
        P("sub", "grp", None),
        P("sub", "grp", None),
        P("sub", None, None, None),
        P("sub", "grp", None, None),
        P("sub", "grp", None),
        P("sub", "grp", None, None),
        P(),
        P("sub", "grp", None),
    )
    return jax.shard_map(
        per_device,
        mesh=mesh,
        in_specs=placed,
        out_specs=(P("sub", "grp", None), P("sub", "grp", None)),
        check_vma=False,
    )
```
